32 devices in a mesh: group: 2 (over x), wide: 16 (over z, y, core).
Axes of the slice: x: 2, y: 2, z: 4, core: 2. Of those that a mesh axis runs over, the one named last changes fastest.
Arguments:
- tokens: bfloat16 [192, 2688], P('group', 'wide'), parts along dimension 0, may hold values from -6 to 6
- mix_gain: bfloat16 [2688], replicated, may hold values from 0.099609375 to 1.8984375
- proj_inner: bfloat16 [2688, 2, 4096], P(None, None, 'wide'), may hold values from -0.125 to 0.125
- proj_maps: bfloat16 [2688, 2048], P(None, 'wide'), may hold values from -0.125 to 0.125
- proj_step: bfloat16 [2688, 64], P(None, 'wide'), may hold values from -0.125 to 0.125
- window_inner: bfloat16 [192, 3, 4096], P('group', None, 'wide'), parts along dimension 0, may hold values from -6 to 6
- window_maps: bfloat16 [192, 3, 2048], P('group', None, 'wide'), parts along dimension 0, may hold values from -6 to 6
- kernel_inner: bfloat16 [4, 4096], P(None, 'wide'), may hold values from -3 to 3
- kernel_maps: bfloat16 [4, 2048], P(None, 'wide'), may hold values from -3 to 3
- step_bias: float32 [64], P('wide'), may hold values from -4 to -1
- decay_log: float32 [64], P('wide'), may hold values from -1 to 2.5
- skip_gain: float32 [64], P('wide'), may hold values from 0.5 to 2
- gated_gain: bfloat16 [4096], P('wide'), may hold values from 0.099609375 to 1.8984375
- proj_out: bfloat16 [4096, 2688], P('wide'), may hold values from -0.125 to 0.125
- ssm_state: float32 [192, 64, 64, 128], P('group', 'wide'), parts along dimension 0, may hold values from -0.6 to 0.6
- moe_gain: bfloat16 [2688], replicated, may hold values from 0.099609375 to 1.8984375
- router_weight: bfloat16 [2688, 16], replicated, may hold values from -0.125 to 0.125
- expert_ids: int32 [192, 6], P('group'), parts along dimension 0, may hold values from 0 to 15, all different within a row; in each aligned block of 96 rows (0 to 95, 96 to 191, ...) at most 96 rows name the same one
- expert_up: bfloat16 [16, 2688, 928], P('wide'), may hold values from -0.125 to 0.125
- expert_down: bfloat16 [16, 928, 2688], P('wide'), may hold values from -0.1875 to 0.1875
Outputs:
- next_hidden: bfloat16 [192, 2688], P('group', 'wide'), parts along dimension 0
- new_state: float32 [192, 64, 64, 128], P('group', 'wide'), parts along dimension 0
The draws below stay inside these ranges and needn't reach their ends.
There are 2 independent parts, one for each index of `group`. The reference program is written for one: setup_inputs(seed, part) draws one part's arguments, and reference() takes and returns one part's arrays. A program takes and returns all parts, laid end to end along the dimension named above; an argument that names none is the same for every part. Nothing has to cross between parts.
Inputs may be any that keep to these rules, and one draw needn't show every extreme that they name: `expert_ids`: each token names 6 different experts; no expert is named by more than 96 tokens of a part, a bound that some block reaches.
All inputs are finite; a program needn't handle non-finite values.
Results may differ from the reference program's by a relative error of at most 0.013.
Values may be sent and summed in bfloat16 or wider, within the bound.
A program may use at most 128 MiB of HBM per device.

```python
import math
import jax
import jax.numpy as jnp
import numpy as np
from jax import lax

WIDTH = 2688
HEADS = 64
HEAD_DIM = 64
STATE = 128
GROUPS = 8
KERNEL = 4
TOPK = 6
HIDDEN_SIZE = 928
SEQS = 96
INNER = 4096
MAPS = 2048
EXPERTS = 16
CAPACITY = 96


def strengthened(drawn, stream_key, source, target, blocks, factor):
    def block_of(dim):
        return (jnp.arange(drawn.shape[dim]) // (drawn.shape[dim] // blocks)).reshape((-1,) + (1,) * (drawn.ndim - 1 - dim))

    first = jax.random.permutation(stream_key, blocks)[block_of(target)]
    other_side = (block_of(target) + blocks // 2) % blocks
    return jnp.where((block_of(source) == first) | (block_of(source) == other_side), factor * drawn, drawn)


def steps_of(own_key, shape, cuts, low, largest):
    def one(dim, parts):
        steps = jax.random.uniform(jax.random.fold_in(jax.random.fold_in(own_key, 6), dim), (parts,), jnp.float32, low / len(cuts), largest / len(cuts))
        return jnp.repeat(jnp.exp(steps), shape[dim] // parts).reshape((-1,) + (1,) * (len(shape) - dim - 1))

    factor_of = one(*cuts[0])
    for cut in cuts[1:]:
        factor_of = factor_of * one(*cut)
    return factor_of


def assign_block(stream_key, own, number, rows, number_of, top, reach, skew):
    order = jax.random.permutation(stream_key, number_of)
    heavy_load, ordinary = shares(number_of, rows * top, reach, skew, True), shares(number_of, rows * top, reach, skew, False)
    places = jnp.arange(number_of)

    def named(sizes, rotation):
        used = int((sizes > 0).sum())
        fixed = max(1, used // 4)
        moved = fixed + (places - fixed + rotation * (used - fixed)) % max(1, number_of - fixed)
        return jnp.zeros((number_of,), jnp.int32).at[order[jnp.where(places < fixed, places, moved)]].set(jnp.asarray(sizes, jnp.int32))

    sizes = jnp.where(number % 4 == 0, named(heavy_load, number // 4), named(ordinary, number - number // 4 - 1))
    mixed = jax.random.permutation(jax.random.fold_in(own, 3), number_of)
    donor, taker = mixed[0:number_of // 2 * 2:2], mixed[1:number_of // 2 * 2:2]
    slack = jnp.minimum(sizes[donor] - 1, reach - sizes[taker]) // 2
    slack = jnp.where((donor == order[0]) | (taker == order[0]) | (sizes[taker] == 0), 0, jnp.maximum(slack, 0))
    moved = jax.random.randint(jax.random.fold_in(own, 4), (number_of // 2,), 0, 1 << 20) % (slack + 1)
    sizes = sizes.at[donor].add(-moved).at[taker].add(moved)
    items = jnp.searchsorted(jnp.cumsum(sizes), jnp.arange(rows * top), side="right").astype(jnp.int32)
    grid = items.reshape(top, rows).T
    grid = grid[jax.random.permutation(jax.random.fold_in(own, 1), rows)]
    rotation = jax.random.randint(jax.random.fold_in(own, 2), (rows, 1), 0, top)
    return jnp.take_along_axis(grid, (jnp.arange(top)[None, :] + rotation) % top, axis=1)


def shares(amount, total, limit, slope, full):
    loads = [(1 << 20) // math.isqrt(standing ** slope) + 1 for standing in range(1, amount + 1)]
    largest = limit if full else min(limit, max(-(-total // amount), total * loads[0] // sum(loads)))
    least = 1 if total - largest >= amount - 1 else 0
    counts, spare = [largest] + [least] * (amount - 1), total - largest - least * (amount - 1)
    while spare > 0:
        movable = [i for i in range(1, amount) if counts[i] < largest] or [i for i in range(1, amount) if counts[i] < limit]
        pool, remaining = sum([loads[i] for i in movable]), spare
        for i in movable:
            addition = min(limit - counts[i], max(1, remaining * loads[i] // pool), spare)
            counts[i] = counts[i] + addition
            spare = spare - addition
    return np.array(counts)


def scatter_about(stream_key, extent, scale, limit, pieces=(), held_as=jnp.bfloat16):
    entries = jax.random.normal(stream_key, extent, jnp.float32) * scale
    if len(pieces) > 0:
        entries = steps_of(stream_key, extent, pieces, -0.22, 0.18) * entries
    return jnp.clip(entries, min=-limit, max=limit).astype(held_as)


def noise_with(rng, extent, scale, reach, pieces, heavy, kind=jnp.bfloat16):
    result = scale * jax.random.normal(rng, extent, jnp.float32)
    if pieces:
        result = result * steps_of(rng, extent, pieces, -0.22, 0.18)
    return jnp.clip(strengthened(result, jax.random.fold_in(rng, 3), *heavy), -reach, reach).astype(kind)


def setup_inputs(seed: int = 0, part: int = 0) -> dict:
    keys = jax.random.split(jax.random.key(seed), 21)
    part_splits = jax.random.split(jax.random.fold_in(keys[20], part), 21)
    tokens = scatter_about(part_splits[0], (SEQS, WIDTH), 1.0, 6.0, ((1, 16),))
    mix_gain = jnp.clip(1.0 + 0.18 * jax.random.normal(keys[1], (WIDTH,), jnp.float32), 0.099609375, 1.8984375).astype(jnp.bfloat16)
    proj_inner = scatter_about(keys[2], (WIDTH, 2, INNER), WIDTH ** -0.5, 0.125, ((2, 16),))
    proj_maps = scatter_about(keys[3], (WIDTH, MAPS), WIDTH ** -0.5, 0.125, ((1, 16),))
    proj_step = scatter_about(keys[4], (WIDTH, HEADS), WIDTH ** -0.5, 0.125, ((1, 16),))
    window_inner = scatter_about(part_splits[5], (SEQS, KERNEL - 1, INNER), 1.0, 6.0, ((2, 16),))
    window_maps = scatter_about(part_splits[6], (SEQS, KERNEL - 1, MAPS), 1.0, 6.0, ((2, 16),))
    kernel_inner = scatter_about(keys[7], (KERNEL, INNER), KERNEL ** -0.5, 3.0, ((1, 16),))
    kernel_maps = scatter_about(keys[8], (KERNEL, MAPS), KERNEL ** -0.5, 3.0, ((1, 16),))
    step_bias = jnp.clip(-4.0 + 3.0 * jax.random.uniform(keys[9], (HEADS,), jnp.float32) ** steps_of(keys[9], (HEADS,), ((0, 16),), -0.2, 0.2), -4.0, -1.0)
    decay_log = jnp.clip(-1.0 + 3.5 * jax.random.uniform(keys[10], (HEADS,), jnp.float32) ** steps_of(keys[10], (HEADS,), ((0, 16),), -0.2, 0.2), -1.0, 2.5)
    skip_gain = jnp.clip(0.5 + 1.5 * jax.random.uniform(keys[11], (HEADS,), jnp.float32) ** steps_of(keys[11], (HEADS,), ((0, 16),), -0.2, 0.2), 0.5, 2.0)
    gated_gain = jnp.clip(1.0 + 0.18 * jax.random.normal(keys[12], (INNER,), jnp.float32), 0.099609375, 1.8984375).astype(jnp.bfloat16)
    proj_out = noise_with(keys[13], (INNER, WIDTH), INNER ** -0.5, 0.125, ((0, 16),), (0, 1, 16, 2.0))
    ssm_state = scatter_about(part_splits[14], (SEQS, HEADS, HEAD_DIM, STATE), 0.1, 0.6, ((1, 16),), jnp.float32)
    moe_gain = jnp.clip(1.0 + 0.18 * jax.random.normal(keys[15], (WIDTH,), jnp.float32), 0.099609375, 1.8984375).astype(jnp.bfloat16)
    router_weight = scatter_about(keys[16], (WIDTH, EXPERTS), WIDTH ** -0.5, 0.125)
    expert_ids_keys = jax.random.split(jax.random.fold_in(part_splits[17], 1), SEQS // SEQS)
    expert_ids_turns = jax.random.permutation(jax.random.fold_in(part_splits[17], 3), SEQS // SEQS)
    expert_ids = jax.vmap(lambda own, number: assign_block(jax.random.fold_in(part_splits[17], 2), own, number, SEQS, EXPERTS, TOPK, CAPACITY, 2))(expert_ids_keys, expert_ids_turns).reshape((SEQS, TOPK))
    expert_up = scatter_about(keys[18], (EXPERTS, WIDTH, HIDDEN_SIZE), WIDTH ** -0.5, 0.125, ((0, 16),))
    expert_down = scatter_about(keys[19], (EXPERTS, HIDDEN_SIZE, WIDTH), HIDDEN_SIZE ** -0.5, 0.1875, ((0, 16),))
    return dict(tokens=tokens, mix_gain=mix_gain, proj_inner=proj_inner, proj_maps=proj_maps, proj_step=proj_step, window_inner=window_inner, window_maps=window_maps, kernel_inner=kernel_inner, kernel_maps=kernel_maps, step_bias=step_bias, decay_log=decay_log, skip_gain=skip_gain, gated_gain=gated_gain, proj_out=proj_out, ssm_state=ssm_state, moe_gain=moe_gain, router_weight=router_weight, expert_ids=expert_ids, expert_up=expert_up, expert_down=expert_down)


epsilon = 1e-05

def rms_scale(values, axis):
    return lax.rsqrt(lax.optimization_barrier(jnp.mean(values * values, axis=axis, keepdims=True)) + epsilon)

def convolve(window, fresh, kernel):
    stacked = jnp.concatenate([window, fresh[:, None, :]], axis=1).astype(jnp.float32)
    mixed = lax.optimization_barrier(jnp.sum(stacked * kernel.astype(jnp.float32)[None], axis=1))
    return jax.nn.silu(mixed).astype(jnp.bfloat16)

def expert_rows(rows, upward, downward):
    hidden_units = jnp.dot(rows, upward, preferred_element_type=jnp.float32)
    active = jnp.square(jnp.maximum(hidden_units, 0.0)).astype(jnp.bfloat16)
    return jnp.dot(active, downward, preferred_element_type=jnp.float32).astype(jnp.bfloat16)

def route_gates(logits, expert_ids):
    onehot = (expert_ids[:, :, None] == jnp.arange(logits.shape[1], dtype=jnp.int32)[None, None, :]).astype(jnp.float32)
    chosen = lax.optimization_barrier(jnp.sum(onehot * logits[:, None, :], axis=2))
    score = jax.nn.sigmoid(chosen)
    return score / lax.optimization_barrier(jnp.sum(score, axis=1, keepdims=True))

def reference(tokens, mix_gain, proj_inner, proj_maps, proj_step, window_inner, window_maps, kernel_inner, kernel_maps, step_bias, decay_log, skip_gain, gated_gain, proj_out, ssm_state, moe_gain, router_weight, expert_ids, expert_up, expert_down):
    tokens_float = tokens.astype(jnp.float32)
    normed = (tokens_float * rms_scale(tokens_float, 1) * mix_gain.astype(jnp.float32)).astype(jnp.bfloat16)
    inner = jnp.dot(normed, proj_inner.reshape(WIDTH, 2 * INNER), preferred_element_type=jnp.float32).astype(jnp.bfloat16)
    gate_input = inner[:, :INNER]
    raw_inner = inner[:, INNER:]
    maps_raw = jnp.dot(normed, proj_maps, preferred_element_type=jnp.float32).astype(jnp.bfloat16)
    step_raw = jnp.dot(normed, proj_step, preferred_element_type=jnp.float32).astype(jnp.bfloat16)
    conv_inner = convolve(window_inner, raw_inner, kernel_inner)
    conv_maps = convolve(window_maps, maps_raw, kernel_maps).astype(jnp.float32)
    in_maps = jnp.repeat(conv_maps[:, :GROUPS * STATE].reshape(SEQS, GROUPS, STATE), HEADS // GROUPS, axis=1)
    out_maps = jnp.repeat(conv_maps[:, GROUPS * STATE:].reshape(SEQS, GROUPS, STATE), HEADS // GROUPS, axis=1)
    step_size = jax.nn.softplus(step_raw.astype(jnp.float32) + step_bias)
    decay = jnp.exp(-jnp.exp(decay_log) * step_size)
    head_inputs = conv_inner.astype(jnp.float32).reshape(SEQS, HEADS, HEAD_DIM)
    driven = (step_size[:, :, None] * head_inputs)[..., None] * in_maps[:, :, None, :]
    new_state = decay[:, :, None, None] * ssm_state + driven
    readout = jnp.einsum('shpn,shn->shp', new_state, out_maps, precision=lax.Precision.HIGHEST) + skip_gain[None, :, None] * head_inputs
    gated = readout.reshape(SEQS, INNER) * jax.nn.silu(gate_input.astype(jnp.float32))
    grouped = gated.reshape(SEQS, GROUPS, INNER // GROUPS)
    gated_out = ((grouped * rms_scale(grouped, 2)).reshape(SEQS, INNER) * gated_gain.astype(jnp.float32)).astype(jnp.bfloat16)
    mixer = jnp.dot(gated_out, proj_out, preferred_element_type=jnp.float32)
    hidden = (tokens_float + mixer).astype(jnp.bfloat16)
    hidden_float = lax.optimization_barrier(hidden).astype(jnp.float32)
    moe_normed = hidden_float * rms_scale(hidden_float, 1) * moe_gain.astype(jnp.float32)
    logits = jnp.dot(moe_normed, router_weight.astype(jnp.float32), precision=lax.Precision.HIGHEST)
    gates = route_gates(logits, expert_ids)
    moe_input = moe_normed.astype(jnp.bfloat16)
    onehot = (expert_ids[:, :, None] == jnp.arange(EXPERTS, dtype=jnp.int32)[None, None, :]).astype(jnp.float32)
    weights = lax.optimization_barrier(jnp.sum(onehot * gates[:, :, None], axis=1))

    def add_expert(total, item):
        upward, downward, column = item
        outputs = expert_rows(moe_input, upward, downward)
        return (total + column[:, None] * outputs.astype(jnp.float32), None)
    total, unused = lax.scan(add_expert, jnp.zeros((SEQS, WIDTH), jnp.float32), (expert_up, expert_down, weights.T))
    next_hidden = (hidden_float + total).astype(jnp.bfloat16)
    return (next_hidden, new_state)
```

```python
import functools

import jax
import jax.numpy as jnp
from jax import lax
from jax.experimental import pallas as pl
from jax.experimental.pallas import tpu as pltpu
from jax.sharding import PartitionSpec as P

HEADS = 64
HEAD_DIM = 64
STATE = 128
GROUPS = 8
EPSILON = 1e-05
MESH = pl.DeviceIdType.MESH
F32 = jnp.float32
BF16 = jnp.bfloat16


def greet_all(n, me):
    barrier = pltpu.get_barrier_semaphore()

    def greet(k, carry):
        pl.semaphore_signal(
            barrier, inc=1, device_id={"wide": lax.rem(me + k, n)}, device_id_type=MESH
        )
        return carry

    lax.fori_loop(1, n, greet, 0)


def await_all(n):
    pl.semaphore_wait(pltpu.get_barrier_semaphore(), n - 1)


def place_of(n, me):
    lines = n // 4
    return lines, me // 4, lax.rem(me // 2, 2), lax.rem(me, 2)


def index_of(line, side, core):
    return line * 4 + side * 2 + core


def gather_all(n, me, own, landing, send_sems, recv_sems, consume, meanwhile=None):
    lines, line, side, core = place_of(n, me)
    across = index_of(line, 1 - side, core)
    partner = index_of(line, side, 1 - core)
    sent = []

    def send(src, origin, peer):
        copy = pltpu.make_async_remote_copy(
            src_ref=src,
            dst_ref=landing.at[origin],
            send_sem=send_sems.at[len(sent)],
            recv_sem=recv_sems.at[origin],
            device_id={"wide": peer},
            device_id_type=MESH,
        )
        copy.start()
        sent.append(copy)

    def arrive(origin):
        pltpu.make_async_remote_copy(
            src_ref=own,
            dst_ref=landing.at[origin],
            send_sem=send_sems.at[0],
            recv_sem=recv_sems.at[origin],
            device_id={"wide": partner},
            device_id_type=MESH,
        ).wait_recv()

    for k in range(1, lines):
        send(own, me, index_of(lax.rem(line + k, lines), side, core))
    send(own, me, across)
    send(own, me, partner)
    if meanwhile is not None:
        meanwhile()
    consume(own, me)
    arrive(partner)
    consume(landing.at[partner], partner)
    for k in range(1, lines):
        origin = index_of(lax.rem(line + lines - k, lines), side, core)
        arrive(origin)
        send(landing.at[origin], origin, across)
        send(landing.at[origin], origin, partner)
        consume(landing.at[origin], origin)
    for k in range(lines):
        origin = index_of(lax.rem(line + lines - k, lines), 1 - side, core)
        arrive(origin)
        send(landing.at[origin], origin, partner)
        consume(landing.at[origin], origin)
    for other in (side, 1 - side):
        for k in range(lines):
            if k == 0 and other is side:
                continue
            origin = index_of(lax.rem(line + lines - k, lines), other, 1 - core)
            arrive(origin)
            consume(landing.at[origin], origin)
    for copy in sent:
        copy.wait_send()


def reduce_all(n, me, blocks, bufs, meanwhile=None):
    core_in, side_out, side_in, line_out, line_in, sends, core_sem, side_sem, line_sem = bufs
    lines, line, side, core = place_of(n, me)
    across = index_of(line, 1 - side, core)
    partner = index_of(line, side, 1 - core)
    sent = []

    def copy_of(src, dst, sem, peer, number):
        return pltpu.make_async_remote_copy(
            src_ref=src,
            dst_ref=dst,
            send_sem=sends.at[number],
            recv_sem=sem,
            device_id={"wide": peer},
            device_id_type=MESH,
        )

    def send(src, dst, sem, peer):
        copy = copy_of(src, dst, sem, peer, len(sent))
        copy.start()
        sent.append(copy)

    def arrive(dst, sem):
        copy_of(dst, dst, sem, partner, 0).wait_recv()

    def ahead(k):
        return lax.rem(line + k, lines)

    for k in range(1, lines + 1):
        for turn in range(2):
            other = 1 - side if turn == 0 else side
            slot = ahead(k) * 2 + other
            send(
                blocks.at[index_of(ahead(k), other, 1 - core)],
                core_in.at[slot],
                core_sem.at[slot],
                partner,
            )

    def pair_sum(k, other):
        slot = ahead(k) * 2 + other
        arrive(core_in.at[slot], core_sem.at[slot])
        return blocks[index_of(ahead(k), other, core)].astype(F32) + core_in[slot].astype(F32)

    def second(k):
        slot = ahead(k)
        side_out[slot] = pair_sum(k, 1 - side).astype(BF16)
        send(side_out.at[slot], side_in.at[slot], side_sem.at[slot], across)

    def third(k):
        slot = ahead(k)
        value = pair_sum(k, side)
        arrive(side_in.at[slot], side_sem.at[slot])
        value = value + side_in[slot].astype(F32)
        if k == lines:
            return value
        line_out[slot] = value.astype(BF16)
        send(
            line_out.at[slot],
            line_in.at[line],
            line_sem.at[line],
            index_of(slot, side, core),
        )

    second(1)
    for k in range(1, lines):
        second(k + 1)
        third(k)
    if meanwhile is not None:
        meanwhile()
    total = third(lines)
    for k in range(1, lines):
        slot = lax.rem(line + lines - k, lines)
        arrive(line_in.at[slot], line_sem.at[slot])
        total = total + line_in[slot].astype(F32)
    for copy in sent:
        copy.wait_send()
    return total


LANES = 128


def packed_shape(width, seqs):
    gap = LANES - seqs
    if gap <= 0 or seqs % gap:
        return width, 0, 0
    chunks = seqs // gap
    rest = width // (chunks + 1) // 8 * 8
    return width - rest, rest, gap


def pack_into(target, source):
    width, seqs = source.shape
    kept, rest, gap = packed_shape(width, seqs)
    target[:, :seqs] = source[:kept, :]
    if rest:
        for c in range(seqs // gap):
            target[c * rest : (c + 1) * rest, seqs:] = source[kept:, c * gap : (c + 1) * gap]


def unpack_into(target, value):
    width, seqs = target.shape
    kept, rest, gap = packed_shape(width, seqs)
    target[:kept, :] = value[:, :seqs]
    if rest:
        for c in range(seqs // gap):
            target[kept:, c * gap : (c + 1) * gap] = value[c * rest : (c + 1) * rest, seqs:]


def lane_ids(rows):
    return lax.broadcasted_iota(jnp.int32, (rows, LANES), 1)


def pack(value, seqs, extra=()):
    kept, rest, gap = packed_shape(value.shape[0], seqs)
    tail = value[kept:, :]
    pieces = [pltpu.roll(tail, seqs - c * gap, 1) for c in range(seqs // gap)]
    pieces += [pltpu.roll(row, seqs - c * gap, 1) for row in extra for c in range(seqs // gap)]
    spare = kept - sum(piece.shape[0] for piece in pieces)
    if spare:
        pieces.append(jnp.zeros((spare, LANES), F32))
    return jnp.where(lane_ids(kept) < seqs, value[:kept], jnp.concatenate(pieces, axis=0))


def unpack(value, width, seqs):
    kept, rest, gap = packed_shape(width, seqs)
    chunk = lane_ids(rest) // gap
    tail = jnp.zeros((rest, LANES), F32)
    for c in range(seqs // gap):
        piece = pltpu.roll(value[c * rest : (c + 1) * rest], LANES - seqs + c * gap, 1)
        tail = jnp.where(chunk == c, piece, tail)
    return jnp.concatenate([value[:kept], tail], axis=0)


def extra_rows(width, seqs):
    kept, rest, gap = packed_shape(width, seqs)
    first = rest * (seqs // gap)
    return first, first + 2 * (seqs // gap)


def own_columns(vector, n, me, width):
    whole = vector[...].astype(F32)[None]
    row = jnp.zeros((1, width), F32)
    for i in range(n):
        row = jnp.where(me == i, whole[:, i * width : (i + 1) * width], row)
    return jnp.broadcast_to(row, (LANES, width)).T


def padded(value):
    rows, lanes = value.shape
    return jnp.concatenate([value, jnp.zeros((rows, LANES - lanes), F32)], axis=1)


def halves(value):
    high = value.astype(BF16).astype(F32)
    return high, value - high


def convolved(fresh, window, kernel):
    mixed = fresh * kernel[3:4]
    for k in range(3):
        mixed = mixed + window[k].astype(F32) * kernel[k : k + 1]
    return (mixed * jax.nn.sigmoid(mixed)).astype(BF16).astype(F32)


def gather_kernel(
    n,
    tokens,
    gain,
    inner_hbm,
    maps_hbm,
    step_weights,
    window,
    window_maps,
    taps,
    taps_maps,
    step_bias,
    decay_log,
    skip_gain,
    state_hbm,
    state,
    columns_out,
    decays_out,
    skips_out,
    gates_out,
    in_out,
    out_out,
    landing,
    own,
    raw_inner,
    raw_maps,
    weights,
    total,
    squares,
    mapped,
    arrived,
    load_sems,
    send_sems,
    recv_sems,
    map_send,
    map_recv,
):
    me = lax.axis_index("wide")
    width, seqs = tokens.shape
    inner = window.shape[2]
    cols = window_maps.shape[2]
    heads = step_weights.shape[0]
    load_inner = pltpu.make_async_copy(inner_hbm, raw_inner, load_sems.at[0])
    load_maps = pltpu.make_async_copy(maps_hbm, raw_maps, load_sems.at[1])
    load_state = pltpu.make_async_copy(state_hbm, state, load_sems.at[2])
    load_inner.start()
    load_maps.start()
    load_state.start()
    greet_all(n, me)
    values = padded(tokens[...].astype(F32))
    sums = jnp.sum(values * values, axis=0, keepdims=True)
    scaled = values * own_columns(gain, n, me, width)
    own[...] = pack(scaled, seqs, halves(sums)).astype(BF16)
    total[...] = jnp.zeros_like(total)
    squares[...] = jnp.zeros_like(squares)
    first, last = extra_rows(width, seqs)

    def prepare():
        load_inner.wait()
        load_maps.wait()
        steps = step_weights[...].astype(F32).T.astype(BF16)
        place = lax.broadcasted_iota(jnp.int32, (2 * width, 2 * width), 0)
        wanted = jnp.where(place < width, 2 * place, 2 * (place - width) + 1)
        found = lax.broadcasted_iota(jnp.int32, (2 * width, 2 * width), 1)
        picks = jnp.where(wanted == found, 1.0, 0.0).astype(BF16)
        for i in range(n):
            rows = slice(i * width, (i + 1) * width)
            weights[i, :, :cols] = raw_maps[rows, :]
            weights[i, :, cols : cols + heads] = steps[rows, :]
            pairs = raw_inner[rows].reshape(2 * width, inner)
            split = jnp.dot(picks, pairs, preferred_element_type=F32).astype(BF16)
            for j in range(2):
                at = LANES * 2 + j * inner
                weights[i, :, at : at + inner] = split[j * width : (j + 1) * width]

    def consume(block, origin):
        value = block[...].astype(F32)
        squares[...] += value[first:last]
        fresh = unpack(value, width, seqs)[:, :seqs].astype(BF16)
        total[...] += lax.dot_general(
            fresh, weights[origin], (((0,), (0,)), ((), ())), preferred_element_type=F32
        )

    await_all(n)
    gather_all(n, me, own, landing, send_sems, recv_sems, consume, prepare)
    chunks = (last - first) // 2
    gap = seqs // chunks
    turned = jnp.concatenate([squares[...], jnp.zeros((LANES - last + first, LANES), F32)], axis=0).T
    pieces = [
        turned[seqs:, c : c + 1] + turned[seqs:, chunks + c : chunks + c + 1] for c in range(chunks)
    ]
    mean = jnp.concatenate(pieces, axis=0) / (n * width)
    scale = lax.rsqrt(mean + EPSILON)

    def projected(at, count):
        return (total[:, at : at + count] * scale).astype(BF16).astype(F32)

    mapped[...] = convolved(projected(0, cols), window_maps, taps_maps[...].astype(F32)).astype(BF16)
    half = n // 2
    per_group = half // GROUPS
    readers = HEADS // GROUPS // heads
    kind = me // half
    own_group = lax.rem(me, half) // per_group
    own_slot = kind * per_group + lax.rem(me, per_group)

    def send(r):
        peer = own_group * readers + r
        return peer, pltpu.make_async_remote_copy(
            src_ref=mapped,
            dst_ref=arrived.at[own_slot],
            send_sem=map_send.at[r],
            recv_sem=map_recv.at[own_slot],
            device_id={"wide": peer},
            device_id_type=MESH,
        )

    for r in range(readers):
        peer, copy = send(r)

        @pl.when(peer != me)
        def _():
            copy.start()

        @pl.when(peer == me)
        def _():
            arrived[own_slot] = mapped[...]

    head_ids = lax.broadcasted_iota(jnp.int32, (1, inner), 1) // HEAD_DIM

    def spread(ref):
        wide = jnp.zeros((1, inner), F32)
        for h in range(heads):
            wide = jnp.where(head_ids == h, ref[h], wide)
        return wide

    gate = projected(2 * LANES, inner)
    inputs = convolved(projected(2 * LANES + inner, inner), window, taps[...].astype(F32))
    raw = projected(cols, heads)
    steps = jnp.zeros((seqs, inner), F32)
    for h in range(heads):
        steps = jnp.where(head_ids == h, raw[:, h : h + 1], steps)
    steps = jax.nn.softplus(steps + spread(step_bias))
    decays = jnp.exp(-jnp.exp(spread(decay_log)) * steps)

    def turn(target, value):
        target[:, seqs:] = jnp.zeros((inner, LANES - seqs), F32)
        target[:, :seqs] = value.T

    turn(columns_out, steps * inputs)
    turn(decays_out, decays)
    turn(skips_out, spread(skip_gain) * inputs)
    turn(gates_out, gate * jax.nn.sigmoid(gate))
    group = me // readers
    for slot in range(2 * per_group):
        origin = (slot // per_group) * half + group * per_group + slot % per_group

        @pl.when(origin != me)
        def _():
            pltpu.make_async_remote_copy(
                src_ref=mapped,
                dst_ref=arrived.at[slot],
                send_sem=map_send.at[0],
                recv_sem=map_recv.at[slot],
                device_id={"wide": me},
                device_id_type=MESH,
            ).wait_recv()

    out_out[...] = jnp.zeros_like(out_out)
    for slot in range(per_group):
        part = slice(slot * cols, (slot + 1) * cols)
        in_out[:, part] = arrived[slot].astype(F32)
        out_out[part, :seqs] = arrived[per_group + slot].astype(F32).T
    load_state.wait()
    for r in range(readers):
        peer, copy = send(r)

        @pl.when(peer != me)
        def _():
            copy.wait_send()


def state_kernel(
    rows, state, columns, decays, skips, gates, in_maps, out_maps, new_state, gated, total
):
    step = pl.program_id(0)
    heads = state.shape[1]
    inner, seqs = gated.shape
    first = step * rows
    back = lax.rem(LANES - first, LANES)
    lane = lax.broadcasted_iota(jnp.int32, (STATE, LANES), 1)

    @pl.when(step == 0)
    def _():
        total[...] = jnp.zeros_like(total)

    drive = pltpu.roll(columns[...], back, 1)
    fade = [pltpu.roll(decays[h * HEAD_DIM : h * HEAD_DIM + 8, :], back, 1) for h in range(heads)]
    batch = 4
    found = total[...]
    for start in range(0, rows, batch):
        left, right = [], []
        for j in range(start, start + batch):
            maps = in_maps[pl.ds(first + j, 1), :]
            parts = []
            for h in range(heads):
                slow = jnp.broadcast_to(fade[h][:, j : j + 1], (8, LANES))
                for p in range(0, HEAD_DIM, 8):
                    at = h * HEAD_DIM + p
                    fresh = slow * state[first + j, h, p : p + 8] + drive[at : at + 8, j : j + 1] * maps
                    new_state[j, h, p : p + 8] = fresh
                    parts.append(fresh)
            left.append(jnp.concatenate(parts, axis=0).astype(BF16))
            right.append(jnp.where(lane == first + j, out_maps[...], 0.0).astype(BF16))
        found = found + jnp.dot(
            jnp.concatenate(left, axis=1),
            jnp.concatenate(right, axis=0),
            preferred_element_type=F32,
        )
    total[...] = found

    @pl.when(step == pl.num_programs(0) - 1)
    def _():
        gated[...] = ((total[...] + skips[...]) * gates[...])[:, :seqs]


def gather_old(n, me, own, landing, send_sems, recv_sems, meanwhile=None):
    lines, line, side, core = place_of(n, me)
    across = index_of(line, 1 - side, core)
    partner = index_of(line, side, 1 - core)
    sent = []

    def send(src, origin, peer):
        copy = pltpu.make_async_remote_copy(
            src_ref=src,
            dst_ref=landing.at[origin],
            send_sem=send_sems.at[len(sent)],
            recv_sem=recv_sems.at[origin],
            device_id={"wide": peer},
            device_id_type=MESH,
        )
        copy.start()
        sent.append(copy)

    def arrive(origin):
        pltpu.make_async_remote_copy(
            src_ref=own,
            dst_ref=landing.at[origin],
            send_sem=send_sems.at[0],
            recv_sem=recv_sems.at[origin],
            device_id={"wide": partner},
            device_id_type=MESH,
        ).wait_recv()

    for k in range(1, lines):
        send(own, me, index_of(lax.rem(line + k, lines), side, core))
    send(own, me, across)
    send(own, me, partner)
    landing[me] = own[...]
    if meanwhile is not None:
        meanwhile()
    for k in range(1, lines):
        origin = index_of(lax.rem(line + lines - k, lines), side, core)
        arrive(origin)
        send(landing.at[origin], origin, across)
        send(landing.at[origin], origin, partner)
    for k in range(lines):
        origin = index_of(lax.rem(line + lines - k, lines), 1 - side, core)
        arrive(origin)
        send(landing.at[origin], origin, partner)
    for k in range(lines):
        for other in range(2):
            arrive(index_of(lax.rem(line + lines - k, lines), other, 1 - core))
    for copy in sent:
        copy.wait_send()


def expert_kernel(
    n,
    partners,
    gated,
    gated_gain,
    proj_out,
    tokens,
    moe_gain,
    router,
    expert_ids,
    up_hbm,
    down_hbm,
    result,
    up,
    down,
    terms,
    gains,
    router_hi,
    router_lo,
    packing,
    own,
    outgoing,
    hidden_own,
    hidden_all,
    squares,
    squares_in,
    load_sems,
    square_send,
    square_recv,
    hid_send,
    hid_recv,
    *bufs,
):
    me = lax.axis_index("wide")
    width, seqs = tokens.shape
    load_up = pltpu.make_async_copy(up_hbm, up, load_sems.at[0])
    load_down = pltpu.make_async_copy(down_hbm, down, load_sems.at[1])
    load_up.start()
    load_down.start()
    greet_all(n, me)
    values = gated[...].T
    own_squares = jnp.sum(values * values, axis=1, keepdims=True)
    squares[...] = jnp.broadcast_to(own_squares, squares.shape)
    packing[...] = jnp.zeros_like(packing)
    own[...] = jnp.zeros_like(own)
    terms[:width, :] = tokens[...].astype(F32)
    pack_into(own, terms.at[:width, :])
    await_all(n)
    first = (me // partners) * partners
    place = lax.rem(me, partners)

    def partner_copy(k):
        other = lax.rem(place + k, partners)
        return pltpu.make_async_remote_copy(
            src_ref=squares,
            dst_ref=squares_in.at[k - 1],
            send_sem=square_send.at[k - 1],
            recv_sem=square_recv.at[k - 1],
            device_id={"wide": first + other},
            device_id_type=MESH,
        )

    for k in range(1, partners):
        partner_copy(k).start()
    weighted = (values * gated_gain[...].astype(F32)[None]).astype(BF16)
    mixed = jnp.dot(weighted, proj_out[...], preferred_element_type=F32)
    total = own_squares
    for k in range(1, partners):
        partner_copy(k).wait()
        total = total + squares_in[k - 1][:, :1]
    channels = values.shape[1] * partners
    terms[...] = (mixed * lax.rsqrt(total / channels + EPSILON)).T
    for i in range(n):
        pack_into(packing.at[i], terms.at[i * width : (i + 1) * width, :])
        outgoing[i] = packing[i].astype(BF16)

    def prepare():
        gain = moe_gain[...].astype(F32)[None]
        gains[...] = jnp.broadcast_to(gain, (seqs, gain.shape[1])).T
        folded = router[...].astype(F32) * gain
        high = folded.astype(BF16)
        router_hi[...] = high
        router_lo[...] = (folded - high.astype(F32)).astype(BF16)

    half = len(bufs) // 2
    reduced = reduce_all(n, me, outgoing, bufs[:half], prepare)
    hidden_own[...] = (own[...] + reduced).astype(BF16)
    gather_old(n, me, hidden_own, hidden_all, hid_send, hid_recv)
    for i in range(n):
        unpack_into(terms.at[i * width : (i + 1) * width, :], hidden_all[i].astype(F32))
    values = terms[...]
    mean = jnp.mean(values * values, axis=0, keepdims=True)
    moe_scale = lax.rsqrt(mean + EPSILON)
    rounded = values.astype(BF16)
    moe_input = (values * moe_scale * gains[...]).astype(BF16)
    load_up.wait()
    units = jnp.dot(up[0], moe_input, preferred_element_type=F32)
    logits = moe_scale * (
        jnp.dot(router_hi[...], rounded, preferred_element_type=F32)
        + jnp.dot(router_lo[...], rounded, preferred_element_type=F32)
    )
    expert = lax.broadcasted_iota(jnp.int32, logits.shape, 0)
    named = jnp.zeros(logits.shape, F32)
    for k in range(expert_ids.shape[0]):
        named = named + jnp.where(expert == expert_ids[k : k + 1, :], 1.0, 0.0)
    score = named * jax.nn.sigmoid(logits)
    mine = jnp.sum(jnp.where(expert == me, score, 0.0), axis=0, keepdims=True)
    weight = mine / jnp.sum(score, axis=0, keepdims=True)
    active = jnp.square(jnp.maximum(units, 0.0)).T.astype(BF16)
    load_down.wait()
    served = jnp.dot(active, down[0], preferred_element_type=F32)
    terms[...] = served.T.astype(BF16).astype(F32) * weight
    for i in range(n):
        pack_into(packing.at[i], terms.at[i * width : (i + 1) * width, :])
        outgoing[i] = packing[i].astype(BF16)
    reduced = reduce_all(n, me, outgoing, bufs[half:])
    unpack_into(terms.at[:width, :], hidden_own[...].astype(F32) + reduced)
    result[...] = terms[:width, :].astype(BF16)


def vmem(count):
    return [pl.BlockSpec(memory_space=pltpu.VMEM)] * count


ANY = pl.BlockSpec(memory_space=pltpu.HBM)
DMA = pltpu.SemaphoreType.DMA


def local(
    n,
    tokens,
    mix_gain,
    proj_inner,
    proj_maps,
    proj_step,
    window_inner,
    window_maps,
    kernel_inner,
    kernel_maps,
    step_bias,
    decay_log,
    skip_gain,
    gated_gain,
    proj_out,
    ssm_state,
    moe_gain,
    router_weight,
    expert_ids,
    expert_up,
    expert_down,
):
    seqs, width = tokens.shape
    full_width = proj_inner.shape[0]
    inner = proj_inner.shape[2]
    cols = proj_maps.shape[1]
    heads = proj_step.shape[1]
    readers = HEADS // GROUPS // heads
    slots = 2 * (STATE // cols)
    kept = packed_shape(width, seqs)[0]
    first, last = extra_rows(width, seqs)
    across = 2 * LANES + 2 * inner
    scalars = pl.BlockSpec(memory_space=pltpu.SMEM)
    state, columns, decays, skips, gates, in_maps, out_maps = pl.pallas_call(
        functools.partial(gather_kernel, n),
        out_shape=(
            pltpu.VMEM(ssm_state.shape, F32),
            pltpu.VMEM((inner, LANES), F32),
            pltpu.VMEM((inner, LANES), F32),
            pltpu.VMEM((inner, LANES), F32),
            pltpu.VMEM((inner, LANES), F32),
            pltpu.VMEM((seqs, STATE), F32),
            pltpu.VMEM((STATE, LANES), F32),
        ),
        in_specs=vmem(2) + [ANY] * 2 + vmem(5) + [scalars] * 3 + [ANY],
        out_specs=tuple(vmem(7)),
        scratch_shapes=[
            pltpu.VMEM((n, kept, LANES), BF16),
            pltpu.VMEM((kept, LANES), BF16),
            pltpu.VMEM((full_width, 2, inner), BF16),
            pltpu.VMEM((full_width, cols), BF16),
            pltpu.VMEM((n, width, across), BF16),
            pltpu.VMEM((seqs, across), F32),
            pltpu.VMEM((last - first, LANES), F32),
            pltpu.VMEM((seqs, cols), BF16),
            pltpu.VMEM((slots, seqs, cols), BF16),
            DMA((3,)),
            DMA((n,)),
            DMA((n,)),
            DMA((readers,)),
            DMA((slots,)),
        ],
        compiler_params=pltpu.CompilerParams(
            collective_id=0, has_side_effects=True, vmem_limit_bytes=51 << 20
        ),
        name="gather_tokens",
    )(
        tokens.T,
        mix_gain,
        proj_inner,
        proj_maps,
        proj_step.T,
        window_inner.transpose(1, 0, 2),
        window_maps.transpose(1, 0, 2),
        kernel_inner,
        kernel_maps,
        step_bias,
        decay_log,
        skip_gain,
        ssm_state,
    )
    rows = 16
    new_state, gated = pl.pallas_call(
        functools.partial(state_kernel, rows),
        grid=(seqs // rows,),
        out_shape=(
            jax.ShapeDtypeStruct(ssm_state.shape, F32),
            pltpu.VMEM((inner, seqs), F32),
        ),
        in_specs=vmem(7),
        out_specs=(
            pl.BlockSpec((rows, heads, HEAD_DIM, STATE), lambda i: (i, 0, 0, 0)),
            vmem(1)[0],
        ),
        scratch_shapes=[pltpu.VMEM((inner, LANES), F32)],
        compiler_params=pltpu.CompilerParams(vmem_limit_bytes=16 << 20),
        name="update_state",
    )(state, columns, decays, skips, gates, in_maps, out_maps)
    lines = n // 4

    def piece(count):
        return pltpu.VMEM((count, kept, LANES), BF16)

    reduce_bufs = [
        piece(2 * lines),
        piece(lines),
        piece(lines),
        piece(lines),
        piece(lines),
        DMA((4 * lines - 1,)),
        DMA((2 * lines,)),
        DMA((lines,)),
        DMA((lines,)),
    ]
    up_shape = (1, expert_up.shape[2], full_width)
    next_hidden = pl.pallas_call(
        functools.partial(expert_kernel, n, readers),
        out_shape=jax.ShapeDtypeStruct((width, seqs), BF16),
        in_specs=vmem(7) + [ANY, ANY],
        out_specs=vmem(1)[0],
        scratch_shapes=[
            pltpu.VMEM(up_shape, BF16),
            pltpu.VMEM(expert_down.shape, BF16),
            pltpu.VMEM((full_width, seqs), F32),
            pltpu.VMEM((full_width, seqs), F32),
            pltpu.VMEM((router_weight.shape[1], full_width), BF16),
            pltpu.VMEM((router_weight.shape[1], full_width), BF16),
            pltpu.VMEM((n, kept, LANES), F32),
            pltpu.VMEM((kept, LANES), F32),
            piece(n),
            pltpu.VMEM((kept, LANES), BF16),
            piece(n),
            pltpu.VMEM((seqs, 128), F32),
            pltpu.VMEM((readers - 1, seqs, 128), F32),
            DMA((2,)),
            DMA((readers - 1,)),
            DMA((readers - 1,)),
            DMA((n,)),
            DMA((n,)),
        ]
        + reduce_bufs * 2,
        compiler_params=pltpu.CompilerParams(
            collective_id=1, has_side_effects=True, vmem_limit_bytes=46 << 20
        ),
        name="mix_and_serve",
    )(
        gated,
        gated_gain,
        proj_out,
        tokens.T,
        moe_gain,
        router_weight.T,
        expert_ids.T,
        expert_up.swapaxes(1, 2),
        expert_down,
    )
    return (next_hidden.T, new_state)


def solution(mesh):
    in_specs = (
        P("group", "wide"),
        P(),
        P(None, None, "wide"),
        P(None, "wide"),
        P(None, "wide"),
        P("group", None, "wide"),
        P("group", None, "wide"),
        P(None, "wide"),
        P(None, "wide"),
        P("wide"),
        P("wide"),
        P("wide"),
        P("wide"),
        P("wide", None),
        P("group", "wide", None, None),
        P(),
        P(),
        P("group", None),
        P("wide", None, None),
        P("wide", None, None),
    )
    out_specs = (P("group", "wide"), P("group", "wide", None, None))
    body = functools.partial(local, mesh.shape["wide"])
    return jax.shard_map(body, mesh=mesh, in_specs=in_specs, out_specs=out_specs, check_vma=False)
```

```python
import functools

import jax
import jax.numpy as jnp
from jax import lax
from jax.experimental import pallas as pl
from jax.experimental.pallas import tpu as pltpu
from jax.sharding import PartitionSpec as P

HEADS = 64
HEAD_DIM = 64
STATE = 128
GROUPS = 8
EPSILON = 1e-05
MESH = pl.DeviceIdType.MESH
F32 = jnp.float32
BF16 = jnp.bfloat16


def greet_all(n, me):
    barrier = pltpu.get_barrier_semaphore()

    def greet(k, carry):
        pl.semaphore_signal(
            barrier, inc=1, device_id={"wide": lax.rem(me + k, n)}, device_id_type=MESH
        )
        return carry

    lax.fori_loop(1, n, greet, 0)


def await_all(n):
    pl.semaphore_wait(pltpu.get_barrier_semaphore(), n - 1)


def place_of(n, me):
    lines = n // 4
    return lines, me // 4, lax.rem(me // 2, 2), lax.rem(me, 2)


def index_of(line, side, core):
    return line * 4 + side * 2 + core


def gather_all(n, me, own, landing, send_sems, recv_sems, consume, meanwhile=None):
    lines, line, side, core = place_of(n, me)
    across = index_of(line, 1 - side, core)
    partner = index_of(line, side, 1 - core)
    sent = []

    def send(src, origin, peer):
        copy = pltpu.make_async_remote_copy(
            src_ref=src,
            dst_ref=landing.at[origin],
            send_sem=send_sems.at[len(sent)],
            recv_sem=recv_sems.at[origin],
            device_id={"wide": peer},
            device_id_type=MESH,
        )
        copy.start()
        sent.append(copy)

    def arrive(origin):
        pltpu.make_async_remote_copy(
            src_ref=own,
            dst_ref=landing.at[origin],
            send_sem=send_sems.at[0],
            recv_sem=recv_sems.at[origin],
            device_id={"wide": partner},
            device_id_type=MESH,
        ).wait_recv()

    for k in range(1, lines):
        send(own, me, index_of(lax.rem(line + k, lines), side, core))
    send(own, me, across)
    send(own, me, partner)
    if meanwhile is not None:
        meanwhile()
    consume(own, me)
    arrive(partner)
    consume(landing.at[partner], partner)
    for k in range(1, lines):
        origin = index_of(lax.rem(line + lines - k, lines), side, core)
        arrive(origin)
        send(landing.at[origin], origin, across)
        send(landing.at[origin], origin, partner)
        consume(landing.at[origin], origin)
    for k in range(lines):
        origin = index_of(lax.rem(line + lines - k, lines), 1 - side, core)
        arrive(origin)
        send(landing.at[origin], origin, partner)
        consume(landing.at[origin], origin)
    for other in (side, 1 - side):
        for k in range(lines):
            if k == 0 and other is side:
                continue
            origin = index_of(lax.rem(line + lines - k, lines), other, 1 - core)
            arrive(origin)
            consume(landing.at[origin], origin)
    for copy in sent:
        copy.wait_send()


def reduce_all(n, me, make, enter, bufs, finish, early, late):
    outgoing, mine, core_in, side_out, side_in, line_out, line_in, sends, core_sem, side_sem, line_sem = bufs
    lines, line, side, core = place_of(n, me)
    across = index_of(line, 1 - side, core)
    partner = index_of(line, side, 1 - core)
    sent = []

    def copy_of(src, dst, sem, peer, number):
        return pltpu.make_async_remote_copy(
            src_ref=src,
            dst_ref=dst,
            send_sem=sends.at[number],
            recv_sem=sem,
            device_id={"wide": peer},
            device_id_type=MESH,
        )

    def send(src, dst, sem, peer):
        copy = copy_of(src, dst, sem, peer, len(sent))
        copy.start()
        sent.append(copy)

    def arrive(dst, sem):
        copy_of(dst, dst, sem, partner, 0).wait_recv()

    def ahead(k):
        return lax.rem(line + k, lines)

    order = [(k, other) for k in range(1, lines + 1) for other in (1 - side, side)]
    if enter is not None:
        for number, (k, other) in enumerate(order):
            outgoing[number] = make(index_of(ahead(k), other, 1 - core)).astype(BF16)
        enter()
    for number, (k, other) in enumerate(order):
        if enter is None:
            outgoing[number] = make(index_of(ahead(k), other, 1 - core)).astype(BF16)
        send(outgoing.at[number], core_in.at[number], core_sem.at[number], partner)
    for number, (k, other) in enumerate(order):
        mine[number] = make(index_of(ahead(k), other, core))

    def pair_sum(number):
        arrive(core_in.at[number], core_sem.at[number])
        return finish(mine[number] + core_in[number].astype(F32))

    for k in range(1, lines + 1):
        slot = k - 1
        side_out[slot] = pair_sum(2 * slot).astype(BF16)
        send(side_out.at[slot], side_in.at[slot], side_sem.at[slot], across)
    early()

    def third(k):
        slot = k - 1
        value = pair_sum(2 * slot + 1)
        arrive(side_in.at[slot], side_sem.at[slot])
        return value + side_in[slot].astype(F32)

    for k in range(1, lines):
        line_out[k - 1] = third(k).astype(BF16)
        send(
            line_out.at[k - 1],
            line_in.at[k - 1],
            line_sem.at[k - 1],
            index_of(ahead(k), side, core),
        )
    total = third(lines)
    late()
    for k in range(1, lines):
        arrive(line_in.at[k - 1], line_sem.at[k - 1])
        total = total + line_in[k - 1].astype(F32)
    for copy in sent:
        copy.wait_send()
    return total


LANES = 128


def packed_shape(width, seqs):
    gap = LANES - seqs
    if gap <= 0 or seqs % gap:
        return width, 0, 0
    chunks = seqs // gap
    rest = width // (chunks + 1) // 8 * 8
    return width - rest, rest, gap


def lane_ids(rows):
    return lax.broadcasted_iota(jnp.int32, (rows, LANES), 1)


def pack(value, seqs, extra=()):
    kept, rest, gap = packed_shape(value.shape[0], seqs)
    tail = value[kept:, :]
    pieces = [pltpu.roll(tail, seqs - c * gap, 1) for c in range(seqs // gap)]
    pieces += [pltpu.roll(row, seqs - c * gap, 1) for row in extra for c in range(seqs // gap)]
    spare = kept - sum(piece.shape[0] for piece in pieces)
    if spare:
        pieces.append(jnp.zeros((spare, LANES), F32))
    return jnp.where(lane_ids(kept) < seqs, value[:kept], jnp.concatenate(pieces, axis=0))


def unpack(value, width, seqs):
    kept, rest, gap = packed_shape(width, seqs)
    chunk = lane_ids(rest) // gap
    tail = jnp.zeros((rest, LANES), F32)
    for c in range(seqs // gap):
        piece = pltpu.roll(value[c * rest : (c + 1) * rest], LANES - seqs + c * gap, 1)
        tail = jnp.where(chunk == c, piece, tail)
    return jnp.concatenate([value[:kept], tail], axis=0)


def extra_rows(width, seqs):
    kept, rest, gap = packed_shape(width, seqs)
    first = rest * (seqs // gap)
    return first, first + 2 * (seqs // gap)


def own_columns(vector, n, me, width):
    whole = vector[...].astype(F32)[None]
    row = jnp.zeros((1, width), F32)
    for i in range(n):
        row = jnp.where(me == i, whole[:, i * width : (i + 1) * width], row)
    return jnp.broadcast_to(row, (LANES, width)).T


def padded(value):
    rows, lanes = value.shape
    return jnp.concatenate([value, jnp.zeros((rows, LANES - lanes), F32)], axis=1)


def by_block(target, value, start, width, columns):
    at, count = 0, value.shape[0]
    while at < count:
        block, row = divmod(start + at, width)
        size = min(width - row, count - at)
        target[block, row : row + size, :columns] = value[at : at + size]
        at += size


def token_scale(squares, seqs, channels):
    rows = squares.shape[0]
    chunks = rows // 2
    turned = jnp.concatenate([squares[...], jnp.zeros((LANES - rows, LANES), F32)], axis=0).T
    pieces = [turned[seqs:, c : c + 1] + turned[seqs:, chunks + c : chunks + c + 1] for c in range(chunks)]
    return lax.rsqrt(jnp.concatenate(pieces, axis=0) / channels + EPSILON)


def halves(value):
    high = value.astype(BF16).astype(F32)
    return high, value - high


def convolved(fresh, window, kernel):
    mixed = fresh * kernel[3:4]
    for k in range(3):
        mixed = mixed + window[k].astype(F32) * kernel[k : k + 1]
    return (mixed * jax.nn.sigmoid(mixed)).astype(BF16).astype(F32)


def gather_kernel(
    n,
    tokens,
    gain,
    inner_hbm,
    maps_hbm,
    step_weights,
    window,
    window_maps,
    taps,
    taps_maps,
    step_bias,
    decay_log,
    skip_gain,
    state_hbm,
    proj_hbm,
    gated_gain,
    state,
    columns_out,
    decays_out,
    skips_out,
    gates_out,
    in_out,
    out_out,
    gains_out,
    proj_turned,
    landing,
    own,
    raw_inner,
    raw_maps,
    raw_proj,
    weights,
    total,
    squares,
    mapped,
    arrived,
    load_sems,
    send_sems,
    recv_sems,
    map_send,
    map_recv,
):
    me = lax.axis_index("wide")
    width, seqs = tokens.shape
    inner = window.shape[2]
    cols = window_maps.shape[2]
    heads = step_weights.shape[0]
    load_inner = pltpu.make_async_copy(inner_hbm, raw_inner, load_sems.at[0])
    load_maps = pltpu.make_async_copy(maps_hbm, raw_maps, load_sems.at[1])
    load_state = pltpu.make_async_copy(state_hbm, state, load_sems.at[2])
    load_proj = pltpu.make_async_copy(proj_hbm, raw_proj, load_sems.at[3])
    load_inner.start()
    load_maps.start()
    load_proj.start()
    load_state.start()
    greet_all(n, me)
    values = padded(tokens[...].astype(F32))
    sums = jnp.sum(values * values, axis=0, keepdims=True)
    scaled = values * own_columns(gain, n, me, width)
    own[...] = pack(scaled, seqs, halves(sums)).astype(BF16)
    total[...] = jnp.zeros_like(total)
    squares[...] = jnp.zeros_like(squares)
    first, last = extra_rows(width, seqs)

    def prepare():
        load_inner.wait()
        load_maps.wait()
        steps = step_weights[...].astype(F32).T.astype(BF16)
        place = lax.broadcasted_iota(jnp.int32, (2 * width, 2 * width), 0)
        wanted = jnp.where(place < width, 2 * place, 2 * (place - width) + 1)
        found = lax.broadcasted_iota(jnp.int32, (2 * width, 2 * width), 1)
        picks = jnp.where(wanted == found, 1.0, 0.0).astype(BF16)
        for i in range(n):
            rows = slice(i * width, (i + 1) * width)
            weights[i, :, :cols] = raw_maps[rows, :]
            weights[i, :, cols : cols + heads] = steps[rows, :]
            pairs = raw_inner[rows].reshape(2 * width, inner)
            split = jnp.dot(picks, pairs, preferred_element_type=F32).astype(BF16)
            for j in range(2):
                at = LANES * 2 + j * inner
                weights[i, :, at : at + inner] = split[j * width : (j + 1) * width]
        gains_out[...] = jnp.broadcast_to(gated_gain[...].astype(F32)[None], (LANES, inner)).T
        load_proj.wait()
        for start in range(0, n * width, LANES):
            by_block(proj_turned, raw_proj[:, start : start + LANES].T, start, width, inner)

    def consume(block, origin):
        value = block[...].astype(F32)
        squares[...] += value[first:last]
        fresh = unpack(value, width, seqs)[:, :seqs].astype(BF16)
        total[...] += lax.dot_general(
            fresh, weights[origin], (((0,), (0,)), ((), ())), preferred_element_type=F32
        )

    await_all(n)
    gather_all(n, me, own, landing, send_sems, recv_sems, consume, prepare)
    scale = token_scale(squares, seqs, n * width)

    def projected(at, count):
        return (total[:, at : at + count] * scale).astype(BF16).astype(F32)

    mapped[...] = convolved(projected(0, cols), window_maps, taps_maps[...].astype(F32)).astype(BF16)
    half = n // 2
    per_group = half // GROUPS
    readers = HEADS // GROUPS // heads
    kind = me // half
    own_group = lax.rem(me, half) // per_group
    own_slot = kind * per_group + lax.rem(me, per_group)

    def send(r):
        peer = own_group * readers + r
        return peer, pltpu.make_async_remote_copy(
            src_ref=mapped,
            dst_ref=arrived.at[own_slot],
            send_sem=map_send.at[r],
            recv_sem=map_recv.at[own_slot],
            device_id={"wide": peer},
            device_id_type=MESH,
        )

    for r in range(readers):
        peer, copy = send(r)

        @pl.when(peer != me)
        def _():
            copy.start()

        @pl.when(peer == me)
        def _():
            arrived[own_slot] = mapped[...]

    head_ids = lax.broadcasted_iota(jnp.int32, (1, inner), 1) // HEAD_DIM

    def spread(ref):
        wide = jnp.zeros((1, inner), F32)
        for h in range(heads):
            wide = jnp.where(head_ids == h, ref[h], wide)
        return wide

    gate = projected(2 * LANES, inner)
    inputs = convolved(projected(2 * LANES + inner, inner), window, taps[...].astype(F32))
    raw = projected(cols, heads)
    steps = jnp.zeros((seqs, inner), F32)
    for h in range(heads):
        steps = jnp.where(head_ids == h, raw[:, h : h + 1], steps)
    steps = jax.nn.softplus(steps + spread(step_bias))
    decays = jnp.exp(-jnp.exp(spread(decay_log)) * steps)

    def turn(target, value):
        target[:, seqs:] = jnp.zeros((inner, LANES - seqs), F32)
        target[:, :seqs] = value.T

    turn(columns_out, steps * inputs)
    turn(decays_out, decays)
    turn(skips_out, spread(skip_gain) * inputs)
    turn(gates_out, gate * jax.nn.sigmoid(gate))
    group = me // readers
    for slot in range(2 * per_group):
        origin = (slot // per_group) * half + group * per_group + slot % per_group

        @pl.when(origin != me)
        def _():
            pltpu.make_async_remote_copy(
                src_ref=mapped,
                dst_ref=arrived.at[slot],
                send_sem=map_send.at[0],
                recv_sem=map_recv.at[slot],
                device_id={"wide": me},
                device_id_type=MESH,
            ).wait_recv()

    out_out[...] = jnp.zeros_like(out_out)
    for slot in range(per_group):
        part = slice(slot * cols, (slot + 1) * cols)
        in_out[:, part] = arrived[slot].astype(F32)
        out_out[part, :seqs] = arrived[per_group + slot].astype(F32).T
    load_state.wait()
    for r in range(readers):
        peer, copy = send(r)

        @pl.when(peer != me)
        def _():
            copy.wait_send()


def state_kernel(
    rows, seqs, state, columns, decays, skips, gates, in_maps, out_maps, gains, new_state, weighted, sums, total
):
    step = pl.program_id(0)
    heads = state.shape[1]
    first = step * rows
    back = lax.rem(LANES - first, LANES)
    lane = lax.broadcasted_iota(jnp.int32, (STATE, LANES), 1)

    @pl.when(step == 0)
    def _():
        total[...] = jnp.zeros_like(total)

    drive = pltpu.roll(columns[...], back, 1)
    fade = [pltpu.roll(decays[h * HEAD_DIM : h * HEAD_DIM + 8, :], back, 1) for h in range(heads)]
    batch = 4
    found = total[...]
    for start in range(0, rows, batch):
        left, right = [], []
        for j in range(start, start + batch):
            maps = in_maps[pl.ds(first + j, 1), :]
            parts = []
            for h in range(heads):
                slow = jnp.broadcast_to(fade[h][:, j : j + 1], (8, LANES))
                for p in range(0, HEAD_DIM, 8):
                    at = h * HEAD_DIM + p
                    fresh = slow * state[first + j, h, p : p + 8] + drive[at : at + 8, j : j + 1] * maps
                    new_state[j, h, p : p + 8] = fresh
                    parts.append(fresh)
            left.append(jnp.concatenate(parts, axis=0).astype(BF16))
            right.append(jnp.where(lane == first + j, out_maps[...], 0.0).astype(BF16))
        found = found + jnp.dot(
            jnp.concatenate(left, axis=1),
            jnp.concatenate(right, axis=0),
            preferred_element_type=F32,
        )
    total[...] = found

    @pl.when(step == pl.num_programs(0) - 1)
    def _():
        gated = (total[...] + skips[...]) * gates[...]
        sums[...] = jnp.broadcast_to(jnp.sum(gated * gated, axis=0, keepdims=True), sums.shape)
        weighted[...] = (gated * gains[...]).astype(BF16)


def expert_kernel(
    n,
    partners,
    weighted,
    sums,
    proj_turned,
    tokens,
    moe_gain,
    router,
    expert_ids,
    up_hbm,
    down_hbm,
    result,
    up,
    down,
    up_turned,
    down_turned,
    own,
    landing,
    total,
    squares,
    gains,
    sums_in,
    load_sems,
    sum_send,
    sum_recv,
    hid_send,
    hid_recv,
    *bufs,
):
    me = lax.axis_index("wide")
    width, seqs = tokens.shape
    hidden_units = up.shape[1]
    experts = router.shape[0]
    extent = up_turned.shape[2]
    kept, rest, gap = packed_shape(width, seqs)
    chunks = seqs // gap
    load_up = pltpu.make_async_copy(up_hbm, up, load_sems.at[0])
    load_down = pltpu.make_async_copy(down_hbm, down, load_sems.at[1])
    load_up.start()
    load_down.start()
    greet_all(n, me)
    first = (me // partners) * partners
    place = lax.rem(me, partners)

    def partner_copy(k):
        other = lax.rem(place + k, partners)
        return pltpu.make_async_remote_copy(
            src_ref=sums,
            dst_ref=sums_in.at[k - 1],
            send_sem=sum_send.at[k - 1],
            recv_sem=sum_recv.at[k - 1],
            device_id={"wide": first + other},
            device_id_type=MESH,
        )

    def mixed(i):
        return pack(jnp.dot(proj_turned[i], weighted[...], preferred_element_type=F32), seqs)

    def enter():
        await_all(n)
        for k in range(1, partners):
            partner_copy(k).start()

    scales = []

    def scaled(value):
        if not scales:
            whole = sums[...]
            for k in range(1, partners):
                partner_copy(k).wait()
                whole = whole + sums_in[k - 1]
            row = lax.rsqrt(whole[:1] / (weighted.shape[0] * partners) + EPSILON)
            scales.append(pack(jnp.broadcast_to(row, (width, LANES)), seqs))
        return value * scales[0]

    def turn_up():
        gains[...] = pack(own_columns(moe_gain, n, me, width), seqs)
        load_up.wait()
        for start in range(0, n * width, LANES):
            lanes = slice(start, start + LANES)
            spare = jnp.zeros((extent - hidden_units - experts, LANES), BF16)
            tall = jnp.concatenate([up[0, :, lanes], router[:, lanes], spare], axis=0)
            by_block(up_turned, tall.T, start, width, extent)

    def turn_down():
        load_down.wait()
        for start in range(0, n * width, LANES):
            by_block(down_turned, down[0, :, start : start + LANES].T, start, width, hidden_units)

    def nothing():
        pass

    half = len(bufs) // 2
    reduced = reduce_all(n, me, mixed, enter, bufs[:half], scaled, turn_up, nothing)
    held = pack(padded(tokens[...].astype(F32)), seqs)
    held = (held + reduced).astype(BF16).astype(F32)
    power = held * held
    main = jnp.sum(power, axis=0, keepdims=True)
    extra = []
    for c in range(chunks):
        tail = jnp.sum(power[c * rest : (c + 1) * rest], axis=0, keepdims=True)
        extra.append(pltpu.roll(main, seqs - c * gap, 1) + tail)
    spare = jnp.zeros((kept - rest * chunks - 2 * chunks, LANES), F32)
    both = [halves(row) for row in extra]
    ending = jnp.concatenate([row[0] for row in both] + [row[1] for row in both] + [spare], axis=0)
    sender = held * gains[...]
    inside = lane_ids(kept - rest * chunks) < seqs
    ending = jnp.where(inside, sender[rest * chunks :], ending)
    own[...] = jnp.concatenate([sender[: rest * chunks], ending], axis=0).astype(BF16)
    total[...] = jnp.zeros_like(total)
    squares[...] = jnp.zeros_like(squares)
    begin, end = extra_rows(width, seqs)

    def consume(block, origin):
        value = block[...].astype(F32)
        squares[...] += value[begin:end]
        fresh = unpack(value, width, seqs)[:, :seqs].astype(BF16)
        total[...] += lax.dot_general(
            fresh, up_turned[origin], (((0,), (0,)), ((), ())), preferred_element_type=F32
        )

    gather_all(n, me, own, landing, hid_send, hid_recv, consume, turn_down)
    scale = token_scale(squares, seqs, n * width)
    logits = total[:, hidden_units : hidden_units + experts] * scale
    expert = lax.broadcasted_iota(jnp.int32, (LANES, seqs), 0)
    named = jnp.zeros((LANES, seqs), F32)
    for k in range(expert_ids.shape[0]):
        named = named + jnp.where(expert == expert_ids[k : k + 1, :], 1.0, 0.0)
    score = named.T[:, :experts] * jax.nn.sigmoid(logits)
    lane = lax.broadcasted_iota(jnp.int32, score.shape, 1)
    mine = jnp.sum(jnp.where(lane == me, score, 0.0), axis=1, keepdims=True)
    weight = mine / jnp.sum(score, axis=1, keepdims=True)
    units = jnp.maximum(total[:, :hidden_units] * scale, 0.0)
    active = jnp.square(units) * weight
    active = jnp.concatenate([active, jnp.zeros((LANES - seqs, hidden_units), F32)], axis=0)
    active = active.astype(BF16).T

    def served(i):
        return pack(jnp.dot(down_turned[i], active, preferred_element_type=F32), seqs)

    reduced = reduce_all(n, me, served, None, bufs[half:], lambda value: value, nothing, nothing)
    result[...] = unpack(held + reduced, width, seqs)[:, :seqs].astype(BF16)


def vmem(count):
    return [pl.BlockSpec(memory_space=pltpu.VMEM)] * count


ANY = pl.BlockSpec(memory_space=pltpu.HBM)
DMA = pltpu.SemaphoreType.DMA


def local(
    n,
    tokens,
    mix_gain,
    proj_inner,
    proj_maps,
    proj_step,
    window_inner,
    window_maps,
    kernel_inner,
    kernel_maps,
    step_bias,
    decay_log,
    skip_gain,
    gated_gain,
    proj_out,
    ssm_state,
    moe_gain,
    router_weight,
    expert_ids,
    expert_up,
    expert_down,
):
    seqs, width = tokens.shape
    full_width = proj_inner.shape[0]
    inner = proj_inner.shape[2]
    cols = proj_maps.shape[1]
    heads = proj_step.shape[1]
    readers = HEADS // GROUPS // heads
    slots = 2 * (STATE // cols)
    kept = packed_shape(width, seqs)[0]
    first, last = extra_rows(width, seqs)
    across = 2 * LANES + 2 * inner
    scalars = pl.BlockSpec(memory_space=pltpu.SMEM)
    state, columns, decays, skips, gates, in_maps, out_maps, gains, proj_turned = pl.pallas_call(
        functools.partial(gather_kernel, n),
        out_shape=(
            pltpu.VMEM(ssm_state.shape, F32),
            pltpu.VMEM((inner, LANES), F32),
            pltpu.VMEM((inner, LANES), F32),
            pltpu.VMEM((inner, LANES), F32),
            pltpu.VMEM((inner, LANES), F32),
            pltpu.VMEM((seqs, STATE), F32),
            pltpu.VMEM((STATE, LANES), F32),
            pltpu.VMEM((inner, LANES), F32),
            pltpu.VMEM((n, width, inner), BF16),
        ),
        in_specs=vmem(2) + [ANY] * 2 + vmem(5) + [scalars] * 3 + [ANY] * 2 + vmem(1),
        out_specs=tuple(vmem(9)),
        scratch_shapes=[
            pltpu.VMEM((n, kept, LANES), BF16),
            pltpu.VMEM((kept, LANES), BF16),
            pltpu.VMEM((full_width, 2, inner), BF16),
            pltpu.VMEM((full_width, cols), BF16),
            pltpu.VMEM((inner, full_width), BF16),
            pltpu.VMEM((n, width, across), BF16),
            pltpu.VMEM((seqs, across), F32),
            pltpu.VMEM((last - first, LANES), F32),
            pltpu.VMEM((seqs, cols), BF16),
            pltpu.VMEM((slots, seqs, cols), BF16),
            DMA((4,)),
            DMA((n,)),
            DMA((n,)),
            DMA((readers,)),
            DMA((slots,)),
        ],
        compiler_params=pltpu.CompilerParams(
            collective_id=0, has_side_effects=True, vmem_limit_bytes=49 << 20
        ),
        name="gather_tokens",
    )(
        tokens.T,
        mix_gain,
        proj_inner,
        proj_maps,
        proj_step.T,
        window_inner.transpose(1, 0, 2),
        window_maps.transpose(1, 0, 2),
        kernel_inner,
        kernel_maps,
        step_bias,
        decay_log,
        skip_gain,
        ssm_state,
        proj_out,
        gated_gain,
    )
    rows = 16
    new_state, weighted, sums = pl.pallas_call(
        functools.partial(state_kernel, rows, seqs),
        grid=(seqs // rows,),
        out_shape=(
            jax.ShapeDtypeStruct(ssm_state.shape, F32),
            pltpu.VMEM((inner, LANES), BF16),
            pltpu.VMEM((8, LANES), F32),
        ),
        in_specs=vmem(8),
        out_specs=(
            pl.BlockSpec((rows, heads, HEAD_DIM, STATE), lambda i: (i, 0, 0, 0)),
            *vmem(2),
        ),
        scratch_shapes=[pltpu.VMEM((inner, LANES), F32)],
        compiler_params=pltpu.CompilerParams(vmem_limit_bytes=16 << 20),
        name="update_state",
    )(state, columns, decays, skips, gates, in_maps, out_maps, gains)
    lines = n // 4

    def piece(count, kind=BF16):
        return pltpu.VMEM((count, kept, LANES), kind)

    reduce_bufs = [
        piece(2 * lines),
        piece(2 * lines, F32),
        piece(2 * lines),
        piece(lines),
        piece(lines),
        piece(lines),
        piece(lines),
        DMA((4 * lines - 1,)),
        DMA((2 * lines,)),
        DMA((lines,)),
        DMA((lines,)),
    ]
    hidden_units = expert_up.shape[2]
    experts = router_weight.shape[1]
    extent = -(-(hidden_units + experts) // LANES) * LANES
    next_hidden = pl.pallas_call(
        functools.partial(expert_kernel, n, readers),
        out_shape=jax.ShapeDtypeStruct((width, seqs), BF16),
        in_specs=vmem(7) + [ANY, ANY],
        out_specs=vmem(1)[0],
        scratch_shapes=[
            pltpu.VMEM((1, hidden_units, full_width), BF16),
            pltpu.VMEM(expert_down.shape, BF16),
            pltpu.VMEM((n, width, extent), BF16),
            pltpu.VMEM((n, width, hidden_units), BF16),
            pltpu.VMEM((kept, LANES), BF16),
            piece(n),
            pltpu.VMEM((seqs, extent), F32),
            pltpu.VMEM((last - first, LANES), F32),
            pltpu.VMEM((kept, LANES), F32),
            pltpu.VMEM((readers - 1, 8, LANES), F32),
            DMA((2,)),
            DMA((readers - 1,)),
            DMA((readers - 1,)),
            DMA((n,)),
            DMA((n,)),
        ]
        + reduce_bufs * 2,
        compiler_params=pltpu.CompilerParams(
            collective_id=1, has_side_effects=True, vmem_limit_bytes=50 << 20
        ),
        name="mix_and_serve",
    )(
        weighted,
        sums,
        proj_turned,
        tokens.T,
        moe_gain,
        router_weight.T,
        expert_ids.T,
        expert_up.swapaxes(1, 2),
        expert_down,
    )
    return (next_hidden.T, new_state)


def solution(mesh):
    in_specs = (
        P("group", "wide"),
        P(),
        P(None, None, "wide"),
        P(None, "wide"),
        P(None, "wide"),
        P("group", None, "wide"),
        P("group", None, "wide"),
        P(None, "wide"),
        P(None, "wide"),
        P("wide"),
        P("wide"),
        P("wide"),
        P("wide"),
        P("wide", None),
        P("group", "wide", None, None),
        P(),
        P(),
        P("group", None),
        P("wide", None, None),
        P("wide", None, None),
    )
    out_specs = (P("group", "wide"), P("group", "wide", None, None))
    body = functools.partial(local, mesh.shape["wide"])
    return jax.shard_map(body, mesh=mesh, in_specs=in_specs, out_specs=out_specs, check_vma=False)
```

```python
import functools

import jax
import jax.numpy as jnp
from jax import lax
from jax.experimental import pallas as pl
from jax.experimental.pallas import tpu as pltpu
from jax.sharding import PartitionSpec as P

HEADS = 64
HEAD_DIM = 64
STATE = 128
GROUPS = 8
EPSILON = 1e-05
MESH = pl.DeviceIdType.MESH
F32 = jnp.float32
BF16 = jnp.bfloat16


def greet(peer):
    pl.semaphore_signal(
        pltpu.get_barrier_semaphore(), inc=1, device_id={"wide": peer}, device_id_type=MESH
    )


def await_peers(count):
    pl.semaphore_wait(pltpu.get_barrier_semaphore(), count)


def place_of(n, me):
    lines = n // 4
    return lines, me // 4, lax.rem(me // 2, 2), lax.rem(me, 2)


def index_of(line, side, core):
    return line * 4 + side * 2 + core


def flipped(line, mask, lines):
    if lines & (lines - 1):
        return lax.rem(mask - line + lines, lines)
    moved, bit = 0, 1
    while bit < lines:
        own = lax.rem(line // bit, 2)
        moved = moved + bit * (1 - own if mask & bit else own)
        bit *= 2
    return moved


def meetings(lines):
    return [(mask, turn) for mask in range(lines - 1, -1, -1) for turn in (1, 0) if mask or turn]


def gather_all(n, me, own, landing, send_sems, recv_sems, consume, meanwhile=None):
    lines, line, side, core = place_of(n, me)
    across = index_of(line, 1 - side, core)
    partner = index_of(line, side, 1 - core)
    corner = index_of(line, 1 - side, 1 - core)
    sent = []

    def send(src, origin, peer):
        copy = pltpu.make_async_remote_copy(
            src_ref=src,
            dst_ref=landing.at[origin],
            send_sem=send_sems.at[len(sent)],
            recv_sem=recv_sems.at[origin],
            device_id={"wide": peer},
            device_id_type=MESH,
        )
        copy.start()
        sent.append(copy)

    def arrive(origin):
        pltpu.make_async_remote_copy(
            src_ref=own,
            dst_ref=landing.at[origin],
            send_sem=send_sems.at[0],
            recv_sem=recv_sems.at[origin],
            device_id={"wide": partner},
            device_id_type=MESH,
        ).wait_recv()

    def take(mask, to_side, to_core, peers):
        origin = index_of(flipped(line, mask, lines), to_side, to_core)
        arrive(origin)
        for peer in peers:
            send(landing.at[origin], origin, peer)
        consume(landing.at[origin], origin)

    for mask in range(lines - 1, 0, -1):
        send(own, me, index_of(flipped(line, mask, lines), side, core))
    send(own, me, across)
    send(own, me, partner)
    if meanwhile is not None:
        meanwhile()
    consume(own, me)
    take(0, side, 1 - core, [])
    for mask in range(1, lines):
        take(mask, side, core, [across, corner, partner] if mask > DIRECT else [across, partner])
        if mask == 1:
            take(0, 1 - side, core, [partner])
    take(1, side, 1 - core, [])
    take(0, 1 - side, 1 - core, [])
    for mask in range(1, lines):
        take(mask, 1 - side, core, [] if mask > DIRECT else [partner])
        if mask > 1:
            take(mask, side, 1 - core, [])
    for mask in range(1, lines):
        take(mask, 1 - side, 1 - core, [])
    for copy in sent:
        copy.wait_send()


def reduce_all(n, me, make, enter, bufs, finish, meanwhile):
    outgoing, mine, core_in, leaving, coming, sends, core_sem, chip_sem = bufs
    lines, line, side, core = place_of(n, me)
    partner = index_of(line, side, 1 - core)
    sent = []

    def copy_of(src, dst, sem, peer, number):
        return pltpu.make_async_remote_copy(
            src_ref=src,
            dst_ref=dst,
            send_sem=sends.at[number],
            recv_sem=sem,
            device_id={"wide": peer},
            device_id_type=MESH,
        )

    def send(src, dst, sem, peer):
        copy = copy_of(src, dst, sem, peer, len(sent))
        copy.start()
        sent.append(copy)

    def arrive(dst, sem):
        copy_of(dst, dst, sem, partner, 0).wait_recv()

    others = meetings(lines)
    order = others + [(0, 0)]

    def met(mask, turn, which):
        return index_of(flipped(line, mask, lines), lax.rem(side + turn, 2), which)

    def fill(number):
        outgoing[number] = make(met(*order[number], 1 - core)).astype(BF16)

    def keep(number):
        mine[number] = make(met(*order[number], core))

    numbers = range(len(order))
    if enter is not None:
        for number in numbers:
            fill(number)
        for number in numbers:
            keep(number)
        enter()
    for number in numbers:
        if enter is None:
            fill(number)
        send(outgoing.at[number], core_in.at[number], core_sem.at[number], partner)

    def pair_sum(number):
        if enter is None:
            keep(number)
        arrive(core_in.at[number], core_sem.at[number])
        return finish(mine[number] + core_in[number].astype(F32))

    for number, (mask, turn) in enumerate(others):
        leaving[number] = pair_sum(number).astype(BF16)
        send(leaving.at[number], coming.at[number], chip_sem.at[number], met(mask, turn, core))
    total = pair_sum(len(others))
    meanwhile()
    for number in reversed(range(len(others))):
        arrive(coming.at[number], chip_sem.at[number])
        total = total + coming[number].astype(F32)
    for copy in sent:
        copy.wait_send()
    return total


LANES = 128
DIRECT = 1


def packed_shape(width, seqs):
    gap = LANES - seqs
    if gap <= 0 or seqs % gap:
        return width, 0, 0
    chunks = seqs // gap
    rest = width // (chunks + 1) // 8 * 8
    return width - rest, rest, gap


def lane_ids(rows):
    return lax.broadcasted_iota(jnp.int32, (rows, LANES), 1)


def pack(value, seqs, extra=()):
    kept, rest, gap = packed_shape(value.shape[0], seqs)
    tail = value[kept:, :]
    pieces = [pltpu.roll(tail, seqs - c * gap, 1) for c in range(seqs // gap)]
    pieces += [pltpu.roll(row, seqs - c * gap, 1) for row in extra for c in range(seqs // gap)]
    spare = kept - sum(piece.shape[0] for piece in pieces)
    if spare:
        pieces.append(jnp.zeros((spare, LANES), F32))
    return jnp.where(lane_ids(kept) < seqs, value[:kept], jnp.concatenate(pieces, axis=0))


def unpack(value, width, seqs):
    kept, rest, gap = packed_shape(width, seqs)
    chunk = lane_ids(rest) // gap
    tail = jnp.zeros((rest, LANES), F32)
    for c in range(seqs // gap):
        piece = pltpu.roll(value[c * rest : (c + 1) * rest], LANES - seqs + c * gap, 1)
        tail = jnp.where(chunk == c, piece, tail)
    return jnp.concatenate([value[:kept], tail], axis=0)


def extra_rows(width, seqs):
    kept, rest, gap = packed_shape(width, seqs)
    first = rest * (seqs // gap)
    return first, first + 2 * (seqs // gap)


def own_columns(vector, n, me, width):
    whole = vector[...].astype(F32)[None]
    row = jnp.zeros((1, width), F32)
    for i in range(n):
        row = jnp.where(me == i, whole[:, i * width : (i + 1) * width], row)
    return jnp.broadcast_to(row, (LANES, width)).T


def padded(value):
    rows, lanes = value.shape
    return jnp.concatenate([value, jnp.zeros((rows, LANES - lanes), F32)], axis=1)


def by_block(target, value, start, width, columns):
    at, count = 0, value.shape[0]
    while at < count:
        block, row = divmod(start + at, width)
        size = min(width - row, count - at)
        target[block, row : row + size, :columns] = value[at : at + size]
        at += size


def token_scale(squares, seqs, channels):
    rows = squares.shape[0]
    chunks = rows // 2
    turned = jnp.concatenate([squares[...], jnp.zeros((LANES - rows, LANES), F32)], axis=0).T
    pieces = [turned[seqs:, c : c + 1] + turned[seqs:, chunks + c : chunks + c + 1] for c in range(chunks)]
    return lax.rsqrt(jnp.concatenate(pieces, axis=0) / channels + EPSILON)


def halves(value):
    high = value.astype(BF16).astype(F32)
    return high, value - high


def convolved(fresh, window, kernel):
    mixed = fresh * kernel[3:4]
    for k in range(3):
        mixed = mixed + window[k].astype(F32) * kernel[k : k + 1]
    return (mixed * jax.nn.sigmoid(mixed)).astype(BF16).astype(F32)


def gather_kernel(
    n,
    tokens,
    gain,
    inner_hbm,
    maps_hbm,
    step_weights,
    window,
    window_maps,
    taps,
    taps_maps,
    step_bias,
    decay_log,
    skip_gain,
    state_hbm,
    proj_hbm,
    gated_gain,
    state,
    faded_out,
    packed_out,
    columns_out,
    decays_out,
    skips_out,
    gates_out,
    in_out,
    out_out,
    gains_out,
    proj_turned,
    landing,
    own,
    raw_inner,
    raw_maps,
    raw_proj,
    weights,
    total,
    squares,
    turned,
    mapped,
    arrived,
    load_sems,
    send_sems,
    recv_sems,
    map_send,
    map_recv,
):
    me = lax.axis_index("wide")
    width, seqs = tokens.shape
    inner = window.shape[2]
    cols = window_maps.shape[2]
    heads = step_weights.shape[0]
    load_inner = pltpu.make_async_copy(inner_hbm, raw_inner, load_sems.at[0])
    load_maps = pltpu.make_async_copy(maps_hbm, raw_maps, load_sems.at[1])
    load_state = pltpu.make_async_copy(state_hbm, state, load_sems.at[2])
    load_proj = pltpu.make_async_copy(proj_hbm, raw_proj, load_sems.at[3])
    load_inner.start()
    load_maps.start()
    load_proj.start()
    load_state.start()
    lines, line, side, core = place_of(n, me)
    half = n // 2
    per_group = half // GROUPS
    readers = HEADS // GROUPS // heads
    group = me // readers
    origins = [
        (slot // per_group) * half + group * per_group + slot % per_group
        for slot in range(2 * per_group)
    ]
    reader = lax.rem(me, half) // per_group * readers
    for mask in range(1, lines):
        greet(index_of(flipped(line, mask, lines), side, core))
    for turn in (0, 1):
        greet(index_of(line, 1 - side, (1 - core if turn else core)))
    greet(index_of(line, side, 1 - core))
    for origin in origins:

        @pl.when(origin != me)
        def _():
            greet(origin)

    expected = lines + 2
    for r in range(readers):
        expected = expected + jnp.where(reader + r != me, 1, 0)
    values = padded(tokens[...].astype(F32))
    sums = jnp.sum(values * values, axis=0, keepdims=True)
    scaled = values * own_columns(gain, n, me, width)
    own[...] = pack(scaled, seqs, halves(sums)).astype(BF16)
    total[...] = jnp.zeros_like(total)
    squares[...] = jnp.zeros_like(squares)
    first, last = extra_rows(width, seqs)

    def prepare():
        load_inner.wait()
        load_maps.wait()
        steps = step_weights[...].astype(F32).T.astype(BF16)
        place = lax.broadcasted_iota(jnp.int32, (2 * width, 2 * width), 0)
        wanted = jnp.where(place < width, 2 * place, 2 * (place - width) + 1)
        found = lax.broadcasted_iota(jnp.int32, (2 * width, 2 * width), 1)
        picks = jnp.where(wanted == found, 1.0, 0.0).astype(BF16)
        for i in range(n):
            rows = slice(i * width, (i + 1) * width)
            weights[i, :, :cols] = raw_maps[rows, :]
            weights[i, :, cols : cols + heads] = steps[rows, :]
            pairs = raw_inner[rows].reshape(2 * width, inner)
            split = jnp.dot(picks, pairs, preferred_element_type=F32).astype(BF16)
            for j in range(2):
                at = LANES * 2 + j * inner
                weights[i, :, at : at + inner] = split[j * width : (j + 1) * width]
        gains_out[...] = jnp.broadcast_to(gated_gain[...].astype(F32)[None], (LANES, inner)).T
        load_proj.wait()
        for start in range(0, n * width, LANES):
            by_block(proj_turned, raw_proj[:, start : start + LANES].T, start, width, inner)

    def consume(block, origin):
        value = block[...].astype(F32)
        squares[...] += value[first:last]
        fresh = unpack(value, width, seqs)[:, :seqs].astype(BF16)
        total[...] += lax.dot_general(
            fresh, weights[origin], (((0,), (0,)), ((), ())), preferred_element_type=F32
        )

    await_peers(expected)
    gather_all(n, me, own, landing, send_sems, recv_sems, consume, prepare)
    scale = token_scale(squares, seqs, n * width)

    def projected(at, count):
        return (total[:, at : at + count] * scale).astype(BF16).astype(F32)

    mapped[...] = convolved(projected(0, cols), window_maps, taps_maps[...].astype(F32)).astype(BF16)
    kind = me // half
    own_slot = kind * per_group + lax.rem(me, per_group)

    def send(r):
        peer = reader + r
        return peer, pltpu.make_async_remote_copy(
            src_ref=mapped,
            dst_ref=arrived.at[own_slot],
            send_sem=map_send.at[r],
            recv_sem=map_recv.at[own_slot],
            device_id={"wide": peer},
            device_id_type=MESH,
        )

    for r in range(readers):
        peer, copy = send(r)

        @pl.when(peer != me)
        def _():
            copy.start()

        @pl.when(peer == me)
        def _():
            arrived[own_slot] = mapped[...]

    head_ids = lax.broadcasted_iota(jnp.int32, (1, inner), 1) // HEAD_DIM

    def spread(ref):
        wide = jnp.zeros((1, inner), F32)
        for h in range(heads):
            wide = jnp.where(head_ids == h, ref[h], wide)
        return wide

    small_ids = lax.broadcasted_iota(jnp.int32, (1, heads), 1)

    def small(ref):
        narrow = jnp.zeros((1, heads), F32)
        for h in range(heads):
            narrow = jnp.where(small_ids == h, ref[h], narrow)
        return narrow

    gate = projected(2 * LANES, inner)
    inputs = convolved(projected(2 * LANES + inner, inner), window, taps[...].astype(F32))
    raw = projected(cols, heads)
    raw = jax.nn.softplus(raw + small(step_bias))
    decays = jnp.exp(-jnp.exp(small(decay_log)) * raw)
    steps = jnp.zeros((seqs, inner), F32)
    for h in range(heads):
        decays_out[h] = jnp.broadcast_to(decays[:, h : h + 1], (seqs, LANES))
        steps = jnp.where(head_ids == h, raw[:, h : h + 1], steps)

    def turn(target, value):
        target[:, seqs:] = jnp.zeros((inner, LANES - seqs), F32)
        target[:, :seqs] = value.T

    turn(turned, steps * inputs)
    moved = turned[...]
    middle = inner // 2
    rows = seqs // columns_out.shape[0]
    ahead = lane_ids(middle) < rows
    for i in range(columns_out.shape[0]):
        top = moved[:middle]
        high, low = halves(top)
        packed_out[i] = jnp.where(ahead, high, pltpu.roll(low, rows, 1)).astype(BF16)
        columns_out[i] = moved[middle:]
        moved = pltpu.roll(moved, LANES - rows, 1)
    skipped = spread(skip_gain) * inputs
    turn(gates_out, gate * jax.nn.sigmoid(gate))
    load_state.wait()

    def fade(s, carry):
        for h in range(heads):
            part = slice(h * HEAD_DIM, (h + 1) * HEAD_DIM)
            faded_out[s, part] = (decays_out[h, pl.ds(s, 1), :] * state[s, h]).astype(BF16)
        return carry

    lax.fori_loop(0, seqs, fade, 0, unroll=4)
    for slot, origin in enumerate(origins):

        @pl.when(origin != me)
        def _():
            pltpu.make_async_remote_copy(
                src_ref=mapped,
                dst_ref=arrived.at[slot],
                send_sem=map_send.at[0],
                recv_sem=map_recv.at[slot],
                device_id={"wide": me},
                device_id_type=MESH,
            ).wait_recv()

    out_out[...] = jnp.zeros_like(out_out)
    met = jnp.zeros((1, seqs), F32)
    for slot in range(per_group):
        part = slice(slot * cols, (slot + 1) * cols)
        in_out[:, part] = arrived[slot].astype(F32)
        readers_turned = arrived[per_group + slot].astype(F32).T
        out_out[part, :seqs] = readers_turned
        met = met + jnp.sum(arrived[slot].astype(F32).T * readers_turned, axis=0, keepdims=True)
    skips_out[:, seqs:] = jnp.zeros((inner, LANES - seqs), F32)
    skips_out[:, :seqs] = skipped.T + turned[:, :seqs] * met
    for r in range(readers):
        peer, copy = send(r)

        @pl.when(peer != me)
        def _():
            copy.wait_send()


def state_kernel(
    rows, seqs, state, faded, packed, columns, decays, skips, gates, in_maps, out_maps, gains, new_state, weighted, sums, total
):
    step = pl.program_id(0)
    heads = state.shape[1]
    first = step * rows
    lane = lax.broadcasted_iota(jnp.int32, (STATE, LANES), 1)

    @pl.when(step == 0)
    def _():
        total[...] = jnp.zeros_like(total)

    drive = packed[step][:, : 2 * rows]
    middle = drive.shape[0]
    maps = in_maps[pl.ds(first, rows), :]
    own = lax.broadcasted_iota(jnp.int32, (rows, STATE), 0)
    batch = 2
    found = total[...]
    for start in range(0, rows, batch):
        picked = []
        for j in range(start, start + batch):
            one = jnp.where(own == j, maps, 0.0)
            picked.append(jnp.concatenate([one, one], axis=0))
        driven = jnp.dot(
            drive, jnp.concatenate(picked, axis=1).astype(BF16), preferred_element_type=F32
        )
        for j in range(start, start + batch):
            lanes = slice((j - start) * STATE, (j - start + 1) * STATE)
            row = in_maps[pl.ds(first + j, 1), :]
            for h in range(heads):
                slow = decays[h, pl.ds(first + j, 1), :]
                for p in range(0, HEAD_DIM, 8):
                    at = h * HEAD_DIM + p
                    if at < middle:
                        fresh = driven[at : at + 8, lanes]
                    else:
                        fresh = columns[step, at - middle : at - middle + 8, j : j + 1] * row
                    new_state[j, h, p : p + 8] = slow * state[first + j, h, p : p + 8] + fresh
        left = [faded[first + j] for j in range(start, start + batch)]
        right = [
            jnp.where(lane == first + j, out_maps[...], 0.0).astype(BF16)
            for j in range(start, start + batch)
        ]
        found = found + jnp.dot(
            jnp.concatenate(left, axis=1),
            jnp.concatenate(right, axis=0),
            preferred_element_type=F32,
        )
    total[...] = found

    @pl.when(step == pl.num_programs(0) - 1)
    def _():
        gated = (total[...] + skips[...]) * gates[...]
        sums[...] = jnp.broadcast_to(jnp.sum(gated * gated, axis=0, keepdims=True), sums.shape)
        weighted[...] = (gated * gains[...]).astype(BF16)


def expert_kernel(
    n,
    partners,
    weighted,
    sums,
    proj_turned,
    tokens,
    moe_gain,
    router,
    expert_ids,
    up_hbm,
    down_hbm,
    result,
    up,
    down,
    up_turned,
    down_turned,
    own,
    landing,
    total,
    squares,
    gains,
    sums_in,
    load_sems,
    sum_send,
    sum_recv,
    hid_send,
    hid_recv,
    *bufs,
):
    me = lax.axis_index("wide")
    width, seqs = tokens.shape
    hidden_units = up.shape[1]
    experts = router.shape[0]
    extent = up_turned.shape[2]
    kept, rest, gap = packed_shape(width, seqs)
    chunks = seqs // gap
    load_up = pltpu.make_async_copy(up_hbm, up, load_sems.at[0])
    load_down = pltpu.make_async_copy(down_hbm, down, load_sems.at[1])
    load_up.start()
    load_down.start()
    lines, line, side, core = place_of(n, me)
    first = (me // partners) * partners
    place = lax.rem(me, partners)
    others = meetings(lines)
    for mask, turn in others:
        greet(index_of(flipped(line, mask, lines), lax.rem(side + turn, 2), core))
    greet(index_of(line, 1 - side, 1 - core))
    greet(index_of(line, side, 1 - core))
    for k in range(1, partners):
        greet(first + lax.rem(place + k, partners))

    def partner_copy(k):
        other = lax.rem(place + k, partners)
        return pltpu.make_async_remote_copy(
            src_ref=sums,
            dst_ref=sums_in.at[k - 1],
            send_sem=sum_send.at[k - 1],
            recv_sem=sum_recv.at[k - 1],
            device_id={"wide": first + other},
            device_id_type=MESH,
        )

    def mixed(i):
        return pack(jnp.dot(proj_turned[i], weighted[...], preferred_element_type=F32), seqs)

    def enter():
        await_peers(len(others) + 1 + partners)
        for k in range(1, partners):
            partner_copy(k).start()

    scales = []

    def scaled(value):
        if not scales:
            whole = sums[...]
            for k in range(1, partners):
                partner_copy(k).wait()
                whole = whole + sums_in[k - 1]
            row = lax.rsqrt(whole[:1] / (weighted.shape[0] * partners) + EPSILON)
            scales.append(pack(jnp.broadcast_to(row, (width, LANES)), seqs))
        return value * scales[0]

    def turn_up():
        gains[...] = pack(own_columns(moe_gain, n, me, width), seqs)
        load_up.wait()
        for start in range(0, n * width, LANES):
            lanes = slice(start, start + LANES)
            spare = jnp.zeros((extent - hidden_units - experts, LANES), BF16)
            tall = jnp.concatenate([up[0, :, lanes], router[:, lanes], spare], axis=0)
            by_block(up_turned, tall.T, start, width, extent)

    def turn_down():
        load_down.wait()
        for start in range(0, n * width, LANES):
            by_block(down_turned, down[0, :, start : start + LANES].T, start, width, hidden_units)

    def nothing():
        pass

    half = len(bufs) // 2
    reduced = reduce_all(n, me, mixed, enter, bufs[:half], scaled, turn_up)
    held = pack(padded(tokens[...].astype(F32)), seqs)
    held = (held + reduced).astype(BF16).astype(F32)
    power = held * held
    main = jnp.sum(power, axis=0, keepdims=True)
    extra = []
    for c in range(chunks):
        tail = jnp.sum(power[c * rest : (c + 1) * rest], axis=0, keepdims=True)
        extra.append(pltpu.roll(main, seqs - c * gap, 1) + tail)
    spare = jnp.zeros((kept - rest * chunks - 2 * chunks, LANES), F32)
    both = [halves(row) for row in extra]
    ending = jnp.concatenate([row[0] for row in both] + [row[1] for row in both] + [spare], axis=0)
    sender = held * gains[...]
    inside = lane_ids(kept - rest * chunks) < seqs
    ending = jnp.where(inside, sender[rest * chunks :], ending)
    own[...] = jnp.concatenate([sender[: rest * chunks], ending], axis=0).astype(BF16)
    total[...] = jnp.zeros_like(total)
    squares[...] = jnp.zeros_like(squares)
    begin, end = extra_rows(width, seqs)

    def consume(block, origin):
        value = block[...].astype(F32)
        squares[...] += value[begin:end]
        fresh = unpack(value, width, seqs)[:, :seqs].astype(BF16)
        total[...] += lax.dot_general(
            fresh, up_turned[origin], (((0,), (0,)), ((), ())), preferred_element_type=F32
        )

    gather_all(n, me, own, landing, hid_send, hid_recv, consume, turn_down)
    scale = token_scale(squares, seqs, n * width)
    logits = total[:, hidden_units : hidden_units + experts] * scale
    expert = lax.broadcasted_iota(jnp.int32, (LANES, seqs), 0)
    named = jnp.zeros((LANES, seqs), F32)
    for k in range(expert_ids.shape[0]):
        named = named + jnp.where(expert == expert_ids[k : k + 1, :], 1.0, 0.0)
    score = named.T[:, :experts] * jax.nn.sigmoid(logits)
    lane = lax.broadcasted_iota(jnp.int32, score.shape, 1)
    mine = jnp.sum(jnp.where(lane == me, score, 0.0), axis=1, keepdims=True)
    weight = mine / jnp.sum(score, axis=1, keepdims=True)
    units = jnp.maximum(total[:, :hidden_units] * scale, 0.0)
    active = jnp.square(units) * weight
    active = jnp.concatenate([active, jnp.zeros((LANES - seqs, hidden_units), F32)], axis=0)
    active = active.astype(BF16).T

    def served(i):
        return pack(jnp.dot(down_turned[i], active, preferred_element_type=F32), seqs)

    reduced = reduce_all(n, me, served, None, bufs[half:], lambda value: value, nothing)
    result[...] = unpack(held + reduced, width, seqs)[:, :seqs].astype(BF16)


def vmem(count):
    return [pl.BlockSpec(memory_space=pltpu.VMEM)] * count


ANY = pl.BlockSpec(memory_space=pltpu.HBM)
DMA = pltpu.SemaphoreType.DMA


def local(
    n,
    tokens,
    mix_gain,
    proj_inner,
    proj_maps,
    proj_step,
    window_inner,
    window_maps,
    kernel_inner,
    kernel_maps,
    step_bias,
    decay_log,
    skip_gain,
    gated_gain,
    proj_out,
    ssm_state,
    moe_gain,
    router_weight,
    expert_ids,
    expert_up,
    expert_down,
):
    seqs, width = tokens.shape
    full_width = proj_inner.shape[0]
    inner = proj_inner.shape[2]
    cols = proj_maps.shape[1]
    heads = proj_step.shape[1]
    readers = HEADS // GROUPS // heads
    slots = 2 * (STATE // cols)
    kept = packed_shape(width, seqs)[0]
    first, last = extra_rows(width, seqs)
    across = 2 * LANES + 2 * inner
    scalars = pl.BlockSpec(memory_space=pltpu.SMEM)
    rows = 16
    state, faded, packed, columns, decays, skips, gates, in_maps, out_maps, gains, proj_turned = pl.pallas_call(
        functools.partial(gather_kernel, n),
        out_shape=(
            pltpu.VMEM(ssm_state.shape, F32),
            pltpu.VMEM((seqs, inner, STATE), BF16),
            pltpu.VMEM((seqs // rows, inner // 2, LANES), BF16),
            pltpu.VMEM((seqs // rows, inner // 2, LANES), F32),
            pltpu.VMEM((heads, seqs, LANES), F32),
            pltpu.VMEM((inner, LANES), F32),
            pltpu.VMEM((inner, LANES), F32),
            pltpu.VMEM((seqs, STATE), F32),
            pltpu.VMEM((STATE, LANES), F32),
            pltpu.VMEM((inner, LANES), F32),
            pltpu.VMEM((n, width, inner), BF16),
        ),
        in_specs=vmem(2) + [ANY] * 2 + vmem(5) + [scalars] * 3 + [ANY] * 2 + vmem(1),
        out_specs=tuple(vmem(11)),
        scratch_shapes=[
            pltpu.VMEM((n, kept, LANES), BF16),
            pltpu.VMEM((kept, LANES), BF16),
            pltpu.VMEM((full_width, 2, inner), BF16),
            pltpu.VMEM((full_width, cols), BF16),
            pltpu.VMEM((inner, full_width), BF16),
            pltpu.VMEM((n, width, across), BF16),
            pltpu.VMEM((seqs, across), F32),
            pltpu.VMEM((last - first, LANES), F32),
            pltpu.VMEM((inner, LANES), F32),
            pltpu.VMEM((seqs, cols), BF16),
            pltpu.VMEM((slots, seqs, cols), BF16),
            DMA((4,)),
            DMA((n,)),
            DMA((n,)),
            DMA((readers,)),
            DMA((slots,)),
        ],
        compiler_params=pltpu.CompilerParams(
            collective_id=0, has_side_effects=True, vmem_limit_bytes=42 << 20
        ),
        name="gather_tokens",
    )(
        tokens.T,
        mix_gain,
        proj_inner,
        proj_maps,
        proj_step.T,
        window_inner.transpose(1, 0, 2),
        window_maps.transpose(1, 0, 2),
        kernel_inner,
        kernel_maps,
        step_bias,
        decay_log,
        skip_gain,
        ssm_state,
        proj_out,
        gated_gain,
    )
    new_state, weighted, sums = pl.pallas_call(
        functools.partial(state_kernel, rows, seqs),
        grid=(seqs // rows,),
        out_shape=(
            jax.ShapeDtypeStruct(ssm_state.shape, F32),
            pltpu.VMEM((inner, LANES), BF16),
            pltpu.VMEM((8, LANES), F32),
        ),
        in_specs=vmem(10),
        out_specs=(
            pl.BlockSpec((rows, heads, HEAD_DIM, STATE), lambda i: (i, 0, 0, 0)),
            *vmem(2),
        ),
        scratch_shapes=[pltpu.VMEM((inner, LANES), F32)],
        compiler_params=pltpu.CompilerParams(vmem_limit_bytes=16 << 20),
        name="update_state",
    )(state, faded, packed, columns, decays, skips, gates, in_maps, out_maps, gains)
    chips = n // 2

    def piece(count, kind=BF16):
        return pltpu.VMEM((count, kept, LANES), kind)

    reduce_bufs = [
        piece(chips),
        piece(chips, F32),
        piece(chips),
        piece(chips - 1),
        piece(chips - 1),
        DMA((2 * chips - 1,)),
        DMA((chips,)),
        DMA((chips - 1,)),
    ]
    hidden_units = expert_up.shape[2]
    experts = router_weight.shape[1]
    extent = -(-(hidden_units + experts) // LANES) * LANES
    next_hidden = pl.pallas_call(
        functools.partial(expert_kernel, n, readers),
        out_shape=jax.ShapeDtypeStruct((width, seqs), BF16),
        in_specs=vmem(7) + [ANY, ANY],
        out_specs=vmem(1)[0],
        scratch_shapes=[
            pltpu.VMEM((1, hidden_units, full_width), BF16),
            pltpu.VMEM(expert_down.shape, BF16),
            pltpu.VMEM((n, width, extent), BF16),
            pltpu.VMEM((n, width, hidden_units), BF16),
            pltpu.VMEM((kept, LANES), BF16),
            piece(n),
            pltpu.VMEM((seqs, extent), F32),
            pltpu.VMEM((last - first, LANES), F32),
            pltpu.VMEM((kept, LANES), F32),
            pltpu.VMEM((readers - 1, 8, LANES), F32),
            DMA((2,)),
            DMA((readers - 1,)),
            DMA((readers - 1,)),
            DMA((n,)),
            DMA((n,)),
        ]
        + reduce_bufs * 2,
        compiler_params=pltpu.CompilerParams(
            collective_id=1, has_side_effects=True, vmem_limit_bytes=50 << 20
        ),
        name="mix_and_serve",
    )(
        weighted,
        sums,
        proj_turned,
        tokens.T,
        moe_gain,
        router_weight.T,
        expert_ids.T,
        expert_up.swapaxes(1, 2),
        expert_down,
    )
    return (next_hidden.T, new_state)


def solution(mesh):
    in_specs = (
        P("group", "wide"),
        P(),
        P(None, None, "wide"),
        P(None, "wide"),
        P(None, "wide"),
        P("group", None, "wide"),
        P("group", None, "wide"),
        P(None, "wide"),
        P(None, "wide"),
        P("wide"),
        P("wide"),
        P("wide"),
        P("wide"),
        P("wide", None),
        P("group", "wide", None, None),
        P(),
        P(),
        P("group", None),
        P("wide", None, None),
        P("wide", None, None),
    )
    out_specs = (P("group", "wide"), P("group", "wide", None, None))
    body = functools.partial(local, mesh.shape["wide"])
    return jax.shard_map(body, mesh=mesh, in_specs=in_specs, out_specs=out_specs, check_vma=False)
```

```python
import functools

import jax
import jax.numpy as jnp
from jax import lax
from jax.experimental import pallas as pl
from jax.experimental.pallas import tpu as pltpu
from jax.sharding import PartitionSpec as P

HEADS = 64
HEAD_DIM = 64
STATE = 128
GROUPS = 8
EPSILON = 1e-05
MESH = pl.DeviceIdType.MESH
F32 = jnp.float32
BF16 = jnp.bfloat16


def greet(peer):
    pl.semaphore_signal(
        pltpu.get_barrier_semaphore(), inc=1, device_id={"wide": peer}, device_id_type=MESH
    )


def await_peers(count):
    pl.semaphore_wait(pltpu.get_barrier_semaphore(), count)


def place_of(n, me):
    lines = n // 4
    return lines, me // 4, lax.rem(me // 2, 2), lax.rem(me, 2)


def index_of(line, side, core):
    return line * 4 + side * 2 + core


def flipped(line, mask, lines):
    if lines & (lines - 1):
        return lax.rem(mask - line + lines, lines)
    moved, bit = 0, 1
    while bit < lines:
        own = lax.rem(line // bit, 2)
        moved = moved + bit * (1 - own if mask & bit else own)
        bit *= 2
    return moved


def meetings(lines):
    return [(mask, turn) for mask in range(lines - 1, -1, -1) for turn in (1, 0) if mask or turn]


def gather_all(n, me, own, landing, send_sems, recv_sems, consume, meanwhile=None):
    lines, line, side, core = place_of(n, me)
    across = index_of(line, 1 - side, core)
    partner = index_of(line, side, 1 - core)
    corner = index_of(line, 1 - side, 1 - core)
    sent = []

    def send(src, origin, peer):
        copy = pltpu.make_async_remote_copy(
            src_ref=src,
            dst_ref=landing.at[origin],
            send_sem=send_sems.at[len(sent)],
            recv_sem=recv_sems.at[origin],
            device_id={"wide": peer},
            device_id_type=MESH,
        )
        copy.start()
        sent.append(copy)

    def arrive(origin):
        pltpu.make_async_remote_copy(
            src_ref=own,
            dst_ref=landing.at[origin],
            send_sem=send_sems.at[0],
            recv_sem=recv_sems.at[origin],
            device_id={"wide": partner},
            device_id_type=MESH,
        ).wait_recv()

    def take(mask, to_side, to_core, peers):
        origin = index_of(flipped(line, mask, lines), to_side, to_core)
        arrive(origin)
        for peer in peers:
            send(landing.at[origin], origin, peer)
        consume(landing.at[origin], origin)

    for mask in range(lines - 1, 0, -1):
        send(own, me, index_of(flipped(line, mask, lines), side, core))
    send(own, me, across)
    send(own, me, partner)
    if meanwhile is not None:
        meanwhile()
    consume(own, me)
    take(0, side, 1 - core, [])
    for mask in range(1, lines):
        take(mask, side, core, [across, corner, partner] if mask > DIRECT else [across, partner])
        if mask == 1:
            take(0, 1 - side, core, [partner])
    take(1, side, 1 - core, [])
    take(0, 1 - side, 1 - core, [])
    for mask in range(1, lines):
        take(mask, 1 - side, core, [] if mask > DIRECT else [partner])
        if mask > 1:
            take(mask, side, 1 - core, [])
    for mask in range(1, lines):
        take(mask, 1 - side, 1 - core, [])
    for copy in sent:
        copy.wait_send()


def reduce_all(n, me, make, enter, bufs, finish, meanwhile):
    outgoing, mine, core_in, leaving, coming, sends, core_sem, chip_sem = bufs
    lines, line, side, core = place_of(n, me)
    partner = index_of(line, side, 1 - core)
    sent = []

    def copy_of(src, dst, sem, peer, number):
        return pltpu.make_async_remote_copy(
            src_ref=src,
            dst_ref=dst,
            send_sem=sends.at[number],
            recv_sem=sem,
            device_id={"wide": peer},
            device_id_type=MESH,
        )

    def send(src, dst, sem, peer):
        copy = copy_of(src, dst, sem, peer, len(sent))
        copy.start()
        sent.append(copy)

    def arrive(dst, sem):
        copy_of(dst, dst, sem, partner, 0).wait_recv()

    others = meetings(lines)
    order = others + [(0, 0)]

    def met(mask, turn, which):
        return index_of(flipped(line, mask, lines), lax.rem(side + turn, 2), which)

    def fill(number):
        outgoing[number] = make(met(*order[number], 1 - core)).astype(BF16)

    def keep(number):
        mine[number] = make(met(*order[number], core))

    numbers = range(len(order))
    if enter is not None:
        for number in numbers:
            fill(number)
        for number in numbers:
            keep(number)
        enter()
    for number in numbers:
        if enter is None:
            fill(number)
        send(outgoing.at[number], core_in.at[number], core_sem.at[number], partner)

    def pair_sum(number):
        if enter is None:
            keep(number)
        arrive(core_in.at[number], core_sem.at[number])
        return finish(mine[number] + core_in[number].astype(F32))

    for number, (mask, turn) in enumerate(others):
        leaving[number] = pair_sum(number).astype(BF16)
        send(leaving.at[number], coming.at[number], chip_sem.at[number], met(mask, turn, core))
    total = pair_sum(len(others))
    meanwhile()
    for number in reversed(range(len(others))):
        arrive(coming.at[number], chip_sem.at[number])
        total = total + coming[number].astype(F32)
    for copy in sent:
        copy.wait_send()
    return total


LANES = 128
DIRECT = 2


def packed_shape(width, seqs):
    gap = LANES - seqs
    if gap <= 0 or seqs % gap:
        return width, 0, 0
    chunks = seqs // gap
    rest = width // (chunks + 1) // 8 * 8
    return width - rest, rest, gap


def lane_ids(rows):
    return lax.broadcasted_iota(jnp.int32, (rows, LANES), 1)


def pack(value, seqs, extra=()):
    kept, rest, gap = packed_shape(value.shape[0], seqs)
    tail = value[kept:, :]
    pieces = [pltpu.roll(tail, seqs - c * gap, 1) for c in range(seqs // gap)]
    pieces += [pltpu.roll(row, seqs - c * gap, 1) for row in extra for c in range(seqs // gap)]
    spare = kept - sum(piece.shape[0] for piece in pieces)
    if spare:
        pieces.append(jnp.zeros((spare, LANES), F32))
    return jnp.where(lane_ids(kept) < seqs, value[:kept], jnp.concatenate(pieces, axis=0))


def unpack(value, width, seqs):
    kept, rest, gap = packed_shape(width, seqs)
    chunk = lane_ids(rest) // gap
    tail = jnp.zeros((rest, LANES), F32)
    for c in range(seqs // gap):
        piece = pltpu.roll(value[c * rest : (c + 1) * rest], LANES - seqs + c * gap, 1)
        tail = jnp.where(chunk == c, piece, tail)
    return jnp.concatenate([value[:kept], tail], axis=0)


def extra_rows(width, seqs):
    kept, rest, gap = packed_shape(width, seqs)
    first = rest * (seqs // gap)
    return first, first + 2 * (seqs // gap)


def own_columns(vector, n, me, width):
    whole = vector[...].astype(F32)[None]
    row = jnp.zeros((1, width), F32)
    for i in range(n):
        row = jnp.where(me == i, whole[:, i * width : (i + 1) * width], row)
    return jnp.broadcast_to(row, (LANES, width)).T


def padded(value):
    rows, lanes = value.shape
    return jnp.concatenate([value, jnp.zeros((rows, LANES - lanes), F32)], axis=1)


def by_block(target, value, start, width, columns):
    at, count = 0, value.shape[0]
    while at < count:
        block, row = divmod(start + at, width)
        size = min(width - row, count - at)
        target[block, row : row + size, :columns] = value[at : at + size]
        at += size


def token_scale(squares, seqs, channels):
    rows = squares.shape[0]
    chunks = rows // 2
    turned = jnp.concatenate([squares[...], jnp.zeros((LANES - rows, LANES), F32)], axis=0).T
    pieces = [turned[seqs:, c : c + 1] + turned[seqs:, chunks + c : chunks + c + 1] for c in range(chunks)]
    return lax.rsqrt(jnp.concatenate(pieces, axis=0) / channels + EPSILON)


def halves(value):
    high = value.astype(BF16).astype(F32)
    return high, value - high


def convolved(fresh, window, kernel):
    mixed = fresh * kernel[3:4]
    for k in range(3):
        mixed = mixed + window[k].astype(F32) * kernel[k : k + 1]
    return (mixed * jax.nn.sigmoid(mixed)).astype(BF16).astype(F32)


def gather_kernel(
    n,
    inner_hbm,
    maps_hbm,
    state_hbm,
    proj_hbm,
    tokens_hbm,
    gain_hbm,
    step_weights_hbm,
    window_hbm,
    window_maps_hbm,
    taps_hbm,
    taps_maps_hbm,
    step_bias_hbm,
    decay_log_hbm,
    skip_gain_hbm,
    gated_gain_hbm,
    state,
    faded_out,
    packed_out,
    columns_out,
    decays_out,
    skips_out,
    gates_out,
    in_out,
    out_out,
    gains_out,
    proj_turned,
    landing,
    own,
    tokens,
    gain,
    step_weights,
    window,
    window_maps,
    taps,
    taps_maps,
    step_bias,
    decay_log,
    skip_gain,
    gated_gain,
    raw_inner,
    raw_maps,
    raw_proj,
    weights,
    total,
    squares,
    turned,
    mapped,
    arrived,
    load_sems,
    send_sems,
    recv_sems,
    map_send,
    map_recv,
):
    me = lax.axis_index("wide")
    width, seqs = tokens.shape
    inner = window.shape[2]
    cols = window_maps.shape[2]
    heads = step_weights.shape[0]
    lines, line, side, core = place_of(n, me)
    half = n // 2
    per_group = half // GROUPS
    readers = HEADS // GROUPS // heads
    group = me // readers
    origins = [
        (slot // per_group) * half + group * per_group + slot % per_group
        for slot in range(2 * per_group)
    ]
    reader = lax.rem(me, half) // per_group * readers
    for mask in range(1, lines):
        greet(index_of(flipped(line, mask, lines), side, core))
    for turn in (0, 1):
        greet(index_of(line, 1 - side, (1 - core if turn else core)))
    greet(index_of(line, side, 1 - core))
    for origin in origins:

        @pl.when(origin != me)
        def _():
            greet(origin)

    small = [
        (tokens_hbm, tokens),
        (gain_hbm, gain),
        (step_weights_hbm, step_weights),
        (window_hbm, window),
        (window_maps_hbm, window_maps),
        (taps_hbm, taps),
        (taps_maps_hbm, taps_maps),
        (step_bias_hbm, step_bias),
        (decay_log_hbm, decay_log),
        (skip_gain_hbm, skip_gain),
        (gated_gain_hbm, gated_gain),
    ]
    loads = [
        pltpu.make_async_copy(source, target, load_sems.at[4 + i])
        for i, (source, target) in enumerate(small)
    ]
    for load in loads:
        load.start()
    load_inner = pltpu.make_async_copy(inner_hbm, raw_inner, load_sems.at[0])
    load_maps = pltpu.make_async_copy(maps_hbm, raw_maps, load_sems.at[1])
    load_state = pltpu.make_async_copy(state_hbm, state, load_sems.at[2])
    load_proj = pltpu.make_async_copy(proj_hbm, raw_proj, load_sems.at[3])
    load_inner.start()
    load_maps.start()
    load_proj.start()
    load_state.start()
    expected = lines + 2
    for r in range(readers):
        expected = expected + jnp.where(reader + r != me, 1, 0)
    loads[0].wait()
    loads[1].wait()
    values = padded(tokens[...].astype(F32))
    sums = jnp.sum(values * values, axis=0, keepdims=True)
    scaled = values * own_columns(gain, n, me, width)
    own[...] = pack(scaled, seqs, halves(sums)).astype(BF16)
    total[...] = jnp.zeros_like(total)
    squares[...] = jnp.zeros_like(squares)
    first, last = extra_rows(width, seqs)

    def prepare():
        for load in loads[2:]:
            load.wait()
        load_inner.wait()
        load_maps.wait()
        steps = step_weights[...].astype(F32).T.astype(BF16)
        place = lax.broadcasted_iota(jnp.int32, (2 * width, 2 * width), 0)
        wanted = jnp.where(place < width, 2 * place, 2 * (place - width) + 1)
        found = lax.broadcasted_iota(jnp.int32, (2 * width, 2 * width), 1)
        picks = jnp.where(wanted == found, 1.0, 0.0).astype(BF16)
        for i in range(n):
            rows = slice(i * width, (i + 1) * width)
            weights[i, :, :cols] = raw_maps[rows, :]
            weights[i, :, cols : cols + heads] = steps[rows, :]
            pairs = raw_inner[rows].reshape(2 * width, inner)
            split = jnp.dot(picks, pairs, preferred_element_type=F32).astype(BF16)
            for j in range(2):
                at = LANES * 2 + j * inner
                weights[i, :, at : at + inner] = split[j * width : (j + 1) * width]
        gains_out[...] = jnp.broadcast_to(gated_gain[...].astype(F32)[None], (LANES, inner)).T
        load_proj.wait()
        for start in range(0, n * width, LANES):
            by_block(proj_turned, raw_proj[:, start : start + LANES].T, start, width, inner)

    def consume(block, origin):
        value = block[...].astype(F32)
        squares[...] += value[first:last]
        fresh = unpack(value, width, seqs)[:, :seqs].astype(BF16)
        total[...] += lax.dot_general(
            fresh, weights[origin], (((0,), (0,)), ((), ())), preferred_element_type=F32
        )

    await_peers(expected)
    gather_all(n, me, own, landing, send_sems, recv_sems, consume, prepare)
    scale = token_scale(squares, seqs, n * width)

    def projected(at, count):
        return (total[:, at : at + count] * scale).astype(BF16).astype(F32)

    mapped[...] = convolved(projected(0, cols), window_maps, taps_maps[...].astype(F32)).astype(BF16)
    kind = me // half
    own_slot = kind * per_group + lax.rem(me, per_group)

    def send(r):
        peer = reader + r
        return peer, pltpu.make_async_remote_copy(
            src_ref=mapped,
            dst_ref=arrived.at[own_slot],
            send_sem=map_send.at[r],
            recv_sem=map_recv.at[own_slot],
            device_id={"wide": peer},
            device_id_type=MESH,
        )

    for r in range(readers):
        peer, copy = send(r)

        @pl.when(peer != me)
        def _():
            copy.start()

        @pl.when(peer == me)
        def _():
            arrived[own_slot] = mapped[...]

    head_ids = lax.broadcasted_iota(jnp.int32, (1, inner), 1) // HEAD_DIM

    def spread(ref):
        wide = jnp.zeros((1, inner), F32)
        for h in range(heads):
            wide = jnp.where(head_ids == h, ref[...][None][:, h : h + 1], wide)
        return wide

    gate = projected(2 * LANES, inner)
    inputs = convolved(projected(2 * LANES + inner, inner), window, taps[...].astype(F32))
    raw = projected(cols, heads)
    raw = jax.nn.softplus(raw + step_bias[...][None])
    decays = jnp.exp(-jnp.exp(decay_log[...][None]) * raw)
    steps = jnp.zeros((seqs, inner), F32)
    for h in range(heads):
        decays_out[h] = jnp.broadcast_to(decays[:, h : h + 1], (seqs, LANES))
        steps = jnp.where(head_ids == h, raw[:, h : h + 1], steps)

    def turn(target, value):
        target[:, seqs:] = jnp.zeros((inner, LANES - seqs), F32)
        target[:, :seqs] = value.T

    turn(turned, steps * inputs)
    moved = turned[...]
    middle = inner // 2
    rows = seqs // columns_out.shape[0]
    ahead = lane_ids(middle) < rows
    for i in range(columns_out.shape[0]):
        top = moved[:middle]
        high, low = halves(top)
        packed_out[i] = jnp.where(ahead, high, pltpu.roll(low, rows, 1)).astype(BF16)
        columns_out[i] = moved[middle:]
        moved = pltpu.roll(moved, LANES - rows, 1)
    skipped = spread(skip_gain) * inputs
    turn(gates_out, gate * jax.nn.sigmoid(gate))
    load_state.wait()

    def fade(s, carry):
        for h in range(heads):
            part = slice(h * HEAD_DIM, (h + 1) * HEAD_DIM)
            faded_out[s, part] = (decays_out[h, pl.ds(s, 1), :] * state[s, h]).astype(BF16)
        return carry

    lax.fori_loop(0, seqs, fade, 0, unroll=4)
    for slot, origin in enumerate(origins):

        @pl.when(origin != me)
        def _():
            pltpu.make_async_remote_copy(
                src_ref=mapped,
                dst_ref=arrived.at[slot],
                send_sem=map_send.at[0],
                recv_sem=map_recv.at[slot],
                device_id={"wide": me},
                device_id_type=MESH,
            ).wait_recv()

    out_out[...] = jnp.zeros_like(out_out)
    met = jnp.zeros((1, seqs), F32)
    for slot in range(per_group):
        part = slice(slot * cols, (slot + 1) * cols)
        in_out[:, part] = arrived[slot].astype(F32)
        readers_turned = arrived[per_group + slot].astype(F32).T
        out_out[part, :seqs] = readers_turned
        met = met + jnp.sum(arrived[slot].astype(F32).T * readers_turned, axis=0, keepdims=True)
    skips_out[:, seqs:] = jnp.zeros((inner, LANES - seqs), F32)
    skips_out[:, :seqs] = skipped.T + turned[:, :seqs] * met
    for r in range(readers):
        peer, copy = send(r)

        @pl.when(peer != me)
        def _():
            copy.wait_send()


def state_kernel(
    rows,
    seqs,
    state,
    faded,
    packed,
    columns,
    decays,
    skips,
    gates,
    in_maps,
    out_maps,
    gains,
    new_state,
    weighted,
    sums,
    fresh,
    total,
    store_sems,
):
    heads = state.shape[1]
    lane = lax.broadcasted_iota(jnp.int32, (STATE, LANES), 1)
    own = lax.broadcasted_iota(jnp.int32, (rows, STATE), 0)
    slots, part = fresh.shape[:2]
    middle = packed.shape[1]
    batch = 2
    copies = []
    for start in range(0, seqs, batch):
        step, first = divmod(start, rows)
        chunk, place = divmod(start, part)
        slot = chunk % slots
        if place == 0 and chunk >= slots:
            copies[chunk - slots].wait()
        picked = []
        maps = in_maps[step * rows : (step + 1) * rows, :]
        for j in range(first, first + batch):
            one = jnp.where(own == j, maps, 0.0)
            picked.append(jnp.concatenate([one, one], axis=0))
        driven = jnp.dot(
            packed[step][:, : 2 * rows],
            jnp.concatenate(picked, axis=1).astype(BF16),
            preferred_element_type=F32,
        )
        for i in range(batch):
            lanes = slice(i * STATE, (i + 1) * STATE)
            row = in_maps[start + i : start + i + 1, :]
            for h in range(heads):
                slow = decays[h, start + i : start + i + 1, :]
                for p in range(0, HEAD_DIM, 8):
                    at = h * HEAD_DIM + p
                    if at < middle:
                        drive = driven[at : at + 8, lanes]
                    else:
                        to = at - middle
                        drive = columns[step, to : to + 8, first + i : first + i + 1] * row
                    value = slow * state[start + i, h, p : p + 8] + drive
                    fresh[slot, place + i, h, p : p + 8] = value
        left = [faded[start + i] for i in range(batch)]
        right = [
            jnp.where(lane == start + i, out_maps[...], 0.0).astype(BF16) for i in range(batch)
        ]
        found = jnp.dot(
            jnp.concatenate(left, axis=1),
            jnp.concatenate(right, axis=0),
            preferred_element_type=F32,
        )
        if start:
            found = found + total[...]
        total[...] = found
        if place + batch == part:
            copy = pltpu.make_async_copy(
                fresh.at[slot], new_state.at[pl.ds(chunk * part, part)], store_sems.at[slot]
            )
            copy.start()
            copies.append(copy)
    gated = (total[...] + skips[...]) * gates[...]
    sums[...] = jnp.broadcast_to(jnp.sum(gated * gated, axis=0, keepdims=True), sums.shape)
    weighted[...] = (gated * gains[...]).astype(BF16)
    for copy in copies[-slots:]:
        copy.wait()


def expert_kernel(
    n,
    partners,
    weighted,
    sums,
    proj_turned,
    tokens,
    moe_gain,
    router,
    expert_ids,
    up_hbm,
    down_hbm,
    result,
    up,
    down,
    up_turned,
    down_turned,
    own,
    landing,
    total,
    squares,
    gains,
    sums_in,
    load_sems,
    sum_send,
    sum_recv,
    hid_send,
    hid_recv,
    *bufs,
):
    me = lax.axis_index("wide")
    width, seqs = tokens.shape
    hidden_units = up.shape[1]
    experts = router.shape[0]
    extent = up_turned.shape[2]
    kept, rest, gap = packed_shape(width, seqs)
    chunks = seqs // gap
    lines, line, side, core = place_of(n, me)
    first = (me // partners) * partners
    place = lax.rem(me, partners)
    others = meetings(lines)
    for mask, turn in others:
        greet(index_of(flipped(line, mask, lines), lax.rem(side + turn, 2), core))
    greet(index_of(line, 1 - side, 1 - core))
    greet(index_of(line, side, 1 - core))
    for k in range(1, partners):
        greet(first + lax.rem(place + k, partners))

    load_up = pltpu.make_async_copy(up_hbm, up, load_sems.at[0])
    load_down = pltpu.make_async_copy(down_hbm, down, load_sems.at[1])
    load_up.start()
    load_down.start()

    def partner_copy(k):
        other = lax.rem(place + k, partners)
        return pltpu.make_async_remote_copy(
            src_ref=sums,
            dst_ref=sums_in.at[k - 1],
            send_sem=sum_send.at[k - 1],
            recv_sem=sum_recv.at[k - 1],
            device_id={"wide": first + other},
            device_id_type=MESH,
        )

    def mixed(i):
        return pack(jnp.dot(proj_turned[i], weighted[...], preferred_element_type=F32), seqs)

    def enter():
        await_peers(len(others) + 1 + partners)
        for k in range(1, partners):
            partner_copy(k).start()

    scales = []

    def scaled(value):
        if not scales:
            whole = sums[...]
            for k in range(1, partners):
                partner_copy(k).wait()
                whole = whole + sums_in[k - 1]
            row = lax.rsqrt(whole[:1] / (weighted.shape[0] * partners) + EPSILON)
            scales.append(pack(jnp.broadcast_to(row, (width, LANES)), seqs))
        return value * scales[0]

    def turn_up():
        gains[...] = pack(own_columns(moe_gain, n, me, width), seqs)
        load_up.wait()
        for start in range(0, n * width, LANES):
            lanes = slice(start, start + LANES)
            spare = jnp.zeros((extent - hidden_units - experts, LANES), BF16)
            tall = jnp.concatenate([up[0, :, lanes], router[:, lanes], spare], axis=0)
            by_block(up_turned, tall.T, start, width, extent)

    def turn_down():
        load_down.wait()
        for start in range(0, n * width, LANES):
            by_block(down_turned, down[0, :, start : start + LANES].T, start, width, hidden_units)

    def nothing():
        pass

    half = len(bufs) // 2
    reduced = reduce_all(n, me, mixed, enter, bufs[:half], scaled, turn_up)
    held = pack(padded(tokens[...].astype(F32)), seqs)
    held = (held + reduced).astype(BF16).astype(F32)
    power = held * held
    main = jnp.sum(power, axis=0, keepdims=True)
    extra = []
    for c in range(chunks):
        tail = jnp.sum(power[c * rest : (c + 1) * rest], axis=0, keepdims=True)
        extra.append(pltpu.roll(main, seqs - c * gap, 1) + tail)
    spare = jnp.zeros((kept - rest * chunks - 2 * chunks, LANES), F32)
    both = [halves(row) for row in extra]
    ending = jnp.concatenate([row[0] for row in both] + [row[1] for row in both] + [spare], axis=0)
    sender = held * gains[...]
    inside = lane_ids(kept - rest * chunks) < seqs
    ending = jnp.where(inside, sender[rest * chunks :], ending)
    own[...] = jnp.concatenate([sender[: rest * chunks], ending], axis=0).astype(BF16)
    total[...] = jnp.zeros_like(total)
    squares[...] = jnp.zeros_like(squares)
    begin, end = extra_rows(width, seqs)

    def consume(block, origin):
        value = block[...].astype(F32)
        squares[...] += value[begin:end]
        fresh = unpack(value, width, seqs)[:, :seqs].astype(BF16)
        total[...] += lax.dot_general(
            fresh, up_turned[origin], (((0,), (0,)), ((), ())), preferred_element_type=F32
        )

    gather_all(n, me, own, landing, hid_send, hid_recv, consume, turn_down)
    scale = token_scale(squares, seqs, n * width)
    logits = total[:, hidden_units : hidden_units + experts] * scale
    expert = lax.broadcasted_iota(jnp.int32, (LANES, seqs), 0)
    named = jnp.zeros((LANES, seqs), F32)
    for k in range(expert_ids.shape[0]):
        named = named + jnp.where(expert == expert_ids[k : k + 1, :], 1.0, 0.0)
    score = named.T[:, :experts] * jax.nn.sigmoid(logits)
    lane = lax.broadcasted_iota(jnp.int32, score.shape, 1)
    mine = jnp.sum(jnp.where(lane == me, score, 0.0), axis=1, keepdims=True)
    weight = mine / jnp.sum(score, axis=1, keepdims=True)
    units = jnp.maximum(total[:, :hidden_units] * scale, 0.0)
    active = jnp.square(units) * weight
    active = jnp.concatenate([active, jnp.zeros((LANES - seqs, hidden_units), F32)], axis=0)
    active = active.astype(BF16).T

    def served(i):
        return pack(jnp.dot(down_turned[i], active, preferred_element_type=F32), seqs)

    reduced = reduce_all(n, me, served, None, bufs[half:], lambda value: value, nothing)
    result[...] = unpack(held + reduced, width, seqs)[:, :seqs].astype(BF16)


def vmem(count):
    return [pl.BlockSpec(memory_space=pltpu.VMEM)] * count


ANY = pl.BlockSpec(memory_space=pltpu.HBM)
DMA = pltpu.SemaphoreType.DMA


def local(
    n,
    tokens,
    mix_gain,
    proj_inner,
    proj_maps,
    proj_step,
    window_inner,
    window_maps,
    kernel_inner,
    kernel_maps,
    step_bias,
    decay_log,
    skip_gain,
    gated_gain,
    proj_out,
    ssm_state,
    moe_gain,
    router_weight,
    expert_ids,
    expert_up,
    expert_down,
):
    seqs, width = tokens.shape
    full_width = proj_inner.shape[0]
    inner = proj_inner.shape[2]
    cols = proj_maps.shape[1]
    heads = proj_step.shape[1]
    readers = HEADS // GROUPS // heads
    slots = 2 * (STATE // cols)
    kept = packed_shape(width, seqs)[0]
    first, last = extra_rows(width, seqs)
    across = 2 * LANES + 2 * inner
    small = (
        tokens.T,
        mix_gain,
        proj_step.T,
        window_inner.transpose(1, 0, 2),
        window_maps.transpose(1, 0, 2),
        kernel_inner,
        kernel_maps,
        step_bias,
        decay_log,
        skip_gain,
        gated_gain,
    )
    rows = 16
    state, faded, packed, columns, decays, skips, gates, in_maps, out_maps, gains, proj_turned = pl.pallas_call(
        functools.partial(gather_kernel, n),
        out_shape=(
            pltpu.VMEM(ssm_state.shape, F32),
            pltpu.VMEM((seqs, inner, STATE), BF16),
            pltpu.VMEM((seqs // rows, inner // 2, LANES), BF16),
            pltpu.VMEM((seqs // rows, inner // 2, LANES), F32),
            pltpu.VMEM((heads, seqs, LANES), F32),
            pltpu.VMEM((inner, LANES), F32),
            pltpu.VMEM((inner, LANES), F32),
            pltpu.VMEM((seqs, STATE), F32),
            pltpu.VMEM((STATE, LANES), F32),
            pltpu.VMEM((inner, LANES), F32),
            pltpu.VMEM((n, width, inner), BF16),
        ),
        in_specs=[ANY] * 15,
        out_specs=tuple(vmem(11)),
        scratch_shapes=[
            pltpu.VMEM((n, kept, LANES), BF16),
            pltpu.VMEM((kept, LANES), BF16),
            *(pltpu.VMEM(value.shape, value.dtype) for value in small),
            pltpu.VMEM((full_width, 2, inner), BF16),
            pltpu.VMEM((full_width, cols), BF16),
            pltpu.VMEM((inner, full_width), BF16),
            pltpu.VMEM((n, width, across), BF16),
            pltpu.VMEM((seqs, across), F32),
            pltpu.VMEM((last - first, LANES), F32),
            pltpu.VMEM((inner, LANES), F32),
            pltpu.VMEM((seqs, cols), BF16),
            pltpu.VMEM((slots, seqs, cols), BF16),
            DMA((4 + len(small),)),
            DMA((n,)),
            DMA((n,)),
            DMA((readers,)),
            DMA((slots,)),
        ],
        compiler_params=pltpu.CompilerParams(
            collective_id=0, has_side_effects=True, vmem_limit_bytes=42 << 20
        ),
        name="gather_tokens",
    )(proj_inner, proj_maps, ssm_state, proj_out, *small)
    new_state, weighted, sums = pl.pallas_call(
        functools.partial(state_kernel, rows, seqs),
        out_shape=(
            jax.ShapeDtypeStruct(ssm_state.shape, F32),
            pltpu.VMEM((inner, LANES), BF16),
            pltpu.VMEM((8, LANES), F32),
        ),
        in_specs=vmem(10),
        out_specs=(ANY, *vmem(2)),
        scratch_shapes=[
            pltpu.VMEM((4, 8, heads, HEAD_DIM, STATE), F32),
            pltpu.VMEM((inner, LANES), F32),
            DMA((4,)),
        ],
        compiler_params=pltpu.CompilerParams(vmem_limit_bytes=16 << 20),
        name="update_state",
    )(state, faded, packed, columns, decays, skips, gates, in_maps, out_maps, gains)
    chips = n // 2

    def piece(count, kind=BF16):
        return pltpu.VMEM((count, kept, LANES), kind)

    reduce_bufs = [
        piece(chips),
        piece(chips, F32),
        piece(chips),
        piece(chips - 1),
        piece(chips - 1),
        DMA((2 * chips - 1,)),
        DMA((chips,)),
        DMA((chips - 1,)),
    ]
    hidden_units = expert_up.shape[2]
    experts = router_weight.shape[1]
    extent = -(-(hidden_units + experts) // LANES) * LANES
    next_hidden = pl.pallas_call(
        functools.partial(expert_kernel, n, readers),
        out_shape=jax.ShapeDtypeStruct((width, seqs), BF16),
        in_specs=vmem(7) + [ANY, ANY],
        out_specs=vmem(1)[0],
        scratch_shapes=[
            pltpu.VMEM((1, hidden_units, full_width), BF16),
            pltpu.VMEM(expert_down.shape, BF16),
            pltpu.VMEM((n, width, extent), BF16),
            pltpu.VMEM((n, width, hidden_units), BF16),
            pltpu.VMEM((kept, LANES), BF16),
            piece(n),
            pltpu.VMEM((seqs, extent), F32),
            pltpu.VMEM((last - first, LANES), F32),
            pltpu.VMEM((kept, LANES), F32),
            pltpu.VMEM((readers - 1, 8, LANES), F32),
            DMA((2,)),
            DMA((readers - 1,)),
            DMA((readers - 1,)),
            DMA((n,)),
            DMA((n,)),
        ]
        + reduce_bufs * 2,
        compiler_params=pltpu.CompilerParams(
            collective_id=1, has_side_effects=True, vmem_limit_bytes=50 << 20
        ),
        name="mix_and_serve",
    )(
        weighted,
        sums,
        proj_turned,
        tokens.T,
        moe_gain,
        router_weight.T,
        expert_ids.T,
        expert_up.swapaxes(1, 2),
        expert_down,
    )
    return (next_hidden.T, new_state)


def solution(mesh):
    in_specs = (
        P("group", "wide"),
        P(),
        P(None, None, "wide"),
        P(None, "wide"),
        P(None, "wide"),
        P("group", None, "wide"),
        P("group", None, "wide"),
        P(None, "wide"),
        P(None, "wide"),
        P("wide"),
        P("wide"),
        P("wide"),
        P("wide"),
        P("wide", None),
        P("group", "wide", None, None),
        P(),
        P(),
        P("group", None),
        P("wide", None, None),
        P("wide", None, None),
    )
    out_specs = (P("group", "wide"), P("group", "wide", None, None))
    body = functools.partial(local, mesh.shape["wide"])
    return jax.shard_map(body, mesh=mesh, in_specs=in_specs, out_specs=out_specs, check_vma=False)
```

```python
import functools

import jax
import jax.numpy as jnp
from jax import lax
from jax.experimental import pallas as pl
from jax.experimental.pallas import tpu as pltpu
from jax.sharding import PartitionSpec as P

HEADS = 64
HEAD_DIM = 64
STATE = 128
GROUPS = 8
EPSILON = 1e-05
MESH = pl.DeviceIdType.MESH
F32 = jnp.float32
BF16 = jnp.bfloat16


def greet(peer):
    pl.semaphore_signal(
        pltpu.get_barrier_semaphore(), inc=1, device_id={"wide": peer}, device_id_type=MESH
    )


def await_peers(count):
    pl.semaphore_wait(pltpu.get_barrier_semaphore(), count)


def place_of(n, me):
    lines = n // 4
    return lines, me // 4, lax.rem(me // 2, 2), lax.rem(me, 2)


def index_of(line, side, core):
    return line * 4 + side * 2 + core


def flipped(line, mask, lines):
    if lines & (lines - 1):
        return lax.rem(mask - line + lines, lines)
    moved, bit = 0, 1
    while bit < lines:
        own = lax.rem(line // bit, 2)
        moved = moved + bit * (1 - own if mask & bit else own)
        bit *= 2
    return moved


def meetings(lines):
    return [(mask, turn) for mask in range(lines - 1, -1, -1) for turn in (1, 0) if mask or turn]


def gather_all(n, me, own, landing, send_sems, recv_sems, consume, meanwhile=None):
    lines, line, side, core = place_of(n, me)
    across = index_of(line, 1 - side, core)
    partner = index_of(line, side, 1 - core)
    corner = index_of(line, 1 - side, 1 - core)
    sent = []

    def send(src, origin, peer):
        copy = pltpu.make_async_remote_copy(
            src_ref=src,
            dst_ref=landing.at[origin],
            send_sem=send_sems.at[len(sent)],
            recv_sem=recv_sems.at[origin],
            device_id={"wide": peer},
            device_id_type=MESH,
        )
        copy.start()
        sent.append(copy)

    def arrive(origin):
        pltpu.make_async_remote_copy(
            src_ref=own,
            dst_ref=landing.at[origin],
            send_sem=send_sems.at[0],
            recv_sem=recv_sems.at[origin],
            device_id={"wide": partner},
            device_id_type=MESH,
        ).wait_recv()

    def take(mask, to_side, to_core, peers):
        origin = index_of(flipped(line, mask, lines), to_side, to_core)
        arrive(origin)
        for peer in peers:
            send(landing.at[origin], origin, peer)
        consume(landing.at[origin], origin)

    for mask in range(lines - 1, 0, -1):
        send(own, me, index_of(flipped(line, mask, lines), side, core))
    send(own, me, across)
    send(own, me, partner)
    if meanwhile is not None:
        meanwhile()
    consume(own, me)
    take(0, side, 1 - core, [])
    for mask in range(1, lines):
        take(mask, side, core, [across, corner, partner] if mask > DIRECT else [across, partner])
        if mask == 1:
            take(0, 1 - side, core, [partner])
    take(1, side, 1 - core, [])
    take(0, 1 - side, 1 - core, [])
    for mask in range(1, lines):
        take(mask, 1 - side, core, [] if mask > DIRECT else [partner])
        if mask > 1:
            take(mask, side, 1 - core, [])
    for mask in range(1, lines):
        take(mask, 1 - side, 1 - core, [])
    for copy in sent:
        copy.wait_send()


def reduce_all(n, me, make, enter, bufs, finish, meanwhile, together=2):
    outgoing, mine, core_in, leaving, coming, sends, core_sem, chip_sem = bufs
    lines, line, side, core = place_of(n, me)
    partner = index_of(line, side, 1 - core)
    sent = []

    def copy_of(src, dst, sem, peer, number):
        return pltpu.make_async_remote_copy(
            src_ref=src,
            dst_ref=dst,
            send_sem=sends.at[number],
            recv_sem=sem,
            device_id={"wide": peer},
            device_id_type=MESH,
        )

    def send(src, dst, sem, peer):
        copy = copy_of(src, dst, sem, peer, len(sent))
        copy.start()
        sent.append(copy)

    def arrive(dst, sem):
        copy_of(dst, dst, sem, partner, 0).wait_recv()

    others = meetings(lines)
    order = others + [(0, 0)]

    def met(mask, turn, which):
        return index_of(flipped(line, mask, lines), lax.rem(side + turn, 2), which)

    def group(number):
        return range(number, min(number + together, len(order)))

    def fill(number):
        blocks = make([met(*order[each], 1 - core) for each in group(number)])
        for each, block in zip(group(number), blocks):
            outgoing[each] = block.astype(BF16)

    def keep(number):
        blocks = make([met(*order[each], core) for each in group(number)])
        for each, block in zip(group(number), blocks):
            mine[each] = block

    numbers = range(len(order))
    if enter is not None:
        for number in numbers[::together]:
            fill(number)
        for number in numbers[::together]:
            keep(number)
        enter()
    def give(number):
        if enter is None and number % together == 0:
            fill(number)
        send(outgoing.at[number], core_in.at[number], core_sem.at[number], partner)

    ahead = len(order) if enter is not None else min(AHEAD, len(order))
    for number in range(ahead):
        give(number)

    def pair_sum(number):
        if enter is None and number % together == 0:
            keep(number)
        arrive(core_in.at[number], core_sem.at[number])
        return finish(mine[number] + core_in[number].astype(F32))

    for number, (mask, turn) in enumerate(others):
        leaving[number] = pair_sum(number).astype(BF16)
        send(leaving.at[number], coming.at[number], chip_sem.at[number], met(mask, turn, core))
        if (number + 1) % together == 0:
            for later in group(number + 1 - together + ahead):
                give(later)
    total = pair_sum(len(others))
    meanwhile()
    for number in reversed(range(len(others))):
        arrive(coming.at[number], chip_sem.at[number])
        total = total + coming[number].astype(F32)
    for copy in sent:
        copy.wait_send()
    return total


LANES = 128
DIRECT = 2
AHEAD = 4


def packed_shape(width, seqs):
    gap = LANES - seqs
    if gap <= 0 or seqs % gap:
        return width, 0, 0
    chunks = seqs // gap
    rest = width // (chunks + 1) // 8 * 8
    return width - rest, rest, gap


def lane_ids(rows):
    return lax.broadcasted_iota(jnp.int32, (rows, LANES), 1)


def pack(value, seqs, extra=()):
    kept, rest, gap = packed_shape(value.shape[0], seqs)
    tail = value[kept:, :]
    pieces = [pltpu.roll(tail, seqs - c * gap, 1) for c in range(seqs // gap)]
    pieces += [pltpu.roll(row, seqs - c * gap, 1) for row in extra for c in range(seqs // gap)]
    spare = kept - sum(piece.shape[0] for piece in pieces)
    if spare:
        pieces.append(jnp.zeros((spare, LANES), F32))
    return jnp.where(lane_ids(kept) < seqs, value[:kept], jnp.concatenate(pieces, axis=0))


def unpack(value, width, seqs):
    kept, rest, gap = packed_shape(width, seqs)
    chunk = lane_ids(rest) // gap
    tail = jnp.zeros((rest, LANES), F32)
    for c in range(seqs // gap):
        piece = pltpu.roll(value[c * rest : (c + 1) * rest], LANES - seqs + c * gap, 1)
        tail = jnp.where(chunk == c, piece, tail)
    return jnp.concatenate([value[:kept], tail], axis=0)


def extra_rows(width, seqs):
    kept, rest, gap = packed_shape(width, seqs)
    first = rest * (seqs // gap)
    return first, first + 2 * (seqs // gap)


def own_columns(vector, n, me, width):
    whole = vector[...].astype(F32)[None]
    row = jnp.zeros((1, width), F32)
    for i in range(n):
        row = jnp.where(me == i, whole[:, i * width : (i + 1) * width], row)
    return jnp.broadcast_to(row, (LANES, width)).T


def padded(value):
    rows, lanes = value.shape
    return jnp.concatenate([value, jnp.zeros((rows, LANES - lanes), F32)], axis=1)


def by_block(target, value, start, width, columns):
    at, count = 0, value.shape[0]
    while at < count:
        block, row = divmod(start + at, width)
        size = min(width - row, count - at)
        target[block, row : row + size, :columns] = value[at : at + size]
        at += size


def token_scale(squares, seqs, channels):
    rows = squares.shape[0]
    chunks = rows // 2
    turned = jnp.concatenate([squares[...], jnp.zeros((LANES - rows, LANES), F32)], axis=0).T
    pieces = [turned[seqs:, c : c + 1] + turned[seqs:, chunks + c : chunks + c + 1] for c in range(chunks)]
    return lax.rsqrt(jnp.concatenate(pieces, axis=0) / channels + EPSILON)


def halves(value):
    high = value.astype(BF16).astype(F32)
    return high, value - high


def convolved(fresh, window, kernel):
    mixed = fresh * kernel[3:4]
    for k in range(3):
        mixed = mixed + window[k].astype(F32) * kernel[k : k + 1]
    return (mixed * jax.nn.sigmoid(mixed)).astype(BF16).astype(F32)


def gather_kernel(
    n,
    inner_hbm,
    maps_hbm,
    state_hbm,
    proj_hbm,
    tokens_hbm,
    gain_hbm,
    step_weights_hbm,
    window_hbm,
    window_maps_hbm,
    taps_hbm,
    taps_maps_hbm,
    step_bias_hbm,
    decay_log_hbm,
    skip_gain_hbm,
    gated_gain_hbm,
    state,
    faded_out,
    packed_out,
    columns_out,
    decays_out,
    skips_out,
    gates_out,
    in_out,
    out_out,
    gains_out,
    proj_turned,
    landing,
    own,
    tokens,
    gain,
    step_weights,
    window,
    window_maps,
    taps,
    taps_maps,
    step_bias,
    decay_log,
    skip_gain,
    gated_gain,
    raw_inner,
    raw_maps,
    raw_proj,
    weights,
    total,
    squares,
    turned,
    mapped,
    arrived,
    load_sems,
    send_sems,
    recv_sems,
    map_send,
    map_recv,
):
    me = lax.axis_index("wide")
    width, seqs = tokens.shape
    inner = window.shape[2]
    cols = window_maps.shape[2]
    heads = step_weights.shape[0]
    lines, line, side, core = place_of(n, me)
    half = n // 2
    per_group = half // GROUPS
    readers = HEADS // GROUPS // heads
    group = me // readers
    origins = [
        (slot // per_group) * half + group * per_group + slot % per_group
        for slot in range(2 * per_group)
    ]
    reader = lax.rem(me, half) // per_group * readers
    for mask in range(1, lines):
        greet(index_of(flipped(line, mask, lines), side, core))
    for turn in (0, 1):
        greet(index_of(line, 1 - side, (1 - core if turn else core)))
    greet(index_of(line, side, 1 - core))
    for origin in origins:

        @pl.when(origin != me)
        def _():
            greet(origin)

    small = [
        (tokens_hbm, tokens),
        (gain_hbm, gain),
        (step_weights_hbm, step_weights),
        (window_hbm, window),
        (window_maps_hbm, window_maps),
        (taps_hbm, taps),
        (taps_maps_hbm, taps_maps),
        (step_bias_hbm, step_bias),
        (decay_log_hbm, decay_log),
        (skip_gain_hbm, skip_gain),
        (gated_gain_hbm, gated_gain),
    ]
    loads = [
        pltpu.make_async_copy(source, target, load_sems.at[4 + i])
        for i, (source, target) in enumerate(small)
    ]
    for load in loads:
        load.start()
    load_inner = pltpu.make_async_copy(inner_hbm, raw_inner, load_sems.at[0])
    load_maps = pltpu.make_async_copy(maps_hbm, raw_maps, load_sems.at[1])
    load_state = pltpu.make_async_copy(state_hbm, state, load_sems.at[2])
    load_proj = pltpu.make_async_copy(proj_hbm, raw_proj, load_sems.at[3])
    load_inner.start()
    load_maps.start()
    load_proj.start()
    load_state.start()
    expected = lines + 2
    for r in range(readers):
        expected = expected + jnp.where(reader + r != me, 1, 0)
    loads[0].wait()
    loads[1].wait()
    values = padded(tokens[...].astype(F32))
    sums = jnp.sum(values * values, axis=0, keepdims=True)
    scaled = values * own_columns(gain, n, me, width)
    own[...] = pack(scaled, seqs, halves(sums)).astype(BF16)
    total[...] = jnp.zeros_like(total)
    squares[...] = jnp.zeros_like(squares)
    first, last = extra_rows(width, seqs)

    def prepare():
        for load in loads[2:]:
            load.wait()
        load_inner.wait()
        load_maps.wait()
        steps = step_weights[...].astype(F32).T.astype(BF16)
        place = lax.broadcasted_iota(jnp.int32, (2 * width, 2 * width), 0)
        wanted = jnp.where(place < width, 2 * place, 2 * (place - width) + 1)
        found = lax.broadcasted_iota(jnp.int32, (2 * width, 2 * width), 1)
        picks = jnp.where(wanted == found, 1.0, 0.0).astype(BF16)
        for i in range(n):
            rows = slice(i * width, (i + 1) * width)
            weights[i, :, :cols] = raw_maps[rows, :]
            weights[i, :, cols : cols + heads] = steps[rows, :]
            pairs = raw_inner[rows].reshape(2 * width, inner)
            split = jnp.dot(picks, pairs, preferred_element_type=F32).astype(BF16)
            for j in range(2):
                at = LANES * 2 + j * inner
                weights[i, :, at : at + inner] = split[j * width : (j + 1) * width]
        gains_out[...] = jnp.broadcast_to(gated_gain[...].astype(F32)[None], (LANES, inner)).T
        load_proj.wait()
        for start in range(0, n * width, LANES):
            by_block(proj_turned, raw_proj[:, start : start + LANES].T, start, width, inner)

    def consume(block, origin):
        value = block[...].astype(F32)
        squares[...] += value[first:last]
        fresh = unpack(value, width, seqs)[:, :seqs].astype(BF16)
        total[...] += lax.dot_general(
            fresh, weights[origin], (((0,), (0,)), ((), ())), preferred_element_type=F32
        )

    await_peers(expected)
    gather_all(n, me, own, landing, send_sems, recv_sems, consume, prepare)
    scale = token_scale(squares, seqs, n * width)

    def projected(at, count):
        return (total[:, at : at + count] * scale).astype(BF16).astype(F32)

    mapped[...] = convolved(projected(0, cols), window_maps, taps_maps[...].astype(F32)).astype(BF16)
    kind = me // half
    own_slot = kind * per_group + lax.rem(me, per_group)

    def send(r):
        peer = reader + r
        return peer, pltpu.make_async_remote_copy(
            src_ref=mapped,
            dst_ref=arrived.at[own_slot],
            send_sem=map_send.at[r],
            recv_sem=map_recv.at[own_slot],
            device_id={"wide": peer},
            device_id_type=MESH,
        )

    for r in range(readers):
        peer, copy = send(r)

        @pl.when(peer != me)
        def _():
            copy.start()

        @pl.when(peer == me)
        def _():
            arrived[own_slot] = mapped[...]

    head_ids = lax.broadcasted_iota(jnp.int32, (1, inner), 1) // HEAD_DIM

    def spread(ref):
        wide = jnp.zeros((1, inner), F32)
        for h in range(heads):
            wide = jnp.where(head_ids == h, ref[...][None][:, h : h + 1], wide)
        return wide

    gate = projected(2 * LANES, inner)
    inputs = convolved(projected(2 * LANES + inner, inner), window, taps[...].astype(F32))
    raw = projected(cols, heads)
    raw = jax.nn.softplus(raw + step_bias[...][None])
    decays = jnp.exp(-jnp.exp(decay_log[...][None]) * raw)
    steps = jnp.zeros((seqs, inner), F32)
    for h in range(heads):
        decays_out[h] = jnp.broadcast_to(decays[:, h : h + 1], (seqs, LANES))
        steps = jnp.where(head_ids == h, raw[:, h : h + 1], steps)

    def turn(target, value):
        target[:, seqs:] = jnp.zeros((inner, LANES - seqs), F32)
        target[:, :seqs] = value.T

    turn(turned, steps * inputs)
    moved = turned[...]
    middle = inner // 2
    rows = seqs // columns_out.shape[0]
    ahead = lane_ids(middle) < rows
    for i in range(columns_out.shape[0]):
        top = moved[:middle]
        high, low = halves(top)
        packed_out[i] = jnp.where(ahead, high, pltpu.roll(low, rows, 1)).astype(BF16)
        columns_out[i] = moved[middle:]
        moved = pltpu.roll(moved, LANES - rows, 1)
    skipped = spread(skip_gain) * inputs
    turn(gates_out, gate * jax.nn.sigmoid(gate))
    load_state.wait()

    def fade(s, carry):
        for h in range(heads):
            part = slice(h * HEAD_DIM, (h + 1) * HEAD_DIM)
            faded_out[s, part] = (decays_out[h, pl.ds(s, 1), :] * state[s, h]).astype(BF16)
        return carry

    lax.fori_loop(0, seqs, fade, 0, unroll=4)
    for slot, origin in enumerate(origins):

        @pl.when(origin != me)
        def _():
            pltpu.make_async_remote_copy(
                src_ref=mapped,
                dst_ref=arrived.at[slot],
                send_sem=map_send.at[0],
                recv_sem=map_recv.at[slot],
                device_id={"wide": me},
                device_id_type=MESH,
            ).wait_recv()

    out_out[...] = jnp.zeros_like(out_out)
    met = jnp.zeros((1, seqs), F32)
    for slot in range(per_group):
        part = slice(slot * cols, (slot + 1) * cols)
        in_out[:, part] = arrived[slot].astype(F32)
        readers_turned = arrived[per_group + slot].astype(F32).T
        out_out[part, :seqs] = readers_turned
        met = met + jnp.sum(arrived[slot].astype(F32).T * readers_turned, axis=0, keepdims=True)
    skips_out[:, seqs:] = jnp.zeros((inner, LANES - seqs), F32)
    skips_out[:, :seqs] = skipped.T + turned[:, :seqs] * met
    for r in range(readers):
        peer, copy = send(r)

        @pl.when(peer != me)
        def _():
            copy.wait_send()


def state_kernel(
    rows,
    seqs,
    state,
    faded,
    packed,
    columns,
    decays,
    skips,
    gates,
    in_maps,
    out_maps,
    gains,
    new_state,
    weighted,
    sums,
    fresh,
    total,
    store_sems,
):
    heads = state.shape[1]
    lane = lax.broadcasted_iota(jnp.int32, (STATE, LANES), 1)
    own = lax.broadcasted_iota(jnp.int32, (rows, STATE), 0)
    slots, part = fresh.shape[:2]
    middle = packed.shape[1]
    batch = 2
    copies = []
    for start in range(0, seqs, batch):
        step, first = divmod(start, rows)
        chunk, place = divmod(start, part)
        slot = chunk % slots
        if place == 0 and chunk >= slots:
            copies[chunk - slots].wait()
        picked = []
        maps = in_maps[step * rows : (step + 1) * rows, :]
        for j in range(first, first + batch):
            one = jnp.where(own == j, maps, 0.0)
            picked.append(jnp.concatenate([one, one], axis=0))
        driven = jnp.dot(
            packed[step][:, : 2 * rows],
            jnp.concatenate(picked, axis=1).astype(BF16),
            preferred_element_type=F32,
        )
        for i in range(batch):
            lanes = slice(i * STATE, (i + 1) * STATE)
            row = in_maps[start + i : start + i + 1, :]
            for h in range(heads):
                slow = decays[h, start + i : start + i + 1, :]
                for p in range(0, HEAD_DIM, 8):
                    at = h * HEAD_DIM + p
                    if at < middle:
                        drive = driven[at : at + 8, lanes]
                    else:
                        to = at - middle
                        drive = columns[step, to : to + 8, first + i : first + i + 1] * row
                    value = slow * state[start + i, h, p : p + 8] + drive
                    fresh[slot, place + i, h, p : p + 8] = value
        left = [faded[start + i] for i in range(batch)]
        right = [
            jnp.where(lane == start + i, out_maps[...], 0.0).astype(BF16) for i in range(batch)
        ]
        found = jnp.dot(
            jnp.concatenate(left, axis=1),
            jnp.concatenate(right, axis=0),
            preferred_element_type=F32,
        )
        if start:
            found = found + total[...]
        total[...] = found
        if place + batch == part:
            copy = pltpu.make_async_copy(
                fresh.at[slot], new_state.at[pl.ds(chunk * part, part)], store_sems.at[slot]
            )
            copy.start()
            copies.append(copy)
    gated = (total[...] + skips[...]) * gates[...]
    sums[...] = jnp.broadcast_to(jnp.sum(gated * gated, axis=0, keepdims=True), sums.shape)
    weighted[...] = (gated * gains[...]).astype(BF16)
    for copy in copies[-slots:]:
        copy.wait()


def expert_kernel(
    n,
    partners,
    weighted,
    sums,
    proj_turned,
    tokens,
    moe_gain,
    router,
    expert_ids,
    up_hbm,
    down_hbm,
    result,
    up,
    down,
    up_turned,
    down_turned,
    own,
    landing,
    total,
    squares,
    gains,
    sums_in,
    load_sems,
    sum_send,
    sum_recv,
    hid_send,
    hid_recv,
    *bufs,
):
    me = lax.axis_index("wide")
    width, seqs = tokens.shape
    hidden_units = up.shape[1]
    experts = router.shape[0]
    extent = up_turned.shape[2]
    kept, rest, gap = packed_shape(width, seqs)
    chunks = seqs // gap
    lines, line, side, core = place_of(n, me)
    first = (me // partners) * partners
    place = lax.rem(me, partners)
    others = meetings(lines)
    for mask, turn in others:
        greet(index_of(flipped(line, mask, lines), lax.rem(side + turn, 2), core))
    greet(index_of(line, 1 - side, 1 - core))
    greet(index_of(line, side, 1 - core))
    for k in range(1, partners):
        greet(first + lax.rem(place + k, partners))

    load_up = pltpu.make_async_copy(up_hbm, up, load_sems.at[0])
    load_down = pltpu.make_async_copy(down_hbm, down, load_sems.at[1])
    load_up.start()
    load_down.start()

    def partner_copy(k):
        other = lax.rem(place + k, partners)
        return pltpu.make_async_remote_copy(
            src_ref=sums,
            dst_ref=sums_in.at[k - 1],
            send_sem=sum_send.at[k - 1],
            recv_sem=sum_recv.at[k - 1],
            device_id={"wide": first + other},
            device_id_type=MESH,
        )

    def products(turned, blocks, right):
        tall = jnp.concatenate([turned[i] for i in blocks], axis=0)
        found = jnp.dot(tall, right, preferred_element_type=F32)
        return [pack(found[k * width : (k + 1) * width], seqs) for k in range(len(blocks))]

    def mixed(blocks):
        return products(proj_turned, blocks, weighted[...])

    def enter():
        await_peers(len(others) + 1 + partners)
        for k in range(1, partners):
            partner_copy(k).start()

    scales = []

    def scaled(value):
        if not scales:
            whole = sums[...]
            for k in range(1, partners):
                partner_copy(k).wait()
                whole = whole + sums_in[k - 1]
            row = lax.rsqrt(whole[:1] / (weighted.shape[0] * partners) + EPSILON)
            scales.append(pack(jnp.broadcast_to(row, (width, LANES)), seqs))
        return value * scales[0]

    def turn_up():
        gains[...] = pack(own_columns(moe_gain, n, me, width), seqs)
        load_up.wait()
        for start in range(0, n * width, LANES):
            lanes = slice(start, start + LANES)
            spare = jnp.zeros((extent - hidden_units - experts, LANES), BF16)
            tall = jnp.concatenate([up[0, :, lanes], router[:, lanes], spare], axis=0)
            by_block(up_turned, tall.T, start, width, extent)

    def turn_down():
        load_down.wait()
        for start in range(0, n * width, LANES):
            by_block(down_turned, down[0, :, start : start + LANES].T, start, width, hidden_units)

    def nothing():
        pass

    half = len(bufs) // 2
    reduced = reduce_all(n, me, mixed, enter, bufs[:half], scaled, turn_up)
    held = pack(padded(tokens[...].astype(F32)), seqs)
    held = (held + reduced).astype(BF16).astype(F32)
    power = held * held
    main = jnp.sum(power, axis=0, keepdims=True)
    extra = []
    for c in range(chunks):
        tail = jnp.sum(power[c * rest : (c + 1) * rest], axis=0, keepdims=True)
        extra.append(pltpu.roll(main, seqs - c * gap, 1) + tail)
    spare = jnp.zeros((kept - rest * chunks - 2 * chunks, LANES), F32)
    both = [halves(row) for row in extra]
    ending = jnp.concatenate([row[0] for row in both] + [row[1] for row in both] + [spare], axis=0)
    sender = held * gains[...]
    inside = lane_ids(kept - rest * chunks) < seqs
    ending = jnp.where(inside, sender[rest * chunks :], ending)
    own[...] = jnp.concatenate([sender[: rest * chunks], ending], axis=0).astype(BF16)
    total[...] = jnp.zeros_like(total)
    squares[...] = jnp.zeros_like(squares)
    begin, end = extra_rows(width, seqs)

    def consume(block, origin):
        value = block[...].astype(F32)
        squares[...] += value[begin:end]
        fresh = unpack(value, width, seqs)[:, :seqs].astype(BF16)
        total[...] += lax.dot_general(
            fresh, up_turned[origin], (((0,), (0,)), ((), ())), preferred_element_type=F32
        )

    gather_all(n, me, own, landing, hid_send, hid_recv, consume, turn_down)
    scale = token_scale(squares, seqs, n * width)
    logits = total[:, hidden_units : hidden_units + experts] * scale
    expert = lax.broadcasted_iota(jnp.int32, (LANES, seqs), 0)
    named = jnp.zeros((LANES, seqs), F32)
    for k in range(expert_ids.shape[0]):
        named = named + jnp.where(expert == expert_ids[k : k + 1, :], 1.0, 0.0)
    score = named.T[:, :experts] * jax.nn.sigmoid(logits)
    lane = lax.broadcasted_iota(jnp.int32, score.shape, 1)
    mine = jnp.sum(jnp.where(lane == me, score, 0.0), axis=1, keepdims=True)
    weight = mine / jnp.sum(score, axis=1, keepdims=True)
    units = jnp.maximum(total[:, :hidden_units] * scale, 0.0)
    active = jnp.square(units) * weight
    active = jnp.concatenate([active, jnp.zeros((LANES - seqs, hidden_units), F32)], axis=0)
    active = active.astype(BF16).T

    def served(blocks):
        return products(down_turned, blocks, active)

    reduced = reduce_all(n, me, served, None, bufs[half:], lambda value: value, nothing)
    result[...] = unpack(held + reduced, width, seqs)[:, :seqs].astype(BF16)


def vmem(count):
    return [pl.BlockSpec(memory_space=pltpu.VMEM)] * count


ANY = pl.BlockSpec(memory_space=pltpu.HBM)
DMA = pltpu.SemaphoreType.DMA


def local(
    n,
    tokens,
    mix_gain,
    proj_inner,
    proj_maps,
    proj_step,
    window_inner,
    window_maps,
    kernel_inner,
    kernel_maps,
    step_bias,
    decay_log,
    skip_gain,
    gated_gain,
    proj_out,
    ssm_state,
    moe_gain,
    router_weight,
    expert_ids,
    expert_up,
    expert_down,
):
    seqs, width = tokens.shape
    full_width = proj_inner.shape[0]
    inner = proj_inner.shape[2]
    cols = proj_maps.shape[1]
    heads = proj_step.shape[1]
    readers = HEADS // GROUPS // heads
    slots = 2 * (STATE // cols)
    kept = packed_shape(width, seqs)[0]
    first, last = extra_rows(width, seqs)
    across = 2 * LANES + 2 * inner
    small = (
        tokens.T,
        mix_gain,
        proj_step.T,
        window_inner.transpose(1, 0, 2),
        window_maps.transpose(1, 0, 2),
        kernel_inner,
        kernel_maps,
        step_bias,
        decay_log,
        skip_gain,
        gated_gain,
    )
    rows = 16
    state, faded, packed, columns, decays, skips, gates, in_maps, out_maps, gains, proj_turned = pl.pallas_call(
        functools.partial(gather_kernel, n),
        out_shape=(
            pltpu.VMEM(ssm_state.shape, F32),
            pltpu.VMEM((seqs, inner, STATE), BF16),
            pltpu.VMEM((seqs // rows, inner // 2, LANES), BF16),
            pltpu.VMEM((seqs // rows, inner // 2, LANES), F32),
            pltpu.VMEM((heads, seqs, LANES), F32),
            pltpu.VMEM((inner, LANES), F32),
            pltpu.VMEM((inner, LANES), F32),
            pltpu.VMEM((seqs, STATE), F32),
            pltpu.VMEM((STATE, LANES), F32),
            pltpu.VMEM((inner, LANES), F32),
            pltpu.VMEM((n, width, inner), BF16),
        ),
        in_specs=[ANY] * 15,
        out_specs=tuple(vmem(11)),
        scratch_shapes=[
            pltpu.VMEM((n, kept, LANES), BF16),
            pltpu.VMEM((kept, LANES), BF16),
            *(pltpu.VMEM(value.shape, value.dtype) for value in small),
            pltpu.VMEM((full_width, 2, inner), BF16),
            pltpu.VMEM((full_width, cols), BF16),
            pltpu.VMEM((inner, full_width), BF16),
            pltpu.VMEM((n, width, across), BF16),
            pltpu.VMEM((seqs, across), F32),
            pltpu.VMEM((last - first, LANES), F32),
            pltpu.VMEM((inner, LANES), F32),
            pltpu.VMEM((seqs, cols), BF16),
            pltpu.VMEM((slots, seqs, cols), BF16),
            DMA((4 + len(small),)),
            DMA((n,)),
            DMA((n,)),
            DMA((readers,)),
            DMA((slots,)),
        ],
        compiler_params=pltpu.CompilerParams(
            collective_id=0, has_side_effects=True, vmem_limit_bytes=42 << 20
        ),
        name="gather_tokens",
    )(proj_inner, proj_maps, ssm_state, proj_out, *small)
    new_state, weighted, sums = pl.pallas_call(
        functools.partial(state_kernel, rows, seqs),
        out_shape=(
            jax.ShapeDtypeStruct(ssm_state.shape, F32),
            pltpu.VMEM((inner, LANES), BF16),
            pltpu.VMEM((8, LANES), F32),
        ),
        in_specs=vmem(10),
        out_specs=(ANY, *vmem(2)),
        scratch_shapes=[
            pltpu.VMEM((4, 8, heads, HEAD_DIM, STATE), F32),
            pltpu.VMEM((inner, LANES), F32),
            DMA((4,)),
        ],
        compiler_params=pltpu.CompilerParams(vmem_limit_bytes=16 << 20),
        name="update_state",
    )(state, faded, packed, columns, decays, skips, gates, in_maps, out_maps, gains)
    chips = n // 2

    def piece(count, kind=BF16):
        return pltpu.VMEM((count, kept, LANES), kind)

    reduce_bufs = [
        piece(chips),
        piece(chips, F32),
        piece(chips),
        piece(chips - 1),
        piece(chips - 1),
        DMA((2 * chips - 1,)),
        DMA((chips,)),
        DMA((chips - 1,)),
    ]
    hidden_units = expert_up.shape[2]
    experts = router_weight.shape[1]
    extent = -(-(hidden_units + experts) // LANES) * LANES
    next_hidden = pl.pallas_call(
        functools.partial(expert_kernel, n, readers),
        out_shape=jax.ShapeDtypeStruct((width, seqs), BF16),
        in_specs=vmem(7) + [ANY, ANY],
        out_specs=vmem(1)[0],
        scratch_shapes=[
            pltpu.VMEM((1, hidden_units, full_width), BF16),
            pltpu.VMEM(expert_down.shape, BF16),
            pltpu.VMEM((n, width, extent), BF16),
            pltpu.VMEM((n, width, hidden_units), BF16),
            pltpu.VMEM((kept, LANES), BF16),
            piece(n),
            pltpu.VMEM((seqs, extent), F32),
            pltpu.VMEM((last - first, LANES), F32),
            pltpu.VMEM((kept, LANES), F32),
            pltpu.VMEM((readers - 1, 8, LANES), F32),
            DMA((2,)),
            DMA((readers - 1,)),
            DMA((readers - 1,)),
            DMA((n,)),
            DMA((n,)),
        ]
        + reduce_bufs * 2,
        compiler_params=pltpu.CompilerParams(
            collective_id=1, has_side_effects=True, vmem_limit_bytes=50 << 20
        ),
        name="mix_and_serve",
    )(
        weighted,
        sums,
        proj_turned,
        tokens.T,
        moe_gain,
        router_weight.T,
        expert_ids.T,
        expert_up.swapaxes(1, 2),
        expert_down,
    )
    return (next_hidden.T, new_state)


def solution(mesh):
    in_specs = (
        P("group", "wide"),
        P(),
        P(None, None, "wide"),
        P(None, "wide"),
        P(None, "wide"),
        P("group", None, "wide"),
        P("group", None, "wide"),
        P(None, "wide"),
        P(None, "wide"),
        P("wide"),
        P("wide"),
        P("wide"),
        P("wide"),
        P("wide", None),
        P("group", "wide", None, None),
        P(),
        P(),
        P("group", None),
        P("wide", None, None),
        P("wide", None, None),
    )
    out_specs = (P("group", "wide"), P("group", "wide", None, None))
    body = functools.partial(local, mesh.shape["wide"])
    return jax.shard_map(body, mesh=mesh, in_specs=in_specs, out_specs=out_specs, check_vma=False)
```

```python
import functools

import jax
import jax.numpy as jnp
from jax import lax
from jax.experimental import pallas as pl
from jax.experimental.pallas import tpu as pltpu
from jax.sharding import PartitionSpec as P

HEADS = 64
HEAD_DIM = 64
STATE = 128
GROUPS = 8
EPSILON = 1e-05
MESH = pl.DeviceIdType.MESH
F32 = jnp.float32
BF16 = jnp.bfloat16


def greet(peer):
    pl.semaphore_signal(
        pltpu.get_barrier_semaphore(), inc=1, device_id={"wide": peer}, device_id_type=MESH
    )


def await_peers(count):
    pl.semaphore_wait(pltpu.get_barrier_semaphore(), count)


def place_of(n, me):
    lines = n // 4
    return lines, me // 4, lax.rem(me // 2, 2), lax.rem(me, 2)


def index_of(line, side, core):
    return line * 4 + side * 2 + core


def flipped(line, mask, lines):
    if lines & (lines - 1):
        return lax.rem(mask - line + lines, lines)
    moved, bit = 0, 1
    while bit < lines:
        own = lax.rem(line // bit, 2)
        moved = moved + bit * (1 - own if mask & bit else own)
        bit *= 2
    return moved


def meetings(lines):
    return [(mask, turn) for mask in range(lines - 1, -1, -1) for turn in (1, 0) if mask or turn]


def gather_all(n, me, own, landing, send_sems, recv_sems, consume, meanwhile=None):
    lines, line, side, core = place_of(n, me)
    across = index_of(line, 1 - side, core)
    partner = index_of(line, side, 1 - core)
    corner = index_of(line, 1 - side, 1 - core)
    sent = []

    def send(src, origin, peer):
        copy = pltpu.make_async_remote_copy(
            src_ref=src,
            dst_ref=landing.at[origin],
            send_sem=send_sems.at[len(sent)],
            recv_sem=recv_sems.at[origin],
            device_id={"wide": peer},
            device_id_type=MESH,
        )
        copy.start()
        sent.append(copy)

    def arrive(origin):
        pltpu.make_async_remote_copy(
            src_ref=own,
            dst_ref=landing.at[origin],
            send_sem=send_sems.at[0],
            recv_sem=recv_sems.at[origin],
            device_id={"wide": partner},
            device_id_type=MESH,
        ).wait_recv()

    def take(mask, to_side, to_core, peers):
        origin = index_of(flipped(line, mask, lines), to_side, to_core)
        arrive(origin)
        for peer in peers:
            send(landing.at[origin], origin, peer)
        consume(landing.at[origin], origin)

    for mask in range(lines - 1, 0, -1):
        send(own, me, index_of(flipped(line, mask, lines), side, core))
    send(own, me, across)
    send(own, me, partner)
    if meanwhile is not None:
        meanwhile()
    consume(own, me)
    take(0, side, 1 - core, [])
    for mask in range(1, lines):
        take(mask, side, core, [across, corner, partner] if mask > DIRECT else [across, partner])
        if mask == 1:
            take(0, 1 - side, core, [partner])
    take(1, side, 1 - core, [])
    take(0, 1 - side, 1 - core, [])
    for mask in range(1, lines):
        take(mask, 1 - side, core, [] if mask > DIRECT else [partner])
        if mask > 1:
            take(mask, side, 1 - core, [])
    for mask in range(1, lines):
        take(mask, 1 - side, 1 - core, [])
    for copy in sent:
        copy.wait_send()


def reduce_all(n, me, make, enter, bufs, finish, meanwhile, together=2):
    outgoing, mine, core_in, leaving, coming, sends, core_sem, chip_sem = bufs
    lines, line, side, core = place_of(n, me)
    partner = index_of(line, side, 1 - core)
    sent = []

    def copy_of(src, dst, sem, peer, number):
        return pltpu.make_async_remote_copy(
            src_ref=src,
            dst_ref=dst,
            send_sem=sends.at[number],
            recv_sem=sem,
            device_id={"wide": peer},
            device_id_type=MESH,
        )

    def send(src, dst, sem, peer):
        copy = copy_of(src, dst, sem, peer, len(sent))
        copy.start()
        sent.append(copy)

    def arrive(dst, sem):
        copy_of(dst, dst, sem, partner, 0).wait_recv()

    others = meetings(lines)
    order = others + [(0, 0)]

    def met(mask, turn, which):
        return index_of(flipped(line, mask, lines), lax.rem(side + turn, 2), which)

    def group(number):
        return range(number, min(number + together, len(order)))

    def fill(number):
        blocks = make([met(*order[each], 1 - core) for each in group(number)])
        for each, block in zip(group(number), blocks):
            outgoing[each] = block.astype(BF16)

    def keep(number):
        blocks = make([met(*order[each], core) for each in group(number)])
        for each, block in zip(group(number), blocks):
            mine[each] = block

    numbers = range(len(order))
    if enter is not None:
        for number in numbers[::together]:
            fill(number)
        for number in numbers[::together]:
            keep(number)
        enter()
    def give(number):
        if enter is None and number % together == 0:
            fill(number)
        send(outgoing.at[number], core_in.at[number], core_sem.at[number], partner)

    ahead = len(order) if enter is not None else min(AHEAD, len(order))
    for number in range(ahead):
        give(number)

    def pair_sum(number):
        if enter is None and number % together == 0:
            keep(number)
        arrive(core_in.at[number], core_sem.at[number])
        return finish(mine[number] + core_in[number].astype(F32))

    for number, (mask, turn) in enumerate(others):
        leaving[number] = pair_sum(number).astype(BF16)
        send(leaving.at[number], coming.at[number], chip_sem.at[number], met(mask, turn, core))
        if (number + 1) % together == 0:
            for later in group(number + 1 - together + ahead):
                give(later)
    total = pair_sum(len(others))
    meanwhile()
    for number in reversed(range(len(others))):
        arrive(coming.at[number], chip_sem.at[number])
        total = total + coming[number].astype(F32)
    for copy in sent:
        copy.wait_send()
    return total


LANES = 128
DIRECT = 2
AHEAD = 4


def packed_shape(width, seqs):
    gap = LANES - seqs
    if gap <= 0 or seqs % gap:
        return width, 0, 0
    chunks = seqs // gap
    rest = width // (chunks + 1) // 8 * 8
    return width - rest, rest, gap


def lane_ids(rows):
    return lax.broadcasted_iota(jnp.int32, (rows, LANES), 1)


def pack(value, seqs, extra=()):
    kept, rest, gap = packed_shape(value.shape[0], seqs)
    tail = value[kept:, :]
    pieces = [pltpu.roll(tail, seqs - c * gap, 1) for c in range(seqs // gap)]
    pieces += [pltpu.roll(row, seqs - c * gap, 1) for row in extra for c in range(seqs // gap)]
    spare = kept - sum(piece.shape[0] for piece in pieces)
    if spare:
        pieces.append(jnp.zeros((spare, LANES), F32))
    return jnp.where(lane_ids(kept) < seqs, value[:kept], jnp.concatenate(pieces, axis=0))


def unpack(value, width, seqs):
    kept, rest, gap = packed_shape(width, seqs)
    chunk = lane_ids(rest) // gap
    tail = jnp.zeros((rest, LANES), F32)
    for c in range(seqs // gap):
        piece = pltpu.roll(value[c * rest : (c + 1) * rest], LANES - seqs + c * gap, 1)
        tail = jnp.where(chunk == c, piece, tail)
    return jnp.concatenate([value[:kept], tail], axis=0)


def extra_rows(width, seqs):
    kept, rest, gap = packed_shape(width, seqs)
    first = rest * (seqs // gap)
    return first, first + 2 * (seqs // gap)


def own_columns(vector, n, me, width):
    whole = vector[...].astype(F32)[None]
    row = jnp.zeros((1, width), F32)
    for i in range(n):
        row = jnp.where(me == i, whole[:, i * width : (i + 1) * width], row)
    return jnp.broadcast_to(row, (LANES, width)).T


def padded(value):
    rows, lanes = value.shape
    return jnp.concatenate([value, jnp.zeros((rows, LANES - lanes), F32)], axis=1)


def by_block(target, value, start, width, columns):
    at, count = 0, value.shape[0]
    while at < count:
        block, row = divmod(start + at, width)
        size = min(width - row, count - at)
        target[block, row : row + size, :columns] = value[at : at + size]
        at += size


def token_scale(squares, seqs, channels):
    rows = squares.shape[0]
    chunks = rows // 2
    turned = jnp.concatenate([squares[...], jnp.zeros((LANES - rows, LANES), F32)], axis=0).T
    pieces = [turned[seqs:, c : c + 1] + turned[seqs:, chunks + c : chunks + c + 1] for c in range(chunks)]
    return lax.rsqrt(jnp.concatenate(pieces, axis=0) / channels + EPSILON)


def halves(value):
    high = value.astype(BF16).astype(F32)
    return high, value - high


def convolved(fresh, window, kernel):
    mixed = fresh * kernel[3:4]
    for k in range(3):
        mixed = mixed + window[k].astype(F32) * kernel[k : k + 1]
    return (mixed * jax.nn.sigmoid(mixed)).astype(BF16).astype(F32)


def gather_kernel(
    n,
    inner_hbm,
    maps_hbm,
    state_hbm,
    proj_hbm,
    tokens_hbm,
    gain_hbm,
    step_weights_hbm,
    window_hbm,
    window_maps_hbm,
    taps_hbm,
    taps_maps_hbm,
    step_bias_hbm,
    decay_log_hbm,
    skip_gain_hbm,
    gated_gain_hbm,
    state,
    faded_out,
    packed_out,
    columns_out,
    decays_out,
    skips_out,
    gates_out,
    in_out,
    out_out,
    gains_out,
    proj_turned,
    landing,
    own,
    tokens,
    gain,
    step_weights,
    window,
    window_maps,
    taps,
    taps_maps,
    step_bias,
    decay_log,
    skip_gain,
    gated_gain,
    raw_inner,
    raw_maps,
    raw_proj,
    weights,
    total,
    squares,
    turned,
    mapped,
    arrived,
    load_sems,
    send_sems,
    recv_sems,
    map_send,
    map_recv,
):
    me = lax.axis_index("wide")
    width, seqs = tokens.shape
    inner = window.shape[2]
    cols = window_maps.shape[2]
    heads = step_weights.shape[0]
    lines, line, side, core = place_of(n, me)
    half = n // 2
    per_group = half // GROUPS
    readers = HEADS // GROUPS // heads
    group = me // readers
    origins = [
        (slot // per_group) * half + group * per_group + slot % per_group
        for slot in range(2 * per_group)
    ]
    reader = lax.rem(me, half) // per_group * readers
    for mask in range(1, lines):
        greet(index_of(flipped(line, mask, lines), side, core))
    for turn in (0, 1):
        greet(index_of(line, 1 - side, (1 - core if turn else core)))
    greet(index_of(line, side, 1 - core))
    for origin in origins:

        @pl.when(origin != me)
        def _():
            greet(origin)

    small = [
        (tokens_hbm, tokens),
        (gain_hbm, gain),
        (step_weights_hbm, step_weights),
        (window_hbm, window),
        (window_maps_hbm, window_maps),
        (taps_hbm, taps),
        (taps_maps_hbm, taps_maps),
        (step_bias_hbm, step_bias),
        (decay_log_hbm, decay_log),
        (skip_gain_hbm, skip_gain),
        (gated_gain_hbm, gated_gain),
    ]
    loads = [
        pltpu.make_async_copy(source, target, load_sems.at[4 + i])
        for i, (source, target) in enumerate(small)
    ]
    for load in loads:
        load.start()
    load_inner = pltpu.make_async_copy(inner_hbm, raw_inner, load_sems.at[0])
    load_maps = pltpu.make_async_copy(maps_hbm, raw_maps, load_sems.at[1])
    load_state = pltpu.make_async_copy(state_hbm, state, load_sems.at[2])
    load_proj = pltpu.make_async_copy(proj_hbm, raw_proj, load_sems.at[3])
    load_inner.start()
    load_maps.start()
    load_proj.start()
    load_state.start()
    expected = lines + 2
    for r in range(readers):
        expected = expected + jnp.where(reader + r != me, 1, 0)
    loads[0].wait()
    loads[1].wait()
    values = padded(tokens[...].astype(F32))
    sums = jnp.sum(values * values, axis=0, keepdims=True)
    scaled = values * own_columns(gain, n, me, width)
    own[...] = pack(scaled, seqs, halves(sums)).astype(BF16)
    total[...] = jnp.zeros_like(total)
    squares[...] = jnp.zeros_like(squares)
    first, last = extra_rows(width, seqs)

    def prepare():
        for load in loads[2:]:
            load.wait()
        load_inner.wait()
        load_maps.wait()
        steps = step_weights[...].astype(F32).T.astype(BF16)
        place = lax.broadcasted_iota(jnp.int32, (2 * width, 2 * width), 0)
        wanted = jnp.where(place < width, 2 * place, 2 * (place - width) + 1)
        found = lax.broadcasted_iota(jnp.int32, (2 * width, 2 * width), 1)
        picks = jnp.where(wanted == found, 1.0, 0.0).astype(BF16)
        for i in range(n):
            rows = slice(i * width, (i + 1) * width)
            weights[i, :, :cols] = raw_maps[rows, :]
            weights[i, :, cols : cols + heads] = steps[rows, :]
            pairs = raw_inner[rows].reshape(2 * width, inner)
            split = jnp.dot(picks, pairs, preferred_element_type=F32).astype(BF16)
            for j in range(2):
                at = LANES * 2 + j * inner
                weights[i, :, at : at + inner] = split[j * width : (j + 1) * width]
        gains_out[...] = jnp.broadcast_to(gated_gain[...].astype(F32)[None], (LANES, inner)).T
        load_proj.wait()
        for start in range(0, n * width, LANES):
            by_block(proj_turned, raw_proj[:, start : start + LANES].T, start, width, inner)

    def consume(block, origin):
        value = block[...].astype(F32)
        squares[...] += value[first:last]
        fresh = unpack(value, width, seqs)[:, :seqs].astype(BF16)
        total[...] += lax.dot_general(
            fresh, weights[origin], (((0,), (0,)), ((), ())), preferred_element_type=F32
        )

    await_peers(expected)
    gather_all(n, me, own, landing, send_sems, recv_sems, consume, prepare)
    scale = token_scale(squares, seqs, n * width)

    def projected(at, count):
        return (total[:, at : at + count] * scale).astype(BF16).astype(F32)

    mapped[...] = convolved(projected(0, cols), window_maps, taps_maps[...].astype(F32)).astype(BF16)
    kind = me // half
    own_slot = kind * per_group + lax.rem(me, per_group)

    def send(r):
        peer = reader + r
        return peer, pltpu.make_async_remote_copy(
            src_ref=mapped,
            dst_ref=arrived.at[own_slot],
            send_sem=map_send.at[r],
            recv_sem=map_recv.at[own_slot],
            device_id={"wide": peer},
            device_id_type=MESH,
        )

    for r in range(readers):
        peer, copy = send(r)

        @pl.when(peer != me)
        def _():
            copy.start()

        @pl.when(peer == me)
        def _():
            arrived[own_slot] = mapped[...]

    head_ids = lax.broadcasted_iota(jnp.int32, (1, inner), 1) // HEAD_DIM

    def spread(ref):
        wide = jnp.zeros((1, inner), F32)
        for h in range(heads):
            wide = jnp.where(head_ids == h, ref[...][None][:, h : h + 1], wide)
        return wide

    gate = projected(2 * LANES, inner)
    inputs = convolved(projected(2 * LANES + inner, inner), window, taps[...].astype(F32))
    raw = projected(cols, heads)
    raw = jax.nn.softplus(raw + step_bias[...][None])
    decays = jnp.exp(-jnp.exp(decay_log[...][None]) * raw)
    steps = jnp.zeros((seqs, inner), F32)
    for h in range(heads):
        decays_out[h] = jnp.broadcast_to(decays[:, h : h + 1], (seqs, LANES))
        steps = jnp.where(head_ids == h, raw[:, h : h + 1], steps)

    def turn(target, value):
        target[:, seqs:] = jnp.zeros((inner, LANES - seqs), F32)
        target[:, :seqs] = value.T

    turn(turned, steps * inputs)
    moved = turned[...]
    middle = inner // 2
    rows = seqs // columns_out.shape[0]
    ahead = lane_ids(middle) < rows
    for i in range(columns_out.shape[0]):
        top = moved[:middle]
        high, low = halves(top)
        packed_out[i] = jnp.where(ahead, high, pltpu.roll(low, rows, 1)).astype(BF16)
        columns_out[i] = moved[middle:]
        moved = pltpu.roll(moved, LANES - rows, 1)
    skipped = spread(skip_gain) * inputs
    turn(gates_out, gate * jax.nn.sigmoid(gate))
    load_state.wait()

    def fade(s, carry):
        for h in range(heads):
            part = slice(h * HEAD_DIM, (h + 1) * HEAD_DIM)
            faded_out[s, part] = (decays_out[h, pl.ds(s, 1), :] * state[s, h]).astype(BF16)
        return carry

    lax.fori_loop(0, seqs, fade, 0, unroll=4)
    for slot, origin in enumerate(origins):

        @pl.when(origin != me)
        def _():
            pltpu.make_async_remote_copy(
                src_ref=mapped,
                dst_ref=arrived.at[slot],
                send_sem=map_send.at[0],
                recv_sem=map_recv.at[slot],
                device_id={"wide": me},
                device_id_type=MESH,
            ).wait_recv()

    out_out[...] = jnp.zeros_like(out_out)
    met = jnp.zeros((1, seqs), F32)
    for slot in range(per_group):
        part = slice(slot * cols, (slot + 1) * cols)
        in_out[:, part] = arrived[slot].astype(F32)
        readers_turned = arrived[per_group + slot].astype(F32).T
        out_out[part, :seqs] = readers_turned
        met = met + jnp.sum(arrived[slot].astype(F32).T * readers_turned, axis=0, keepdims=True)
    skips_out[:, seqs:] = jnp.zeros((inner, LANES - seqs), F32)
    skips_out[:, :seqs] = skipped.T + turned[:, :seqs] * met
    for r in range(readers):
        peer, copy = send(r)

        @pl.when(peer != me)
        def _():
            copy.wait_send()


def state_kernel(
    rows,
    seqs,
    state,
    faded,
    packed,
    columns,
    decays,
    skips,
    gates,
    in_maps,
    out_maps,
    gains,
    new_state,
    weighted,
    sums,
    fresh,
    total,
    store_sems,
):
    heads = state.shape[1]
    lane = lax.broadcasted_iota(jnp.int32, (STATE, LANES), 1)
    own = lax.broadcasted_iota(jnp.int32, (rows, STATE), 0)
    slots, part = fresh.shape[:2]
    middle = packed.shape[1]
    batch = 2
    copies = []
    for start in range(0, seqs, batch):
        step, first = divmod(start, rows)
        chunk, place = divmod(start, part)
        slot = chunk % slots
        if place == 0 and chunk >= slots:
            copies[chunk - slots].wait()
        picked = []
        maps = in_maps[step * rows : (step + 1) * rows, :]
        for j in range(first, first + batch):
            one = jnp.where(own == j, maps, 0.0)
            picked.append(jnp.concatenate([one, one], axis=0))
        driven = jnp.dot(
            packed[step][:, : 2 * rows],
            jnp.concatenate(picked, axis=1).astype(BF16),
            preferred_element_type=F32,
        )
        for i in range(batch):
            lanes = slice(i * STATE, (i + 1) * STATE)
            row = in_maps[start + i : start + i + 1, :]
            for h in range(heads):
                slow = decays[h, start + i : start + i + 1, :]
                for p in range(0, HEAD_DIM, 8):
                    at = h * HEAD_DIM + p
                    if at < middle:
                        drive = driven[at : at + 8, lanes]
                    else:
                        to = at - middle
                        drive = columns[step, to : to + 8, first + i : first + i + 1] * row
                    value = slow * state[start + i, h, p : p + 8] + drive
                    fresh[slot, place + i, h, p : p + 8] = value
        left = [faded[start + i] for i in range(batch)]
        right = [
            jnp.where(lane == start + i, out_maps[...], 0.0).astype(BF16) for i in range(batch)
        ]
        found = jnp.dot(
            jnp.concatenate(left, axis=1),
            jnp.concatenate(right, axis=0),
            preferred_element_type=F32,
        )
        if start:
            found = found + total[...]
        total[...] = found
        if place + batch == part:
            copy = pltpu.make_async_copy(
                fresh.at[slot], new_state.at[pl.ds(chunk * part, part)], store_sems.at[slot]
            )
            copy.start()
            copies.append(copy)
    gated = (total[...] + skips[...]) * gates[...]
    sums[...] = jnp.broadcast_to(jnp.sum(gated * gated, axis=0, keepdims=True), sums.shape)
    weighted[...] = (gated * gains[...]).astype(BF16)
    for copy in copies[-slots:]:
        copy.wait()


def expert_kernel(
    n,
    partners,
    weighted,
    sums,
    proj_turned,
    tokens,
    moe_gain,
    router,
    expert_ids,
    up_hbm,
    down_hbm,
    result,
    up,
    down,
    up_turned,
    down_turned,
    own,
    landing,
    total,
    squares,
    gains,
    sums_in,
    load_sems,
    sum_send,
    sum_recv,
    hid_send,
    hid_recv,
    *bufs,
):
    me = lax.axis_index("wide")
    width, seqs = tokens.shape
    hidden_units = up.shape[1]
    experts = router.shape[0]
    extent = up_turned.shape[2]
    kept, rest, gap = packed_shape(width, seqs)
    chunks = seqs // gap
    lines, line, side, core = place_of(n, me)
    first = (me // partners) * partners
    place = lax.rem(me, partners)
    others = meetings(lines)
    for mask, turn in others:
        greet(index_of(flipped(line, mask, lines), lax.rem(side + turn, 2), core))
    greet(index_of(line, 1 - side, 1 - core))
    greet(index_of(line, side, 1 - core))
    for k in range(1, partners):
        greet(first + lax.rem(place + k, partners))

    load_up = pltpu.make_async_copy(up_hbm, up, load_sems.at[0])
    load_down = pltpu.make_async_copy(down_hbm, down, load_sems.at[1])
    load_up.start()
    load_down.start()

    def partner_copy(k):
        other = lax.rem(place + k, partners)
        return pltpu.make_async_remote_copy(
            src_ref=sums,
            dst_ref=sums_in.at[k - 1],
            send_sem=sum_send.at[k - 1],
            recv_sem=sum_recv.at[k - 1],
            device_id={"wide": first + other},
            device_id_type=MESH,
        )

    def products(turned, blocks, right):
        tall = jnp.concatenate([turned[i] for i in blocks], axis=0)
        found = jnp.dot(tall, right, preferred_element_type=F32)
        return [pack(found[k * width : (k + 1) * width], seqs) for k in range(len(blocks))]

    def mixed(blocks):
        return products(proj_turned, blocks, weighted[...])

    def enter():
        await_peers(len(others) + 1 + partners)
        for k in range(1, partners):
            partner_copy(k).start()

    scales = []

    def scaled(value):
        if not scales:
            whole = sums[...]
            for k in range(1, partners):
                partner_copy(k).wait()
                whole = whole + sums_in[k - 1]
            row = lax.rsqrt(whole[:1] / (weighted.shape[0] * partners) + EPSILON)
            scales.append(pack(jnp.broadcast_to(row, (width, LANES)), seqs))
        return value * scales[0]

    def turn_up():
        gains[...] = pack(own_columns(moe_gain, n, me, width), seqs)
        load_up.wait()
        for start in range(0, n * width, LANES):
            lanes = slice(start, start + LANES)
            spare = jnp.zeros((extent - hidden_units - experts, LANES), BF16)
            tall = jnp.concatenate([up[0, :, lanes], router[:, lanes], spare], axis=0)
            by_block(up_turned, tall.T, start, width, extent)

    def turn_down():
        load_down.wait()
        for start in range(0, n * width, LANES):
            by_block(down_turned, down[0, :, start : start + LANES].T, start, width, hidden_units)

    def nothing():
        pass

    half = len(bufs) // 2
    reduced = reduce_all(n, me, mixed, enter, bufs[:half], scaled, turn_up, 4)
    held = pack(padded(tokens[...].astype(F32)), seqs)
    held = (held + reduced).astype(BF16).astype(F32)
    power = held * held
    main = jnp.sum(power, axis=0, keepdims=True)
    extra = []
    for c in range(chunks):
        tail = jnp.sum(power[c * rest : (c + 1) * rest], axis=0, keepdims=True)
        extra.append(pltpu.roll(main, seqs - c * gap, 1) + tail)
    spare = jnp.zeros((kept - rest * chunks - 2 * chunks, LANES), F32)
    both = [halves(row) for row in extra]
    ending = jnp.concatenate([row[0] for row in both] + [row[1] for row in both] + [spare], axis=0)
    sender = held * gains[...]
    inside = lane_ids(kept - rest * chunks) < seqs
    ending = jnp.where(inside, sender[rest * chunks :], ending)
    own[...] = jnp.concatenate([sender[: rest * chunks], ending], axis=0).astype(BF16)
    total[...] = jnp.zeros_like(total)
    squares[...] = jnp.zeros_like(squares)
    begin, end = extra_rows(width, seqs)

    def consume(block, origin):
        value = block[...].astype(F32)
        squares[...] += value[begin:end]
        fresh = unpack(value, width, seqs)[:, :seqs].astype(BF16)
        total[...] += lax.dot_general(
            fresh, up_turned[origin], (((0,), (0,)), ((), ())), preferred_element_type=F32
        )

    gather_all(n, me, own, landing, hid_send, hid_recv, consume, turn_down)
    scale = token_scale(squares, seqs, n * width)
    logits = total[:, hidden_units : hidden_units + experts] * scale
    expert = lax.broadcasted_iota(jnp.int32, (LANES, seqs), 0)
    named = jnp.zeros((LANES, seqs), F32)
    for k in range(expert_ids.shape[0]):
        named = named + jnp.where(expert == expert_ids[k : k + 1, :], 1.0, 0.0)
    score = named.T[:, :experts] * jax.nn.sigmoid(logits)
    lane = lax.broadcasted_iota(jnp.int32, score.shape, 1)
    mine = jnp.sum(jnp.where(lane == me, score, 0.0), axis=1, keepdims=True)
    weight = mine / jnp.sum(score, axis=1, keepdims=True)
    units = jnp.maximum(total[:, :hidden_units] * scale, 0.0)
    active = jnp.square(units) * weight
    active = jnp.concatenate([active, jnp.zeros((LANES - seqs, hidden_units), F32)], axis=0)
    active = active.astype(BF16).T

    def served(blocks):
        return products(down_turned, blocks, active)

    reduced = reduce_all(n, me, served, None, bufs[half:], lambda value: value, nothing)
    result[...] = unpack(held + reduced, width, seqs)[:, :seqs].astype(BF16)


def vmem(count):
    return [pl.BlockSpec(memory_space=pltpu.VMEM)] * count


ANY = pl.BlockSpec(memory_space=pltpu.HBM)
DMA = pltpu.SemaphoreType.DMA


def local(
    n,
    tokens,
    mix_gain,
    proj_inner,
    proj_maps,
    proj_step,
    window_inner,
    window_maps,
    kernel_inner,
    kernel_maps,
    step_bias,
    decay_log,
    skip_gain,
    gated_gain,
    proj_out,
    ssm_state,
    moe_gain,
    router_weight,
    expert_ids,
    expert_up,
    expert_down,
):
    seqs, width = tokens.shape
    full_width = proj_inner.shape[0]
    inner = proj_inner.shape[2]
    cols = proj_maps.shape[1]
    heads = proj_step.shape[1]
    readers = HEADS // GROUPS // heads
    slots = 2 * (STATE // cols)
    kept = packed_shape(width, seqs)[0]
    first, last = extra_rows(width, seqs)
    across = 2 * LANES + 2 * inner
    small = (
        tokens.T,
        mix_gain,
        proj_step.T,
        window_inner.transpose(1, 0, 2),
        window_maps.transpose(1, 0, 2),
        kernel_inner,
        kernel_maps,
        step_bias,
        decay_log,
        skip_gain,
        gated_gain,
    )
    rows = 16
    state, faded, packed, columns, decays, skips, gates, in_maps, out_maps, gains, proj_turned = pl.pallas_call(
        functools.partial(gather_kernel, n),
        out_shape=(
            pltpu.VMEM(ssm_state.shape, F32),
            pltpu.VMEM((seqs, inner, STATE), BF16),
            pltpu.VMEM((seqs // rows, inner // 2, LANES), BF16),
            pltpu.VMEM((seqs // rows, inner // 2, LANES), F32),
            pltpu.VMEM((heads, seqs, LANES), F32),
            pltpu.VMEM((inner, LANES), F32),
            pltpu.VMEM((inner, LANES), F32),
            pltpu.VMEM((seqs, STATE), F32),
            pltpu.VMEM((STATE, LANES), F32),
            pltpu.VMEM((inner, LANES), F32),
            pltpu.VMEM((n, width, inner), BF16),
        ),
        in_specs=[ANY] * 15,
        out_specs=tuple(vmem(11)),
        scratch_shapes=[
            pltpu.VMEM((n, kept, LANES), BF16),
            pltpu.VMEM((kept, LANES), BF16),
            *(pltpu.VMEM(value.shape, value.dtype) for value in small),
            pltpu.VMEM((full_width, 2, inner), BF16),
            pltpu.VMEM((full_width, cols), BF16),
            pltpu.VMEM((inner, full_width), BF16),
            pltpu.VMEM((n, width, across), BF16),
            pltpu.VMEM((seqs, across), F32),
            pltpu.VMEM((last - first, LANES), F32),
            pltpu.VMEM((inner, LANES), F32),
            pltpu.VMEM((seqs, cols), BF16),
            pltpu.VMEM((slots, seqs, cols), BF16),
            DMA((4 + len(small),)),
            DMA((n,)),
            DMA((n,)),
            DMA((readers,)),
            DMA((slots,)),
        ],
        compiler_params=pltpu.CompilerParams(
            collective_id=0, has_side_effects=True, vmem_limit_bytes=42 << 20
        ),
        name="gather_tokens",
    )(proj_inner, proj_maps, ssm_state, proj_out, *small)
    new_state, weighted, sums = pl.pallas_call(
        functools.partial(state_kernel, rows, seqs),
        out_shape=(
            jax.ShapeDtypeStruct(ssm_state.shape, F32),
            pltpu.VMEM((inner, LANES), BF16),
            pltpu.VMEM((8, LANES), F32),
        ),
        in_specs=vmem(10),
        out_specs=(ANY, *vmem(2)),
        scratch_shapes=[
            pltpu.VMEM((4, 8, heads, HEAD_DIM, STATE), F32),
            pltpu.VMEM((inner, LANES), F32),
            DMA((4,)),
        ],
        compiler_params=pltpu.CompilerParams(vmem_limit_bytes=16 << 20),
        name="update_state",
    )(state, faded, packed, columns, decays, skips, gates, in_maps, out_maps, gains)
    chips = n // 2

    def piece(count, kind=BF16):
        return pltpu.VMEM((count, kept, LANES), kind)

    reduce_bufs = [
        piece(chips),
        piece(chips, F32),
        piece(chips),
        piece(chips - 1),
        piece(chips - 1),
        DMA((2 * chips - 1,)),
        DMA((chips,)),
        DMA((chips - 1,)),
    ]
    hidden_units = expert_up.shape[2]
    experts = router_weight.shape[1]
    extent = -(-(hidden_units + experts) // LANES) * LANES
    next_hidden = pl.pallas_call(
        functools.partial(expert_kernel, n, readers),
        out_shape=jax.ShapeDtypeStruct((width, seqs), BF16),
        in_specs=vmem(7) + [ANY, ANY],
        out_specs=vmem(1)[0],
        scratch_shapes=[
            pltpu.VMEM((1, hidden_units, full_width), BF16),
            pltpu.VMEM(expert_down.shape, BF16),
            pltpu.VMEM((n, width, extent), BF16),
            pltpu.VMEM((n, width, hidden_units), BF16),
            pltpu.VMEM((kept, LANES), BF16),
            piece(n),
            pltpu.VMEM((seqs, extent), F32),
            pltpu.VMEM((last - first, LANES), F32),
            pltpu.VMEM((kept, LANES), F32),
            pltpu.VMEM((readers - 1, 8, LANES), F32),
            DMA((2,)),
            DMA((readers - 1,)),
            DMA((readers - 1,)),
            DMA((n,)),
            DMA((n,)),
        ]
        + reduce_bufs * 2,
        compiler_params=pltpu.CompilerParams(
            collective_id=1, has_side_effects=True, vmem_limit_bytes=50 << 20
        ),
        name="mix_and_serve",
    )(
        weighted,
        sums,
        proj_turned,
        tokens.T,
        moe_gain,
        router_weight.T,
        expert_ids.T,
        expert_up.swapaxes(1, 2),
        expert_down,
    )
    return (next_hidden.T, new_state)


def solution(mesh):
    in_specs = (
        P("group", "wide"),
        P(),
        P(None, None, "wide"),
        P(None, "wide"),
        P(None, "wide"),
        P("group", None, "wide"),
        P("group", None, "wide"),
        P(None, "wide"),
        P(None, "wide"),
        P("wide"),
        P("wide"),
        P("wide"),
        P("wide"),
        P("wide", None),
        P("group", "wide", None, None),
        P(),
        P(),
        P("group", None),
        P("wide", None, None),
        P("wide", None, None),
    )
    out_specs = (P("group", "wide"), P("group", "wide", None, None))
    body = functools.partial(local, mesh.shape["wide"])
    return jax.shard_map(body, mesh=mesh, in_specs=in_specs, out_specs=out_specs, check_vma=False)
```
